32 devices in a mesh: rep: 16 (over z, y, x), opt: 2 (over core).
Axes of the slice: x: 2, y: 2, z: 4, core: 2. Of those that a mesh axis runs over, the one named last changes fastest.
Arguments:
- tokens: bfloat16 [65536, 512], P(('rep', 'opt')), may hold values from -40 to 40
- out_grad: bfloat16 [65536, 512], P(('rep', 'opt')), may hold values from -5 to 5
- vectors: bfloat16 [6, 512], P(None, 'opt'), may hold values from -2 to 2
- qkv_weight: bfloat16 [512, 1536], P('opt'), may hold values from -0.25 to 0.25
- qkv_bias: bfloat16 [1536], P('opt'), may hold values from -1.5 to 1.5
- out_weight: bfloat16 [512, 512], P('opt'), may hold values from -1 to 1
- fc_weight: bfloat16 [512, 2048], P('opt'), may hold values from -0.25 to 0.25
- fc_bias: bfloat16 [2048], P('opt'), may hold values from -2.5 to 2.5
- proj_weight: bfloat16 [2048, 512], P('opt'), may hold values from -0.125 to 0.125
- mean_vectors: float32 [6, 512], P(None, 'opt'), may hold values from -24 to 24
- mean_qkv_weight: float32 [512, 1536], P('opt'), may hold values from -24 to 24
- mean_qkv_bias: float32 [1536], P('opt'), may hold values from -24 to 24
- mean_out_weight: float32 [512, 512], P('opt'), may hold values from -24 to 24
- mean_fc_weight: float32 [512, 2048], P('opt'), may hold values from -24 to 24
- mean_fc_bias: float32 [2048], P('opt'), may hold values from -24 to 24
- mean_proj_weight: float32 [2048, 512], P('opt'), may hold values from -24 to 24
- square_vectors: float32 [6, 512], P(None, 'opt'), may hold values from 32 to 512
- square_qkv_weight: float32 [512, 1536], P('opt'), may hold values from 32 to 512
- square_qkv_bias: float32 [1536], P('opt'), may hold values from 32 to 512
- square_out_weight: float32 [512, 512], P('opt'), may hold values from 32 to 512
- square_fc_weight: float32 [512, 2048], P('opt'), may hold values from 32 to 512
- square_fc_bias: float32 [2048], P('opt'), may hold values from 32 to 512
- square_proj_weight: float32 [2048, 512], P('opt'), may hold values from 32 to 512
Outputs:
- layer_out: bfloat16 [65536, 512], P(('rep', 'opt'))
- tokens_grad: bfloat16 [65536, 512], P(('rep', 'opt'))
- grad_vectors: float32 [6, 512], P(None, 'opt')
- grad_qkv_weight: float32 [512, 1536], P('opt')
- grad_qkv_bias: float32 [1536], P('opt')
- grad_out_weight: float32 [512, 512], P('opt')
- grad_fc_weight: float32 [512, 2048], P('opt')
- grad_fc_bias: float32 [2048], P('opt')
- grad_proj_weight: float32 [2048, 512], P('opt')
- step_vectors: float32 [6, 512], P(None, 'opt')
- step_qkv_weight: float32 [512, 1536], P('opt')
- step_qkv_bias: float32 [1536], P('opt')
- step_out_weight: float32 [512, 512], P('opt')
- step_fc_weight: float32 [512, 2048], P('opt')
- step_fc_bias: float32 [2048], P('opt')
- step_proj_weight: float32 [2048, 512], P('opt')
- new_mean_vectors: float32 [6, 512], P(None, 'opt')
- new_mean_qkv_weight: float32 [512, 1536], P('opt')
- new_mean_qkv_bias: float32 [1536], P('opt')
- new_mean_out_weight: float32 [512, 512], P('opt')
- new_mean_fc_weight: float32 [512, 2048], P('opt')
- new_mean_fc_bias: float32 [2048], P('opt')
- new_mean_proj_weight: float32 [2048, 512], P('opt')
- new_square_vectors: float32 [6, 512], P(None, 'opt')
- new_square_qkv_weight: float32 [512, 1536], P('opt')
- new_square_qkv_bias: float32 [1536], P('opt')
- new_square_out_weight: float32 [512, 512], P('opt')
- new_square_fc_weight: float32 [512, 2048], P('opt')
- new_square_fc_bias: float32 [2048], P('opt')
- new_square_proj_weight: float32 [2048, 512], P('opt')
The draws below stay inside these ranges and needn't reach their ends.
All inputs are finite; a program needn't handle non-finite values.
Results may differ from the reference program's by a relative error of at most 0.015.
The reference program's roundings to bfloat16 on the way count: a program that leaves them out, or rounds other values in their place, can miss the bound.
Values may be sent and summed in bfloat16 or wider, within the bound.
No kernel may reach another device: no remote copies, remote signals or barrier semaphores. Data moves between devices by JAX's collectives and lax.ppermute only.
A program may use at most 256 MiB of HBM per device.

```python
import math
import jax
import jax.numpy as jnp
from jax import lax

D = 512
H = 8
FF = 2048
HD = 64
ROT = 16
LEN = 512
ADAM_STEP = 10
TOKENS = 65536


def draw_tokens(key, part):
    key_base, key_cols, key_rows = jax.random.split(key, 3)
    base = jnp.clip(jax.random.normal(key_base, (TOKENS, D), jnp.float32), -4.0, 4.0)
    col_scale = jnp.exp(jax.random.uniform(key_cols, (1, D), jnp.float32, -1.15, 1.15))
    row_scale = jnp.exp(jax.random.uniform(key_rows, (TOKENS, 1), jnp.float32, -1.15, 1.15))
    return (base * col_scale * row_scale).astype(jnp.bfloat16)


def draw_vectors(key, part):
    key_gain, key_bias = jax.random.split(key, 2)
    gains = jax.random.uniform(key_gain, (2, D), jnp.float32, 0.5, 1.5)
    shifts = jnp.clip(0.5 * jax.random.normal(key_bias, (4, D), jnp.float32), -2.0, 2.0)
    return jnp.stack([gains[0], shifts[0], gains[1], shifts[1], shifts[2], shifts[3]]).astype(jnp.bfloat16)


def levels(rng, extent, pieces, least, top_value):
    level, own = 1.0, jax.random.fold_in(rng, 6)
    for position, shards_of in pieces:
        heights = jnp.exp(jax.random.uniform(jax.random.fold_in(own, position), (shards_of,), jnp.float32, least / len(pieces), top_value / len(pieces)))
        level = level * jnp.repeat(heights, extent[position] // shards_of).reshape([-1 if axis == position else 1 for axis in range(len(extent))])
    return level


def centred(own_key, extent, deviation, reach, shards=(), held_as=jnp.bfloat16):
    drawn = deviation * jax.random.normal(own_key, extent, jnp.float32)
    if shards:
        drawn = drawn * levels(own_key, extent, shards, -0.22, 0.18)
    return jnp.clip(drawn, -reach, reach).astype(held_as)


def setup_inputs(seed: int = 0) -> dict:
    seeds = jax.random.split(jax.random.key(seed), 24)
    tokens = draw_tokens(jax.random.fold_in(seeds[23], 71), 0)
    out_grad = centred(seeds[1], (TOKENS, D), 1.0, 5.0, ((0, 32),))
    vectors = draw_vectors(jax.random.fold_in(seeds[23], 71), 0)
    qkv_weight = centred(seeds[3], (D, 3 * D), D ** -0.5, 0.25, ((0, 2),))
    qkv_bias = centred(seeds[4], (3 * D,), 0.3, 1.5, ((0, 2),))
    out_weight = centred(seeds[5], (D, D), (D // 16) ** -0.5, 1.0, ((0, 2),))
    fc_weight = centred(seeds[6], (D, FF), D ** -0.5, 0.25, ((0, 2),))
    fc_bias = centred(seeds[7], (FF,), 0.5, 2.5, ((0, 2),))
    proj_weight = centred(seeds[8], (FF, D), FF ** -0.5, 0.125, ((0, 2),))
    mean_vectors = centred(seeds[9], (6, D), (max(1, TOKENS // 16384)), 24.0, ((1, 2),), jnp.float32)
    mean_qkv_weight = centred(seeds[10], (D, 3 * D), (max(1, TOKENS // 16384)), 24.0, ((0, 2),), jnp.float32)
    mean_qkv_bias = centred(seeds[11], (3 * D,), (max(1, TOKENS // 16384)), 24.0, ((0, 2),), jnp.float32)
    mean_out_weight = centred(seeds[12], (D, D), (max(1, TOKENS // 16384)), 24.0, ((0, 2),), jnp.float32)
    mean_fc_weight = centred(seeds[13], (D, FF), (max(1, TOKENS // 16384)), 24.0, ((0, 2),), jnp.float32)
    mean_fc_bias = centred(seeds[14], (FF,), (max(1, TOKENS // 16384)), 24.0, ((0, 2),), jnp.float32)
    mean_proj_weight = centred(seeds[15], (FF, D), (max(1, TOKENS // 16384)), 24.0, ((0, 2),), jnp.float32)
    square_vectors = jnp.clip(jnp.exp(math.log(512.0) - 2.7725887 * jax.random.uniform(seeds[16], (6, D), jnp.float32) ** levels(seeds[16], (6, D), ((1, 2),), -0.2, 0.2)), 32.0, 512.0)
    square_qkv_weight = jnp.clip(jnp.exp(math.log(512.0) - 2.7725887 * jax.random.uniform(seeds[17], (D, 3 * D), jnp.float32) ** levels(seeds[17], (D, 3 * D), ((0, 2),), -0.2, 0.2)), 32.0, 512.0)
    square_qkv_bias = jnp.clip(jnp.exp(math.log(512.0) - 2.7725887 * jax.random.uniform(seeds[18], (3 * D,), jnp.float32) ** levels(seeds[18], (3 * D,), ((0, 2),), -0.2, 0.2)), 32.0, 512.0)
    square_out_weight = jnp.clip(jnp.exp(math.log(512.0) - 2.7725887 * jax.random.uniform(seeds[19], (D, D), jnp.float32) ** levels(seeds[19], (D, D), ((0, 2),), -0.2, 0.2)), 32.0, 512.0)
    square_fc_weight = jnp.clip(jnp.exp(math.log(512.0) - 2.7725887 * jax.random.uniform(seeds[20], (D, FF), jnp.float32) ** levels(seeds[20], (D, FF), ((0, 2),), -0.2, 0.2)), 32.0, 512.0)
    square_fc_bias = jnp.clip(jnp.exp(math.log(512.0) - 2.7725887 * jax.random.uniform(seeds[21], (FF,), jnp.float32) ** levels(seeds[21], (FF,), ((0, 2),), -0.2, 0.2)), 32.0, 512.0)
    square_proj_weight = jnp.clip(jnp.exp(math.log(512.0) - 2.7725887 * jax.random.uniform(seeds[22], (FF, D), jnp.float32) ** levels(seeds[22], (FF, D), ((0, 2),), -0.2, 0.2)), 32.0, 512.0)
    return {"tokens": tokens, "out_grad": out_grad, "vectors": vectors, "qkv_weight": qkv_weight, "qkv_bias": qkv_bias, "out_weight": out_weight, "fc_weight": fc_weight, "fc_bias": fc_bias, "proj_weight": proj_weight, "mean_vectors": mean_vectors, "mean_qkv_weight": mean_qkv_weight, "mean_qkv_bias": mean_qkv_bias, "mean_out_weight": mean_out_weight, "mean_fc_weight": mean_fc_weight, "mean_fc_bias": mean_fc_bias, "mean_proj_weight": mean_proj_weight, "square_vectors": square_vectors, "square_qkv_weight": square_qkv_weight, "square_qkv_bias": square_qkv_bias, "square_out_weight": square_out_weight, "square_fc_weight": square_fc_weight, "square_fc_bias": square_fc_bias, "square_proj_weight": square_proj_weight}


LN_EPS = 1e-05
ADAM_EPS = 1e-08
BETA_ONE = 0.9
BETA_TWO = 0.95
LEARN_RATE = 0.02
WEIGHT_DECAY = 0.01
HIGHEST = lax.Precision.HIGHEST

@jax.custom_vjp
def low(v):
    return lax.optimization_barrier(v.astype(jnp.bfloat16)).astype(jnp.float32)

@jax.custom_vjp
def low_back(v):
    return v

def low_keep(v):
    return (low(v), None)

def low_pass(kept, grad):
    return (grad,)

def back_keep(v):
    return (v, None)

def back_low(kept, grad):
    return (low(grad),)
low.defvjp(low_keep, low_pass)
low_back.defvjp(back_keep, back_low)

def matmul(left, right):
    return jnp.dot(left, right, precision=HIGHEST, preferred_element_type=jnp.float32)

def layer_norm(inputs, gain, shift):
    centre = inputs - lax.optimization_barrier(jnp.mean(inputs, -1, keepdims=True))
    inv_dev = lax.rsqrt(lax.optimization_barrier(jnp.mean(centre * centre, -1, keepdims=True)) + LN_EPS)
    return centre * inv_dev * gain + shift

def rotary_tables():
    freqs = jnp.power(10000.0, -jnp.arange(0, ROT, 2).astype(jnp.float32) / ROT)
    angles = jnp.arange(LEN).astype(jnp.float32)[:, None] * freqs[None, :]
    angles = jnp.concatenate([angles, angles], -1)[:, None, :]
    return (jnp.cos(angles), jnp.sin(angles))

def rotate(inputs, cosine, sine):
    half_rot = ROT // 2
    leading = inputs[..., :ROT]
    turned = jnp.concatenate([-leading[..., half_rot:], leading[..., :half_rot]], -1)
    return jnp.concatenate([leading * cosine + turned * sine, inputs[..., ROT:]], -1)

def group_pass(params, block):
    vectors, qkv_weight, qkv_bias, out_weight, fc_weight, fc_bias, proj_weight = params
    seq_count = block.shape[0]
    flat = block.reshape(-1, D)
    first_in = low(layer_norm(flat, vectors[0], vectors[1]))
    second_in = low(layer_norm(flat, vectors[2], vectors[3]))
    mixed = low_back(matmul(first_in, qkv_weight) + qkv_bias).reshape(seq_count, LEN, 3, H, HD)
    cosine, sine = rotary_tables()
    queries = low(rotate(mixed[:, :, 0], cosine, sine))
    keys_rot = low(rotate(mixed[:, :, 1], cosine, sine))
    values = low(mixed[:, :, 2])
    scale = HD ** (-0.5)
    scores = low_back(jnp.einsum('sqhd,skhd->shqk', queries, keys_rot, precision=HIGHEST) * scale)
    causal = jnp.arange(LEN)[:, None] >= jnp.arange(LEN)[None, :]
    scores = jnp.where(causal, scores, -1e+30)
    exps = jnp.exp(scores - lax.optimization_barrier(jnp.max(scores, -1, keepdims=True)))
    probs = low(exps / lax.optimization_barrier(jnp.sum(exps, -1, keepdims=True)))
    attended = jnp.einsum('shqk,skhd->sqhd', probs, values, precision=HIGHEST).reshape(-1, D)
    attended = low(low_back(attended))
    attn_out = matmul(attended, out_weight) + vectors[4]
    hidden = low_back(matmul(second_in, fc_weight) + fc_bias)
    activated = low(jax.nn.gelu(hidden, approximate=False))
    mlp_out = matmul(activated, proj_weight) + vectors[5]
    return (flat + attn_out + mlp_out).reshape(block.shape)

def reference(tokens, out_grad, vectors, qkv_weight, qkv_bias, out_weight, fc_weight, fc_bias, proj_weight, mean_vectors, mean_qkv_weight, mean_qkv_bias, mean_out_weight, mean_fc_weight, mean_fc_bias, mean_proj_weight, square_vectors, square_qkv_weight, square_qkv_bias, square_out_weight, square_fc_weight, square_fc_bias, square_proj_weight):
    weights = (vectors, qkv_weight, qkv_bias, out_weight, fc_weight, fc_bias, proj_weight)
    params = tuple((weight.astype(jnp.float32) for weight in weights))
    group_seqs = math.gcd(TOKENS // LEN, max(1, 4096 // LEN))

    def whole(inputs, prm):
        blocks = inputs.reshape(-1, group_seqs, LEN, D)

        def advance(carry, block):
            return (carry, jax.checkpoint(group_pass)(prm, block))
        _, outputs = lax.scan(advance, jnp.zeros((), jnp.float32), blocks)
        return outputs.reshape(-1, D)
    layer_f, pullback = jax.vjp(whole, tokens.astype(jnp.float32), params)
    input_grad, grads = pullback(out_grad.astype(jnp.float32))
    means = (mean_vectors, mean_qkv_weight, mean_qkv_bias, mean_out_weight, mean_fc_weight, mean_fc_bias, mean_proj_weight)
    squares = (square_vectors, square_qkv_weight, square_qkv_bias, square_out_weight, square_fc_weight, square_fc_bias, square_proj_weight)
    fix_one = 1.0 - BETA_ONE ** ADAM_STEP
    fix_two = 1.0 - BETA_TWO ** ADAM_STEP
    steps = []
    new_means = []
    new_squares = []
    for index in range(7):
        gradient = grads[index]
        new_mean = BETA_ONE * means[index] + (1.0 - BETA_ONE) * gradient
        new_square = BETA_TWO * squares[index] + (1.0 - BETA_TWO) * gradient * gradient
        update = -LEARN_RATE * (new_mean / fix_one / (jnp.sqrt(new_square / fix_two) + ADAM_EPS) + WEIGHT_DECAY * params[index])
        steps.append(update)
        new_means.append(new_mean)
        new_squares.append(new_square)
    return (layer_f.astype(jnp.bfloat16), input_grad.astype(jnp.bfloat16), grads[0], grads[1], grads[2], grads[3], grads[4], grads[5], grads[6], steps[0], steps[1], steps[2], steps[3], steps[4], steps[5], steps[6], new_means[0], new_means[1], new_means[2], new_means[3], new_means[4], new_means[5], new_means[6], new_squares[0], new_squares[1], new_squares[2], new_squares[3], new_squares[4], new_squares[5], new_squares[6])
```

```python
import functools

import jax
import jax.numpy as jnp
import numpy as np
from jax import lax
from jax.experimental import pallas as pl
from jax.experimental.pallas import tpu as pltpu
from jax.sharding import PartitionSpec as P

H = 8
ROT = 16
LEN = 512
ADAM_STEP = 10

LN_EPS = 1e-05
ADAM_EPS = 1e-08
BETA_ONE = 0.9
BETA_TWO = 0.95
LEARN_RATE = 0.02
WEIGHT_DECAY = 0.01
FIX_ONE = 1.0 - BETA_ONE**ADAM_STEP
FIX_TWO = 1.0 - BETA_TWO**ADAM_STEP
INV_ROOT_TWO = 0.7071067811865476
INV_ROOT_TWO_PI = 0.3989422804014327

bf16 = jnp.bfloat16
f32 = jnp.float32
SMALL_ROWS = 26


def dot_nn(a, b):
    return lax.dot_general(a, b, (((1,), (0,)), ((), ())), preferred_element_type=f32)


def dot_nt(a, b):
    return lax.dot_general(a, b, (((1,), (1,)), ((), ())), preferred_element_type=f32)


def dot_tn(a, b):
    return lax.dot_general(a, b, (((0,), (0,)), ((), ())), preferred_element_type=f32)


def full_spec(shape):
    zeros = (0,) * len(shape)
    return pl.BlockSpec(shape, lambda *_: zeros)


def cost(flops, moved, transcendentals=0):
    return pl.CostEstimate(
        flops=int(flops), bytes_accessed=int(moved), transcendentals=int(transcendentals)
    )


def vec_row(small_ref, i):
    n = SMALL_ROWS
    rows = [small_ref[o * n + 2 * i + k] for o in range(2) for k in range(2)]
    return jnp.concatenate(rows, 1)


def normalise(x):
    centre = x - jnp.mean(x, -1, keepdims=True)
    inv_dev = lax.rsqrt(jnp.mean(centre * centre, -1, keepdims=True) + LN_EPS)
    return centre * inv_dev, inv_dev


def norm_kernel(tok_ref, small_ref, first_ref, second_ref):
    normed, _ = normalise(tok_ref[...].astype(f32))
    first_ref[...] = (normed * vec_row(small_ref, 0) + vec_row(small_ref, 1)).astype(bf16)
    second_ref[...] = (normed * vec_row(small_ref, 2) + vec_row(small_ref, 3)).astype(bf16)


def norm_call(tokens, small):
    rows, width = tokens.shape
    tile = 512
    spec = pl.BlockSpec((tile, width), lambda i: (i, 0))
    out = jax.ShapeDtypeStruct((rows, width), bf16)
    return pl.pallas_call(
        norm_kernel,
        grid=(rows // tile,),
        in_specs=[spec, full_spec(small.shape)],
        out_specs=[spec, spec],
        out_shape=[out, out],
        cost_estimate=cost(20 * rows * width, 6 * rows * width),
        name="norm",
    )(tokens, small)


def ff_kernel(j, reps, meta, second_ref, grad_ref, fco_ref, fcx_ref, pro_ref, prx_ref, small_ref,
              own_ref, send_ref, act_ref, hg_ref, bias_ref):
    rel = pl.program_id(0)
    c = meta[0]
    idx = meta[1]
    o = rel ^ c
    rows, width = second_ref.shape
    half = width // 2
    cols = act_ref.shape[1]
    rr = own_ref.shape[2]
    proj = jnp.where(rel == 0, pro_ref[...], prx_ref[...])
    fco = fco_ref[...]
    fcx = fcx_ref[...]
    base = o * SMALL_ROWS + 18 + 4 * j
    bias = jnp.concatenate([small_ref[base + k] for k in range(cols // 128)], 1)
    own_lanes = pl.ds(pl.multiple_of(c * half, half), half)
    far_lanes = pl.ds(pl.multiple_of((1 - c) * half, half), half)
    tile = 256

    def block(i, total):
        r = pl.ds(pl.multiple_of(i * tile, tile), tile)
        hidden = dot_nn(second_ref[r, own_lanes], fco) + dot_nn(second_ref[r, far_lanes], fcx) + bias
        act_grad = dot_nt(grad_ref[r, :], proj)
        phi_cap = 0.5 + 0.5 * lax.erf(hidden * INV_ROOT_TWO)
        slope = phi_cap + hidden * (jnp.exp(-0.5 * hidden * hidden) * INV_ROOT_TWO_PI)
        act_ref[r, :] = (hidden * phi_cap).astype(bf16)
        hg = (act_grad * slope).astype(bf16)
        hg_ref[r, :] = hg
        return total + jnp.sum(hg.astype(f32).reshape(tile // 8, 8, cols), 0)

    total = lax.fori_loop(0, rows // tile, block, jnp.zeros((8, cols), f32))
    bias_ref[...] = jnp.sum(total, 0, keepdims=True)[None]

    gp = dot_tn(act_ref[...], grad_ref[...])

    def put_proj(ref):
        for a in range(reps):
            piece = gp[a * 2 * rr : (a + 1) * 2 * rr]
            ref[0, a ^ idx] = jnp.concatenate([piece[:rr], piece[rr:]], 1).astype(bf16)

    pl.when(rel == 0)(lambda: put_proj(own_ref))
    pl.when(rel == 1)(lambda: put_proj(send_ref))
    lanes = pl.ds(pl.multiple_of(o * cols, cols), cols)
    for ref, side in ((own_ref, own_lanes), (send_ref, far_lanes)):
        gf = dot_tn(second_ref[:, side], hg_ref[...])
        for a in range(reps):
            ref[1, a ^ idx, :, lanes] = gf[a * rr : (a + 1) * rr].astype(bf16)


def ff_call(j, reps, meta, second, grad, fc_own, fc_far, proj_own, proj_far, small):
    rows, width = second.shape
    ff = fc_own.shape[1]
    half = width // 2
    cols = ff // 4
    rr = half // reps
    buf = (2, reps, rr, 2 * cols)
    fc_spec = pl.BlockSpec((half, cols), lambda i, m: (0, (i ^ m[0]) * 2 + j))
    proj_spec = pl.BlockSpec((cols, width), lambda i, m: (j, 0))
    grid_spec = pltpu.PrefetchScalarGridSpec(
        num_scalar_prefetch=1,
        grid=(2,),
        in_specs=[
            full_spec((rows, width)),
            full_spec((rows, width)),
            fc_spec,
            fc_spec,
            proj_spec,
            proj_spec,
            full_spec(small.shape),
        ],
        out_specs=[
            full_spec(buf),
            full_spec(buf),
            pl.BlockSpec((rows, cols), lambda i, m: (0, i)),
            pl.BlockSpec((rows, cols), lambda i, m: (0, i)),
            pl.BlockSpec((1, 1, cols), lambda i, m: (i, 0, 0)),
        ],
    )
    return pl.pallas_call(
        functools.partial(ff_kernel, j, reps),
        grid_spec=grid_spec,
        out_shape=[
            jax.ShapeDtypeStruct(buf, bf16),
            jax.ShapeDtypeStruct(buf, bf16),
            jax.ShapeDtypeStruct((rows, 2 * cols), bf16),
            jax.ShapeDtypeStruct((rows, 2 * cols), bf16),
            jax.ShapeDtypeStruct((2, 1, cols), f32),
        ],
        cost_estimate=cost(8 * rows * width * 2 * cols, 4 * rows * width + 8 * rows * cols),
        name=f"feed_forward_{j}",
    )(meta, second, grad, fc_own, fc_far, proj_own, proj_far, small)


def rotate_rows(x, cosine, sine):
    parts = []
    for h in range(2):
        low, high = x[64 * h : 64 * h + 8], x[64 * h + 8 : 64 * h + 16]
        parts += [low * cosine - high * sine, high * cosine + low * sine, x[64 * h + 16 : 64 * h + 64]]
    return jnp.concatenate(parts, 0)


def attention_kernel(j, reps, meta, first_ref, grad_ref, wq_ref, wk_ref, wv_ref, xq_ref, xk_ref, xv_ref,
                     oo_ref, ox_ref, small_ref, trig_ref,
                     own_ref, send_ref, qg_ref, att_ref, bias_ref,
                     wt_ref, bcol_ref, qgs_ref, attt_ref, btot_ref):
    rel = pl.program_id(0)
    s = pl.program_id(1)
    c = meta[0]
    idx = meta[1]
    o = rel ^ c
    rows, width = first_ref.shape
    half = width // 2
    rr = own_ref.shape[2]
    own_lanes = pl.ds(pl.multiple_of(c * half, half), half)
    far_lanes = pl.ds(pl.multiple_of((1 - c) * half, half), half)

    @pl.when(s == 0)
    def _():
        for p, (own, far) in enumerate(((wq_ref, xq_ref), (wk_ref, xk_ref), (wv_ref, xv_ref))):
            wt_ref[128 * p : 128 * (p + 1), own_lanes] = own[...].T
            wt_ref[128 * p : 128 * (p + 1), far_lanes] = far[...].T
            row = p * 4 + o * 2 + j
            owner = row // 6
            bias = small_ref[owner * SMALL_ROWS + 12 + row - 6 * owner]
            bcol_ref[128 * p : 128 * (p + 1), :] = jnp.broadcast_to(bias, (128, 128)).T
        btot_ref[...] = jnp.zeros_like(btot_ref)

    seq = pl.ds(pl.multiple_of(s * LEN, LEN), LEN)
    first = first_ref[seq, :]
    grad = grad_ref[seq, :]
    out_w = jnp.where(rel == 0, oo_ref[...], ox_ref[...])
    mixed = dot_nt(wt_ref[...], first) + bcol_ref[:, :1]
    da_t = dot_nt(out_w, grad).astype(bf16)
    cosine, sine = trig_ref[0], trig_ref[1]
    q_t = rotate_rows(mixed[:128], cosine, sine).astype(bf16) * jnp.asarray(0.125, bf16)
    k_t = rotate_rows(mixed[128:256], cosine, sine).astype(bf16)
    v_t = mixed[256:].astype(bf16)
    k_tok = k_t.T
    v_tok = v_t.T
    hl = LEN // 2
    row_id = lax.broadcasted_iota(jnp.int32, (hl, hl), 0)
    col_id = lax.broadcasted_iota(jnp.int32, (hl, hl), 1)
    keep = row_id <= col_id
    zeros = jnp.zeros((64, LEN), bf16)
    att, dq, dk, dv = [], [], [], []
    for h in range(2):
        hs = slice(64 * h, 64 * h + 64)
        qh, kh, vh, dah = q_t[hs], k_t[hs], v_t[hs], da_t[hs]
        pad = (lambda u: jnp.concatenate([u, zeros], 0)) if h == 0 else (lambda u: jnp.concatenate([zeros, u], 0))
        qz, daz = pad(qh), pad(dah)
        att_h, dq_h = [], []
        dk_h = dv_h = None
        for t in range(2):
            ts = slice(hl * t, hl * t + hl)
            n = hl * (t + 1)
            score = dot_nn(k_tok[:n], qz[:, ts])
            diag = jnp.where(keep, score[n - hl :], -1e30)
            score = diag if t == 0 else jnp.concatenate([score[:hl], diag], 0)
            exps = jnp.exp(score - jnp.max(score, 0, keepdims=True))
            prob = exps * (1.0 / jnp.sum(exps, 0, keepdims=True))
            prob_b = prob.astype(bf16)
            att_h.append(dot_nn(vh[:, :n], prob_b))
            pg = dot_nn(v_tok[:n], daz[:, ts])
            sg = (prob * (pg - jnp.sum(pg * prob, 0, keepdims=True))).astype(bf16)
            dq_h.append(dot_nn(kh[:, :n], sg))
            dv_t = dot_nt(dah[:, ts], prob_b)
            dk_t = dot_nt(qh[:, ts], sg)
            if t == 0:
                dv_h, dk_h = dv_t, dk_t
            else:
                dv_h = jnp.concatenate([dv_h + dv_t[:, :hl], dv_t[:, hl:]], 1)
                dk_h = jnp.concatenate([dk_h + dk_t[:, :hl], dk_t[:, hl:]], 1)
        att.append(jnp.concatenate(att_h, 1))
        dq.append(jnp.concatenate(dq_h, 1) * 0.125)
        dk.append(dk_h)
        dv.append(dv_h)
    att_t = jnp.concatenate(att, 0).astype(bf16)
    dq_t = rotate_rows(jnp.concatenate(dq, 0), cosine, -sine)
    dk_t = rotate_rows(jnp.concatenate(dk, 0), cosine, -sine)
    qkv_t = jnp.concatenate([dq_t, dk_t, jnp.concatenate(dv, 0)], 0).astype(bf16)
    qkv_g = qkv_t.T
    qg_ref[...] = qkv_g
    qgs_ref[seq, :] = qkv_g
    att_ref[...] = att_t.T
    attt_ref[:, seq] = att_t
    btot_ref[...] += jnp.sum(qkv_g.astype(f32).reshape(LEN // 8, 8, 384), 0)

    @pl.when(s == pl.num_programs(1) - 1)
    def _():
        bias_ref[...] = jnp.sum(btot_ref[...], 0, keepdims=True)[None]
        for ref, side in ((own_ref, own_lanes), (send_ref, far_lanes)):
            gw = dot_tn(first_ref[:, side], qgs_ref[...])
            for a in range(reps):
                ref[o, a ^ idx, :, 0:384] = gw[a * rr : (a + 1) * rr].astype(bf16)
        go = dot_nn(attt_ref[...], grad_ref[...])
        hr = rr // 2

        def put_out(ref):
            for a in range(reps):
                piece = go[a * hr : (a + 1) * hr]
                for part in range(2):
                    both = [piece[:, 256 * part + 128 * k : 256 * part + 128 * (k + 1)] for k in range(2)]
                    ref[part, a ^ idx, :, 384:512] = jnp.concatenate(both, 0).astype(bf16)

        pl.when(rel == 0)(lambda: put_out(own_ref))
        pl.when(rel == 1)(lambda: put_out(send_ref))


def trig_tables():
    freqs = np.power(np.float32(10000.0), -np.arange(0, ROT, 2).astype(np.float32) / np.float32(ROT))
    angles = (np.arange(LEN).astype(np.float32)[None, :] * freqs[:, None]).astype(np.float32)
    return np.stack([np.cos(angles), np.sin(angles)]).astype(np.float32)


def attention_call(j, reps, meta, first, grad, qkv_own, qkv_far, out_own, out_far, small, trig):
    rows, width = first.shape
    half = width // 2
    rr = half // reps
    buf = (2, reps, rr, 512)
    w_specs = [
        pl.BlockSpec((half, 128), functools.partial(lambda p, r, s, m: (0, p * 4 + (r ^ m[0]) * 2 + j), p))
        for p in range(3)
    ]
    o_spec = pl.BlockSpec((128, width), lambda r, s, m: (j, 0))
    grid_spec = pltpu.PrefetchScalarGridSpec(
        num_scalar_prefetch=1,
        grid=(2, rows // LEN),
        in_specs=[
            full_spec((rows, width)),
            full_spec((rows, width)),
            *w_specs,
            *w_specs,
            o_spec,
            o_spec,
            full_spec(small.shape),
            full_spec(trig.shape),
        ],
        out_specs=[
            full_spec(buf),
            full_spec(buf),
            pl.BlockSpec((LEN, 384), lambda r, s, m: (s, r)),
            pl.BlockSpec((LEN, 128), lambda r, s, m: (s, r)),
            pl.BlockSpec((1, 1, 384), lambda r, s, m: (r, 0, 0)),
        ],
        scratch_shapes=[
            pltpu.VMEM((384, width), bf16),
            pltpu.VMEM((384, 128), f32),
            pltpu.VMEM((rows, 384), bf16),
            pltpu.VMEM((128, rows), bf16),
            pltpu.VMEM((8, 384), f32),
        ],
    )
    flops = 2 * rows * width * (2 * 768 + 2 * 256) + 4 * 6 * 2 * rows * LEN * 128
    return pl.pallas_call(
        functools.partial(attention_kernel, j, reps),
        grid_spec=grid_spec,
        out_shape=[
            jax.ShapeDtypeStruct(buf, bf16),
            jax.ShapeDtypeStruct(buf, bf16),
            jax.ShapeDtypeStruct((rows, 768), bf16),
            jax.ShapeDtypeStruct((rows, 256), bf16),
            jax.ShapeDtypeStruct((2, 1, 384), f32),
        ],
        cost_estimate=cost(flops, 4 * rows * width + 2 * rows * 1024),
        name=f"attention_{j}",
    )(meta, first, grad, *[qkv_own] * 3, *[qkv_far] * 3, out_own, out_far, small, trig)


def output_kernel(meta, tok_ref, grad_ref, at0_ref, at1_ref, ac0_ref, ac1_ref, hg0_ref, hg1_ref, qg0_ref, qg1_ref,
                  oo_ref, ox_ref, po_ref, px_ref, fo_ref, fx_ref, wo_ref, wx_ref, small_ref,
                  qb0_ref, qb1_ref, fb0_ref, fb1_ref,
                  lay_ref, tg_ref, own_ref, send_ref,
                  wgo_ref, wgx_ref, sg_ref, fg_ref, tot_ref, qb_ref):
    i = pl.program_id(0)
    c = meta[0]
    tile, width = tok_ref.shape
    half = width // 2
    own_lanes = pl.ds(pl.multiple_of(c * half, half), half)
    far_lanes = pl.ds(pl.multiple_of((1 - c) * half, half), half)

    @pl.when(i == 0)
    def _():
        for w_ref, g_ref in ((wo_ref, wgo_ref), (wx_ref, wgx_ref)):
            for j in range(2):
                for rel in range(2):
                    for p in range(3):
                        src = pl.ds(pl.multiple_of((p * 4 + (rel ^ c) * 2 + j) * 128, 128), 128)
                        dst = (j * 6 + rel * 3 + p) * 128
                        g_ref[:, dst : dst + 128] = w_ref[:, src]
        tot_ref[...] = jnp.zeros_like(tot_ref)

    x = tok_ref[...].astype(f32)
    grad = grad_ref[...].astype(f32)
    normed, inv_dev = normalise(x)
    at0, at1 = at0_ref[...], at1_ref[...]
    acc = dot_nn(jnp.concatenate([at0[:, :128], at1[:, :128]], 1), oo_ref[...])
    acc += dot_nn(jnp.concatenate([at0[:, 128:], at1[:, 128:]], 1), ox_ref[...])
    for j, ac_ref in enumerate((ac0_ref, ac1_ref)):
        acc += dot_nn(ac_ref[:, :512], po_ref[512 * j : 512 * (j + 1), :])
        acc += dot_nn(ac_ref[:, 512:], px_ref[512 * j : 512 * (j + 1), :])
    lay_ref[...] = (x + acc + (vec_row(small_ref, 4) + vec_row(small_ref, 5))).astype(bf16)

    for f_ref, wg_ref, lanes in ((fo_ref, wgo_ref, own_lanes), (fx_ref, wgx_ref, far_lanes)):
        total = None
        for j, hg_ref in enumerate((hg0_ref, hg1_ref)):
            for rel in range(2):
                cols = pl.ds(pl.multiple_of((rel ^ c) * 1024 + 512 * j, 512), 512)
                term = dot_nt(hg_ref[:, 512 * rel : 512 * (rel + 1)], f_ref[:, cols])
                total = term if total is None else total + term
        sg_ref[:, lanes] = total
        fg_ref[:, lanes] = dot_nt(qg0_ref[...], wg_ref[:, :768]) + dot_nt(qg1_ref[...], wg_ref[:, 768:])
    second_g = sg_ref[...]
    first_g = fg_ref[...]
    e = first_g * vec_row(small_ref, 0) + second_g * vec_row(small_ref, 2)
    ln = inv_dev * (
        e - jnp.mean(e, -1, keepdims=True) - normed * jnp.mean(e * normed, -1, keepdims=True)
    )
    tg_ref[...] = (grad + ln).astype(bf16)
    for k, term in enumerate((first_g * normed, first_g, second_g * normed, second_g, grad)):
        tot_ref[k] += jnp.sum(term.reshape(tile // 8, 8, width), 0)

    @pl.when(i == pl.num_programs(0) - 1)
    def _():
        for j, b_ref in enumerate((qb0_ref, qb1_ref)):
            for rel in range(2):
                for p in range(3):
                    qb_ref[p * 4 + (rel ^ c) * 2 + j] = b_ref[rel][:, 128 * p : 128 * (p + 1)]
        sums = [jnp.sum(tot_ref[k], 0, keepdims=True) for k in range(5)]
        sums.append(sums[4])
        for ref, rel in ((own_ref, 0), (send_ref, 1)):
            owner = rel ^ c
            for k in range(6):
                for part in range(2):
                    low = sums[k][:, 128 * part : 128 * (part + 1)]
                    high = sums[k][:, 256 + 128 * part : 256 + 128 * (part + 1)]
                    ref[2 * k + part] = jnp.where(owner == 0, low, high)
            for k in range(6):
                ref[12 + k] = qb_ref[owner * 6 + k]
            for j, b_ref in enumerate((fb0_ref, fb1_ref)):
                for k in range(4):
                    ref[18 + 4 * j + k] = b_ref[rel][:, 128 * k : 128 * (k + 1)]
            for k in range(SMALL_ROWS, 32):
                ref[k] = jnp.zeros((1, 128), f32)


def output_call(meta, tokens, grad, atts, acts, hgs, qgs, out_w, proj_w, fc_w, qkv_w, small, qbs, fbs):
    rows, width = tokens.shape
    tile = 256
    blk = lambda n: pl.BlockSpec((tile, n), lambda i, m: (i, 0))
    weights = [*out_w, *proj_w, *fc_w, *qkv_w]
    tail = [small, *qbs, *fbs]
    packed = (32, 1, 128)
    grid_spec = pltpu.PrefetchScalarGridSpec(
        num_scalar_prefetch=1,
        grid=(rows // tile,),
        in_specs=[
            blk(width),
            blk(width),
            *[blk(a.shape[1]) for a in (*atts, *acts, *hgs, *qgs)],
            *[full_spec(w.shape) for w in weights],
            *[full_spec(w.shape) for w in tail],
        ],
        out_specs=[blk(width), blk(width), full_spec(packed), full_spec(packed)],
        scratch_shapes=[
            pltpu.VMEM(qkv_w[0].shape, bf16),
            pltpu.VMEM(qkv_w[0].shape, bf16),
            pltpu.VMEM((tile, width), f32),
            pltpu.VMEM((tile, width), f32),
            pltpu.VMEM((5, 8, width), f32),
            pltpu.VMEM((12, 1, 128), f32),
        ],
    )
    return pl.pallas_call(
        output_kernel,
        grid_spec=grid_spec,
        out_shape=[
            jax.ShapeDtypeStruct((rows, width), bf16),
            jax.ShapeDtypeStruct((rows, width), bf16),
            jax.ShapeDtypeStruct(packed, f32),
            jax.ShapeDtypeStruct(packed, f32),
        ],
        cost_estimate=cost(2 * rows * width * (512 + 2048 * 2 + 1536), 2 * rows * (4 * 512 + 4 * 2048)),
        name="outputs",
    )(meta, tokens, grad, *atts, *acts, *hgs, *qgs, *weights, *tail)


def sum_kernel(n_in, groups_out, *refs):
    parts = len(groups_out)
    ins, outs = refs[: parts * n_in], refs[parts * n_in :]
    k = 0
    for part, count in enumerate(groups_out):
        terms = [r for r in ins[part * n_in : (part + 1) * n_in]]
        rows = terms[0].shape[0] // count
        for piece in range(count):
            sl = slice(piece * rows, (piece + 1) * rows)
            total = terms[0][sl].astype(f32)
            for t in terms[1:]:
                total += t[sl].astype(f32)
            outs[k][...] = total.astype(outs[k].dtype)
            k += 1


def sum_call(parts, count, name):
    n_in = len(parts[0])
    ins = [a for part in parts for a in part]
    outs = []
    for part in parts:
        a = part[0]
        outs += [jax.ShapeDtypeStruct((a.shape[0] // count, *a.shape[1:]), a.dtype)] * count
    moved = sum(a.size * a.dtype.itemsize for a in ins)
    got = pl.pallas_call(
        functools.partial(sum_kernel, n_in, [count] * len(parts)),
        out_shape=outs,
        cost_estimate=cost(moved, 2 * moved),
        name=name,
    )(*ins)
    return [got[i * count : (i + 1) * count] for i in range(len(parts))]


def join_kernel(n_in, *refs):
    parts = len(refs) // (n_in + 1)
    for part in range(parts):
        out = refs[parts * n_in + part]
        rows = out.shape[0] // n_in
        for k in range(n_in):
            out[k * rows : (k + 1) * rows] = refs[part * n_in + k][...]


def join_call(parts, name):
    n_in = len(parts[0])
    ins = [a for part in parts for a in part]
    outs = [
        jax.ShapeDtypeStruct((part[0].shape[0] * n_in, *part[0].shape[1:]), part[0].dtype) for part in parts
    ]
    moved = sum(a.size * a.dtype.itemsize for a in ins)
    return pl.pallas_call(
        functools.partial(join_kernel, n_in),
        out_shape=outs,
        cost_estimate=cost(0, 2 * moved),
        name=name,
    )(*ins)


def exchange(a, reps, mask):
    return lax.ppermute(a, "rep", [(i, i ^ mask) for i in range(reps)])


def swap(a):
    return lax.ppermute(a, "opt", [(0, 1), (1, 0)])


def bit_groups(reps):
    bits = reps.bit_length() - 1
    return [(lo, min(2, bits - lo)) for lo in range(0, bits, 2)]


def relative_base(index, reps):
    out = 0
    for lo, n in bit_groups(reps):
        out = (out << n) | ((index >> lo) & ((1 << n) - 1))
    return out


def reduce_set(own, received, reps, tag):
    groups = bit_groups(reps)
    parts = None
    n = 1 << groups[0][1]
    w = own.shape[1:]
    own2, rec2 = own.reshape(2 * w[0], *w[1:]), received.reshape(2 * w[0], *w[1:])
    (pieces,) = sum_call([[own2, rec2]], 2 * n, f"{tag}_pair")
    pieces = [pieces[:n], pieces[n:]]
    for g, (lo, bits) in enumerate(groups):
        terms = [
            [part[0], *[exchange(part[k], reps, k << lo) for k in range(1, 1 << bits)]] for part in pieces
        ]
        n = 1 << groups[g + 1][1] if g + 1 < len(groups) else 1
        pieces = sum_call(terms, n, f"{tag}_sum{g}")
    parts = [part[0] for part in pieces]
    for g, (lo, bits) in reversed(list(enumerate(groups))):
        pieces = [
            [part, *[exchange(part, reps, k << lo) for k in range(1, 1 << bits)]] for part in parts
        ]
        if g:
            parts = join_call(pieces, f"{tag}_join{g}")
    return pieces


def adamw(grad, mean, square, weight):
    new_mean = BETA_ONE * mean + (1.0 - BETA_ONE) * grad
    new_square = BETA_TWO * square + (1.0 - BETA_TWO) * grad * grad
    step = -LEARN_RATE * (
        new_mean * (1.0 / FIX_ONE) / (jnp.sqrt(new_square * (1.0 / FIX_TWO)) + ADAM_EPS)
        + WEIGHT_DECAY * weight.astype(f32)
    )
    return step, new_mean, new_square


def pick(refs, which, row, cols):
    out = refs[0][row, :, cols]
    for k in range(1, len(refs)):
        out = jnp.where(which == k, refs[k][row, :, cols], out)
    return out.astype(f32)


def adam_block(grad, m_ref, s_ref, w_ref, g_out, st_out, m_out, s_out, at):
    step, mean, square = adamw(grad, m_ref[at], s_ref[at], w_ref[at])
    g_out[at] = grad
    st_out[at] = step
    m_out[at] = mean
    s_out[at] = square


def adam_ff_kernel(n, low, meta, *refs):
    pieces, refs = refs[: 4 * n], refs[4 * n :]
    proj, fc = refs[0:3], refs[3:6]
    proj_out, fc_out = refs[6:10], refs[10:14]
    q = pl.program_id(0)
    idx = meta[1]
    which = q ^ (idx // low)
    idx_low = idx % low
    for j in range(2):
        p_refs = pieces[2 * n * j : 2 * n * j + n]
        f_refs = pieces[2 * n * j + n : 2 * n * j + 2 * n]
        rr = p_refs[0].shape[1]
        for z in range(low):
            row = z ^ idx_low
            for k in range(2):
                grad = pick(p_refs, which, row, slice(512 * k, 512 * k + 512))
                at = (j, slice((2 * z + k) * rr, (2 * z + k + 1) * rr), slice(None))
                adam_block(grad, *proj, *proj_out, at)
                grad = pick(f_refs, which, row, slice(512 * k, 512 * k + 512))
                at = (slice(z * rr, (z + 1) * rr), slice(1024 * k + 512 * j, 1024 * k + 512 * j + 512))
                adam_block(grad, *fc, *fc_out, at)


def adam_qkv_kernel(n, low, meta, *refs):
    pieces, refs = refs[: 4 * n], refs[4 * n :]
    qkv, out = refs[0:3], refs[3:6]
    qkv_out, out_out = refs[6:10], refs[10:14]
    q = pl.program_id(0)
    idx = meta[1]
    which = q ^ (idx // low)
    idx_low = idx % low
    for j in range(2):
        for part in range(2):
            g_refs = pieces[2 * n * j + n * part : 2 * n * j + n * part + n]
            rr = g_refs[0].shape[1]
            hr = rr // 2
            for z in range(low):
                grad = pick(g_refs, which, z ^ idx_low, slice(None))
                for p in range(3):
                    col = (p * 4 + part * 2 + j) * 128
                    at = (slice(z * rr, (z + 1) * rr), slice(col, col + 128))
                    adam_block(grad[:, 128 * p : 128 * (p + 1)], *qkv, *qkv_out, at)
                for k in range(2):
                    col = 256 * part + 128 * k
                    at = (j, slice(z * hr, (z + 1) * hr), slice(col, col + 128))
                    adam_block(grad[k * hr : (k + 1) * hr, 384:], *out, *out_out, at)


def adam_call(kernel, reps, meta, sets, first, second, first_spec, second_spec, name):
    pieces = [a for pair in sets for part in pair for a in part]
    n = len(sets[0][0])
    low = reps // n
    ins = [*pieces, *first, *second]
    outs = [jax.ShapeDtypeStruct(first[0].shape, f32)] * 4 + [jax.ShapeDtypeStruct(second[0].shape, f32)] * 4
    grid_spec = pltpu.PrefetchScalarGridSpec(
        num_scalar_prefetch=1,
        grid=(n,),
        in_specs=[*[full_spec(a.shape) for a in pieces], *[first_spec] * 3, *[second_spec] * 3],
        out_specs=[*[first_spec] * 4, *[second_spec] * 4],
    )
    size = first[0].size + second[0].size
    return pl.pallas_call(
        functools.partial(kernel, n, low),
        grid_spec=grid_spec,
        out_shape=outs,
        cost_estimate=cost(20 * size, 28 * size),
        name=name,
    )(meta, *ins)


def body(
    tokens,
    out_grad,
    vectors,
    qkv_weight,
    qkv_bias,
    out_weight,
    fc_weight,
    fc_bias,
    proj_weight,
    mean_vectors,
    mean_qkv_weight,
    mean_qkv_bias,
    mean_out_weight,
    mean_fc_weight,
    mean_fc_bias,
    mean_proj_weight,
    square_vectors,
    square_qkv_weight,
    square_qkv_bias,
    square_out_weight,
    square_fc_weight,
    square_fc_bias,
    square_proj_weight,
):
    reps = lax.axis_size("rep")
    c = lax.axis_index("opt")
    idx = relative_base(lax.axis_index("rep"), reps)
    meta = jnp.stack([c, idx]).astype(jnp.int32)
    trig = jnp.asarray(trig_tables())

    packed = jnp.concatenate(
        [vectors.reshape(12, 128), qkv_bias.reshape(6, 128), fc_bias.reshape(8, 128)], 0
    )
    small = lax.all_gather(packed, "opt", axis=0, tiled=True).astype(f32).reshape(2 * SMALL_ROWS, 1, 128)
    fc_far = swap(fc_weight)
    proj_far = swap(proj_weight)
    qkv_far = swap(qkv_weight)
    out_far = swap(out_weight)

    first, second = norm_call(tokens, small)
    ff = [
        ff_call(j, reps, meta, second, out_grad, fc_weight, fc_far, proj_weight, proj_far, small)
        for j in range(2)
    ]
    ff_sets = [reduce_set(r[0], swap(r[1]), reps, f"ff{j}") for j, r in enumerate(ff)]
    att = [
        attention_call(j, reps, meta, first, out_grad, qkv_weight, qkv_far, out_weight, out_far, small, trig)
        for j in range(2)
    ]
    att_sets = [reduce_set(r[0], swap(r[1]), reps, f"att{j}") for j, r in enumerate(att)]
    layer_out, tokens_grad, small_own, small_send = output_call(
        meta,
        tokens,
        out_grad,
        [r[3] for r in att],
        [r[2] for r in ff],
        [r[3] for r in ff],
        [r[2] for r in att],
        (out_weight, out_far),
        (proj_weight, proj_far),
        (fc_weight, fc_far),
        (qkv_weight, qkv_far),
        small,
        [r[4] for r in att],
        [r[4] for r in ff],
    )

    ((total,),) = sum_call([[small_own, swap(small_send)]], 1, "small_pair")
    for g, (lo, bits) in enumerate(bit_groups(reps)):
        terms = [total, *[exchange(total, reps, k << lo) for k in range(1, 1 << bits)]]
        ((total,),) = sum_call([terms], 1, f"small_sum{g}")
    flat = total.reshape(32, 128)
    g_vec = flat[:12].reshape(6, 256)
    g_qb = flat[12:18].reshape(768)
    g_fb = flat[18:26].reshape(1024)

    n = 1 << bit_groups(reps)[0][1]
    view = lambda a: a.reshape(2, 512, 512)
    fq = proj_weight.shape[0] // 2 // n
    proj_adam = adam_call(
        adam_ff_kernel,
        reps,
        meta,
        ff_sets,
        [view(a) for a in (mean_proj_weight, square_proj_weight, proj_weight)],
        [mean_fc_weight, square_fc_weight, fc_weight],
        pl.BlockSpec((2, fq, 512), lambda q, m: (0, q, 0)),
        pl.BlockSpec((256 // n, 2048), lambda q, m: (q, 0)),
        "adam_ff",
    )
    a_proj = [a.reshape(1024, 512) for a in proj_adam[:4]]
    a_fc = proj_adam[4:]
    view_o = lambda a: a.reshape(2, 128, 512)
    qkv_adam = adam_call(
        adam_qkv_kernel,
        reps,
        meta,
        att_sets,
        [mean_qkv_weight, square_qkv_weight, qkv_weight],
        [view_o(a) for a in (mean_out_weight, square_out_weight, out_weight)],
        pl.BlockSpec((256 // n, 1536), lambda q, m: (q, 0)),
        pl.BlockSpec((2, 128 // n, 512), lambda q, m: (0, q, 0)),
        "adam_qkv",
    )
    a_qkv = qkv_adam[:4]
    a_out = [a.reshape(256, 512) for a in qkv_adam[4:]]
    a_vec = (g_vec, *adamw(g_vec, mean_vectors, square_vectors, vectors))
    a_qb = (g_qb, *adamw(g_qb, mean_qkv_bias, square_qkv_bias, qkv_bias))
    a_fb = (g_fb, *adamw(g_fb, mean_fc_bias, square_fc_bias, fc_bias))
    order = (a_vec, a_qkv, a_qb, a_out, a_fc, a_fb, a_proj)
    return (layer_out, tokens_grad, *[a[k] for k in range(4) for a in order])


def solution(mesh):
    rows = P(("rep", "opt"), None)
    weights = (P(None, "opt"), P("opt", None), P("opt"), P("opt", None), P("opt", None), P("opt"), P("opt", None))
    in_specs = (rows, rows, *weights, *weights, *weights)
    out_specs = (rows, rows, *weights, *weights, *weights, *weights)
    return jax.shard_map(body, mesh=mesh, in_specs=in_specs, out_specs=out_specs, check_vma=False)
```

```python
import functools

import jax
import jax.numpy as jnp
import numpy as np
from jax import lax
from jax.experimental import pallas as pl
from jax.experimental.pallas import tpu as pltpu
from jax.sharding import PartitionSpec as P

H = 8
ROT = 16
LEN = 512
ADAM_STEP = 10

LN_EPS = 1e-05
ADAM_EPS = 1e-08
BETA_ONE = 0.9
BETA_TWO = 0.95
LEARN_RATE = 0.02
WEIGHT_DECAY = 0.01
FIX_ONE = 1.0 - BETA_ONE**ADAM_STEP
FIX_TWO = 1.0 - BETA_TWO**ADAM_STEP
INV_ROOT_TWO = 0.7071067811865476
INV_ROOT_TWO_PI = 0.3989422804014327

bf16 = jnp.bfloat16
f32 = jnp.float32
SMALL_ROWS = 26


def dot_nn(a, b):
    return lax.dot_general(a, b, (((1,), (0,)), ((), ())), preferred_element_type=f32)


def dot_nt(a, b):
    return lax.dot_general(a, b, (((1,), (1,)), ((), ())), preferred_element_type=f32)


def dot_tn(a, b):
    return lax.dot_general(a, b, (((0,), (0,)), ((), ())), preferred_element_type=f32)


def full_spec(shape):
    zeros = (0,) * len(shape)
    return pl.BlockSpec(shape, lambda *_: zeros)


def cost(flops, moved, transcendentals=0):
    return pl.CostEstimate(
        flops=int(flops), bytes_accessed=int(moved), transcendentals=int(transcendentals)
    )


def vec_row(small_ref, i):
    n = SMALL_ROWS
    rows = [small_ref[o * n + 2 * i + k] for o in range(2) for k in range(2)]
    return jnp.concatenate(rows, 1)


def normalise(x):
    centre = x - jnp.mean(x, -1, keepdims=True)
    inv_dev = lax.rsqrt(jnp.mean(centre * centre, -1, keepdims=True) + LN_EPS)
    return centre * inv_dev, inv_dev


def norm_kernel(tok_ref, small_ref, first_ref, second_ref):
    normed, _ = normalise(tok_ref[...].astype(f32))
    first_ref[...] = (normed * vec_row(small_ref, 0) + vec_row(small_ref, 1)).astype(bf16)
    second_ref[...] = (normed * vec_row(small_ref, 2) + vec_row(small_ref, 3)).astype(bf16)


def norm_call(tokens, small):
    rows, width = tokens.shape
    tile = 512
    spec = pl.BlockSpec((tile, width), lambda i: (i, 0))
    out = jax.ShapeDtypeStruct((rows, width), bf16)
    return pl.pallas_call(
        norm_kernel,
        grid=(rows // tile,),
        in_specs=[spec, full_spec(small.shape)],
        out_specs=[spec, spec],
        out_shape=[out, out],
        cost_estimate=cost(20 * rows * width, 6 * rows * width),
        name="norm",
        compiler_params=pltpu.CompilerParams(vmem_limit_bytes=12 << 20),
    )(tokens, small)


def ff_kernel(meta, second_ref, grad_ref, fco_ref, fcx_ref, pro_ref, prx_ref, small_ref,
              own_ref, send_ref, act_ref, hg_ref, bias_ref, fc_ref):
    j = pl.program_id(0)
    rel = pl.program_id(1)
    c = meta[0]
    rank, far_rank = meta[1], meta[2]
    o = rel ^ c
    rows, width = second_ref.shape
    half = width // 2
    cols = act_ref.shape[1]
    quarter = half // 4
    proj = jnp.where(rel == 0, pro_ref[...], prx_ref[...])
    own_lanes = pl.ds(pl.multiple_of(c * half, half), half)
    far_lanes = pl.ds(pl.multiple_of((1 - c) * half, half), half)
    fc_ref[own_lanes, :] = fco_ref[...]
    fc_ref[far_lanes, :] = fcx_ref[...]
    fc = fc_ref[...]
    base = o * SMALL_ROWS + 18 + 4 * j
    bias = jnp.concatenate([small_ref[base + k] for k in range(cols // 128)], 1)
    tile = 256

    def block(i, total):
        r = pl.ds(pl.multiple_of(i * tile, tile), tile)
        hidden = dot_nn(second_ref[r, :], fc) + bias
        act_grad = dot_nt(grad_ref[r, :], proj)
        phi_cap = 0.5 + 0.5 * lax.erf(hidden * INV_ROOT_TWO)
        slope = phi_cap + hidden * (jnp.exp(-0.5 * hidden * hidden) * INV_ROOT_TWO_PI)
        act_ref[r, :] = (hidden * phi_cap).astype(bf16)
        hg = (act_grad * slope).astype(bf16)
        hg_ref[r, :] = hg
        return total + jnp.sum(hg.astype(f32).reshape(tile // 8, 8, cols), 0)

    total = lax.fori_loop(0, rows // tile, block, jnp.zeros((8, cols), f32))
    bias_ref[...] = jnp.sum(total, 0, keepdims=True)[None]

    gp = dot_tn(act_ref[...], grad_ref[...])
    pcols = pl.ds(pl.multiple_of(j * 1024, 1024), 1024)

    def put_proj(ref, number):
        for a in range(4):
            piece = gp[a * 2 * quarter : (a + 1) * 2 * quarter]
            ref[a ^ number, :, pcols] = jnp.concatenate([piece[:quarter], piece[quarter:]], 1).astype(bf16)

    pl.when(rel == 0)(lambda: put_proj(own_ref, rank))
    pl.when(rel == 1)(lambda: put_proj(send_ref, far_rank))
    lanes = pl.ds(pl.multiple_of(2048 + o * 1024 + j * cols, cols), cols)
    for ref, side, number in ((own_ref, own_lanes, rank), (send_ref, far_lanes, far_rank)):
        gf = dot_tn(second_ref[:, side], hg_ref[...])
        for a in range(4):
            ref[a ^ number, :, lanes] = gf[a * quarter : (a + 1) * quarter].astype(bf16)


def ff_call(meta, second, grad, fc_own, fc_far, proj_own, proj_far, small):
    rows, width = second.shape
    ff = fc_own.shape[1]
    half = width // 2
    cols = ff // 4
    buf = (4, half // 4, 2 * ff)
    fc_spec = pl.BlockSpec((half, cols), lambda j, r, m: (0, (r ^ m[0]) * 2 + j))
    proj_spec = pl.BlockSpec((cols, width), lambda j, r, m: (j, 0))
    act_spec = pl.BlockSpec((rows, cols), lambda j, r, m: (0, 2 * j + r))
    grid_spec = pltpu.PrefetchScalarGridSpec(
        num_scalar_prefetch=1,
        grid=(2, 2),
        in_specs=[
            full_spec((rows, width)),
            full_spec((rows, width)),
            fc_spec,
            fc_spec,
            proj_spec,
            proj_spec,
            full_spec(small.shape),
        ],
        out_specs=[
            full_spec(buf),
            full_spec(buf),
            act_spec,
            act_spec,
            pl.BlockSpec((1, 1, cols), lambda j, r, m: (2 * j + r, 0, 0)),
        ],
        scratch_shapes=[pltpu.VMEM((width, cols), bf16)],
    )
    return pl.pallas_call(
        ff_kernel,
        grid_spec=grid_spec,
        out_shape=[
            jax.ShapeDtypeStruct(buf, bf16),
            jax.ShapeDtypeStruct(buf, bf16),
            jax.ShapeDtypeStruct((rows, ff), bf16),
            jax.ShapeDtypeStruct((rows, ff), bf16),
            jax.ShapeDtypeStruct((4, 1, cols), f32),
        ],
        cost_estimate=cost(8 * rows * width * ff, 4 * rows * width + 4 * rows * ff),
        name="feed_forward",
        compiler_params=pltpu.CompilerParams(vmem_limit_bytes=40 << 20),
    )(meta, second, grad, fc_own, fc_far, proj_own, proj_far, small)


def rotate_rows(x, cosine, sine):
    parts = []
    for h in range(2):
        low, high = x[64 * h : 64 * h + 8], x[64 * h + 8 : 64 * h + 16]
        parts += [low * cosine - high * sine, high * cosine + low * sine, x[64 * h + 16 : 64 * h + 64]]
    return jnp.concatenate(parts, 0)


def attention_kernel(j, rel, meta, first_ref, grad_ref, wq_ref, wk_ref, wv_ref, xq_ref, xk_ref, xv_ref,
                     ow_ref, small_ref, trig_ref,
                     own_ref, send_ref, og_ref, qg_ref, att_ref, bias_ref,
                     wt_ref, bcol_ref, qgs_ref, attt_ref, btot_ref):
    s = pl.program_id(0)
    c = meta[0]
    rank, far_rank = meta[1], meta[2]
    o = rel ^ c
    rows, width = first_ref.shape
    half = width // 2
    quarter = half // 4
    own_lanes = pl.ds(pl.multiple_of(c * half, half), half)
    far_lanes = pl.ds(pl.multiple_of((1 - c) * half, half), half)

    @pl.when(s == 0)
    def _():
        for p, (own, far) in enumerate(((wq_ref, xq_ref), (wk_ref, xk_ref), (wv_ref, xv_ref))):
            wt_ref[128 * p : 128 * (p + 1), own_lanes] = own[...].T
            wt_ref[128 * p : 128 * (p + 1), far_lanes] = far[...].T
            row = p * 4 + o * 2 + j
            owner = row // 6
            bias = small_ref[owner * SMALL_ROWS + 12 + row - 6 * owner]
            bcol_ref[128 * p : 128 * (p + 1), :] = jnp.broadcast_to(bias, (128, 128)).T
        btot_ref[...] = jnp.zeros_like(btot_ref)

    seq = pl.ds(pl.multiple_of(s * LEN, LEN), LEN)
    first = first_ref[seq, :]
    grad = grad_ref[seq, :]
    mixed = dot_nt(wt_ref[...], first) + bcol_ref[:, :1]
    da_t = dot_nt(ow_ref[...], grad).astype(bf16)
    cosine, sine = trig_ref[0], trig_ref[1]
    q_t = rotate_rows(mixed[:128], cosine, sine).astype(bf16) * jnp.asarray(0.125, bf16)
    k_t = rotate_rows(mixed[128:256], cosine, sine).astype(bf16)
    v_t = mixed[256:].astype(bf16)
    k_tok = k_t.T
    v_tok = v_t.T
    hl = LEN // 2
    row_id = lax.broadcasted_iota(jnp.int32, (hl, hl), 0)
    col_id = lax.broadcasted_iota(jnp.int32, (hl, hl), 1)
    keep = row_id <= col_id
    zeros = jnp.zeros((64, LEN), bf16)
    att, dq, dk, dv = [], [], [], []
    for h in range(2):
        hs = slice(64 * h, 64 * h + 64)
        qh, kh, vh, dah = q_t[hs], k_t[hs], v_t[hs], da_t[hs]
        pad = (lambda u: jnp.concatenate([u, zeros], 0)) if h == 0 else (lambda u: jnp.concatenate([zeros, u], 0))
        qz, daz = pad(qh), pad(dah)
        att_h, dq_h = [], []
        dk_h = dv_h = None
        for t in range(2):
            ts = slice(hl * t, hl * t + hl)
            n = hl * (t + 1)
            score = dot_nn(k_tok[:n], qz[:, ts])
            diag = jnp.where(keep, score[n - hl :], -1e30)
            score = diag if t == 0 else jnp.concatenate([score[:hl], diag], 0)
            exps = jnp.exp(score - jnp.max(score, 0, keepdims=True))
            prob = exps * (1.0 / jnp.sum(exps, 0, keepdims=True))
            prob_b = prob.astype(bf16)
            att_h.append(dot_nn(vh[:, :n], prob_b))
            pg = dot_nn(v_tok[:n], daz[:, ts])
            sg = (prob * (pg - jnp.sum(pg * prob, 0, keepdims=True))).astype(bf16)
            dq_h.append(dot_nn(kh[:, :n], sg))
            dv_t = dot_nt(dah[:, ts], prob_b)
            dk_t = dot_nt(qh[:, ts], sg)
            if t == 0:
                dv_h, dk_h = dv_t, dk_t
            else:
                dv_h = jnp.concatenate([dv_h + dv_t[:, :hl], dv_t[:, hl:]], 1)
                dk_h = jnp.concatenate([dk_h + dk_t[:, :hl], dk_t[:, hl:]], 1)
        att.append(jnp.concatenate(att_h, 1))
        dq.append(jnp.concatenate(dq_h, 1) * 0.125)
        dk.append(dk_h)
        dv.append(dv_h)
    att_t = jnp.concatenate(att, 0).astype(bf16)
    dq_t = rotate_rows(jnp.concatenate(dq, 0), cosine, -sine)
    dk_t = rotate_rows(jnp.concatenate(dk, 0), cosine, -sine)
    qkv_t = jnp.concatenate([dq_t, dk_t, jnp.concatenate(dv, 0)], 0).astype(bf16)
    qkv_g = qkv_t.T
    qg_ref[...] = qkv_g
    qgs_ref[seq, :] = qkv_g
    att_ref[...] = att_t.T
    attt_ref[:, seq] = att_t
    btot_ref[...] += jnp.sum(qkv_g.astype(f32).reshape(LEN // 8, 8, 384), 0)

    @pl.when(s == pl.num_programs(0) - 1)
    def _():
        bias_ref[...] = jnp.sum(btot_ref[...], 0, keepdims=True)
        for ref, side, number in ((own_ref, own_lanes, rank), (send_ref, far_lanes, far_rank)):
            gw = dot_tn(first_ref[:, side], qgs_ref[...])
            for a in range(4):
                ref[a ^ number] = gw[a * quarter : (a + 1) * quarter].astype(bf16)
        go = dot_nn(attt_ref[...], grad_ref[...])
        hq = quarter // 2
        for a in range(4):
            piece = go[a * hq : (a + 1) * hq]
            og_ref[a ^ (far_rank if rel else rank)] = jnp.concatenate([piece[:, :256], piece[:, 256:]], 0).astype(bf16)


def trig_tables():
    freqs = np.power(np.float32(10000.0), -np.arange(0, ROT, 2).astype(np.float32) / np.float32(ROT))
    angles = (np.arange(LEN).astype(np.float32)[None, :] * freqs[:, None]).astype(np.float32)
    return np.stack([np.cos(angles), np.sin(angles)]).astype(np.float32)


def attention_call(j, rel, meta, first, grad, qkv_own, qkv_far, out_w, small, trig):
    rows, width = first.shape
    half = width // 2
    qbuf = (4, half // 4, 384)
    obuf = (4, half // 4, 256)
    w_specs = [
        pl.BlockSpec((half, 128), functools.partial(lambda p, s, m: (0, p * 4 + (rel ^ m[0]) * 2 + j), p))
        for p in range(3)
    ]
    grid_spec = pltpu.PrefetchScalarGridSpec(
        num_scalar_prefetch=1,
        grid=(rows // LEN,),
        in_specs=[
            full_spec((rows, width)),
            full_spec((rows, width)),
            *w_specs,
            *w_specs,
            pl.BlockSpec((128, width), lambda s, m: (j, 0)),
            full_spec(small.shape),
            full_spec(trig.shape),
        ],
        out_specs=[
            full_spec(qbuf),
            full_spec(qbuf),
            full_spec(obuf),
            pl.BlockSpec((LEN, 384), lambda s, m: (s, 0)),
            pl.BlockSpec((LEN, 128), lambda s, m: (s, 0)),
            full_spec((1, 384)),
        ],
        scratch_shapes=[
            pltpu.VMEM((384, width), bf16),
            pltpu.VMEM((384, 128), f32),
            pltpu.VMEM((rows, 384), bf16),
            pltpu.VMEM((128, rows), bf16),
            pltpu.VMEM((8, 384), f32),
        ],
    )
    flops = 2 * rows * width * (2 * 384 + 2 * 128) + 2 * 6 * 2 * rows * LEN * 128
    return pl.pallas_call(
        functools.partial(attention_kernel, j, rel),
        grid_spec=grid_spec,
        out_shape=[
            jax.ShapeDtypeStruct(qbuf, bf16),
            jax.ShapeDtypeStruct(qbuf, bf16),
            jax.ShapeDtypeStruct(obuf, bf16),
            jax.ShapeDtypeStruct((rows, 384), bf16),
            jax.ShapeDtypeStruct((rows, 128), bf16),
            jax.ShapeDtypeStruct((1, 384), f32),
        ],
        cost_estimate=cost(flops, 4 * rows * width + 2 * rows * 512),
        name=f"attention_{j}{rel}",
        compiler_params=pltpu.CompilerParams(vmem_limit_bytes=26 << 20),
    )(meta, first, grad, *[qkv_own] * 3, *[qkv_far] * 3, out_w, small, trig)


def output_kernel(meta, tok_ref, grad_ref, act_ref, hg_ref, *refs):
    at_refs, qg_refs, refs = refs[0:4], refs[4:8], refs[8:]
    oo_ref, ox_ref, po_ref, px_ref, fo_ref, fx_ref, wo_ref, wx_ref, small_ref = refs[:9]
    qb_refs, fb_ref, refs = refs[9:13], refs[13], refs[14:]
    lay_ref, tg_ref, own_ref, send_ref, wgo_ref, wgx_ref, sg_ref, fg_ref, tot_ref, qb_ref = refs
    i = pl.program_id(0)
    c = meta[0]
    tile, width = tok_ref.shape
    half = width // 2
    own_lanes = pl.ds(pl.multiple_of(c * half, half), half)
    far_lanes = pl.ds(pl.multiple_of((1 - c) * half, half), half)

    @pl.when(i == 0)
    def _():
        for w_ref, g_ref in ((wo_ref, wgo_ref), (wx_ref, wgx_ref)):
            for j in range(2):
                for rel in range(2):
                    for p in range(3):
                        src = pl.ds(pl.multiple_of((p * 4 + (rel ^ c) * 2 + j) * 128, 128), 128)
                        dst = (j * 6 + rel * 3 + p) * 128
                        g_ref[:, dst : dst + 128] = w_ref[:, src]
        tot_ref[...] = jnp.zeros_like(tot_ref)

    x = tok_ref[...].astype(f32)
    grad = grad_ref[...].astype(f32)
    normed, inv_dev = normalise(x)
    acc = dot_nn(jnp.concatenate([at_refs[0][...], at_refs[2][...]], 1), oo_ref[...])
    acc += dot_nn(jnp.concatenate([at_refs[1][...], at_refs[3][...]], 1), ox_ref[...])
    for j in range(2):
        for rel, p_ref in enumerate((po_ref, px_ref)):
            k = 512 * (2 * j + rel)
            acc += dot_nn(act_ref[:, k : k + 512], p_ref[512 * j : 512 * (j + 1), :])
    lay_ref[...] = (x + acc + (vec_row(small_ref, 4) + vec_row(small_ref, 5))).astype(bf16)

    for f_ref, wg_ref, lanes in ((fo_ref, wgo_ref, own_lanes), (fx_ref, wgx_ref, far_lanes)):
        total = None
        for j in range(2):
            for rel in range(2):
                k = 512 * (2 * j + rel)
                cols = pl.ds(pl.multiple_of((rel ^ c) * 1024 + 512 * j, 512), 512)
                term = dot_nt(hg_ref[:, k : k + 512], f_ref[:, cols])
                total = term if total is None else total + term
        sg_ref[:, lanes] = total
        qg = [jnp.concatenate([qg_refs[2 * j][...], qg_refs[2 * j + 1][...]], 1) for j in range(2)]
        fg_ref[:, lanes] = dot_nt(qg[0], wg_ref[:, :768]) + dot_nt(qg[1], wg_ref[:, 768:])
    second_g = sg_ref[...]
    first_g = fg_ref[...]
    e = first_g * vec_row(small_ref, 0) + second_g * vec_row(small_ref, 2)
    ln = inv_dev * (
        e - jnp.mean(e, -1, keepdims=True) - normed * jnp.mean(e * normed, -1, keepdims=True)
    )
    tg_ref[...] = (grad + ln).astype(bf16)
    for k, term in enumerate((first_g * normed, first_g, second_g * normed, second_g, grad)):
        tot_ref[k] += jnp.sum(term.reshape(tile // 8, 8, width), 0)

    @pl.when(i == pl.num_programs(0) - 1)
    def _():
        for j in range(2):
            for rel in range(2):
                for p in range(3):
                    qb_ref[p * 4 + (rel ^ c) * 2 + j] = qb_refs[2 * j + rel][:, 128 * p : 128 * (p + 1)]
        sums = [jnp.sum(tot_ref[k], 0, keepdims=True) for k in range(5)]
        sums.append(sums[4])
        for ref, rel in ((own_ref, 0), (send_ref, 1)):
            owner = rel ^ c
            for k in range(6):
                for part in range(2):
                    low = sums[k][:, 128 * part : 128 * (part + 1)]
                    high = sums[k][:, 256 + 128 * part : 256 + 128 * (part + 1)]
                    ref[2 * k + part] = jnp.where(owner == 0, low, high)
            for k in range(6):
                ref[12 + k] = qb_ref[owner * 6 + k]
            for j in range(2):
                for k in range(4):
                    ref[18 + 4 * j + k] = fb_ref[2 * j + rel][:, 128 * k : 128 * (k + 1)]
            for k in range(SMALL_ROWS, 32):
                ref[k] = jnp.zeros((1, 128), f32)


def output_call(meta, tokens, grad, act, hg, atts, qgs, out_w, proj_w, fc_w, qkv_w, small, qbs, fb):
    rows, width = tokens.shape
    tile = 256
    blk = lambda n: pl.BlockSpec((tile, n), lambda i, m: (i, 0))
    weights = [*out_w, *proj_w, *fc_w, *qkv_w]
    tail = [small, *qbs, fb]
    packed = (32, 1, 128)
    grid_spec = pltpu.PrefetchScalarGridSpec(
        num_scalar_prefetch=1,
        grid=(rows // tile,),
        in_specs=[
            blk(width),
            blk(width),
            *[blk(a.shape[1]) for a in (act, hg, *atts, *qgs)],
            *[full_spec(w.shape) for w in weights],
            *[full_spec(w.shape) for w in tail],
        ],
        out_specs=[blk(width), blk(width), full_spec(packed), full_spec(packed)],
        scratch_shapes=[
            pltpu.VMEM(qkv_w[0].shape, bf16),
            pltpu.VMEM(qkv_w[0].shape, bf16),
            pltpu.VMEM((tile, width), f32),
            pltpu.VMEM((tile, width), f32),
            pltpu.VMEM((5, 8, width), f32),
            pltpu.VMEM((12, 1, 128), f32),
        ],
    )
    return pl.pallas_call(
        output_kernel,
        grid_spec=grid_spec,
        out_shape=[
            jax.ShapeDtypeStruct((rows, width), bf16),
            jax.ShapeDtypeStruct((rows, width), bf16),
            jax.ShapeDtypeStruct(packed, f32),
            jax.ShapeDtypeStruct(packed, f32),
        ],
        cost_estimate=cost(2 * rows * width * (512 + 2048 * 2 + 1536), 2 * rows * (4 * 512 + 4 * 2048)),
        name="outputs",
        compiler_params=pltpu.CompilerParams(vmem_limit_bytes=44 << 20),
    )(meta, tokens, grad, act, hg, *atts, *qgs, *weights, *tail)


def sum_kernel(n_in, *refs):
    ins, outs = refs[:n_in], refs[n_in:]
    for k, out in enumerate(outs):
        rows = out.shape[0]
        for i in range(rows):
            total = ins[0][k * rows + i].astype(f32)
            for term in ins[1:]:
                total += term[k * rows + i].astype(f32)
            out[i] = total.astype(out.dtype)


def sum_call(terms, count, name):
    shape, dtype = terms[0].shape, terms[0].dtype
    moved = len(terms) * terms[0].size * terms[0].dtype.itemsize
    return pl.pallas_call(
        functools.partial(sum_kernel, len(terms)),
        out_shape=[jax.ShapeDtypeStruct((shape[0] // count, *shape[1:]), dtype)] * count,
        compiler_params=pltpu.CompilerParams(vmem_limit_bytes=(moved * 3) // 2 + (4 << 20)),
        cost_estimate=cost(moved, 2 * moved),
        name=name,
    )(*terms)


def pair_kernel(*refs):
    own, got, outs = refs[:6], refs[6:12], refs[12:]
    col = 0
    for mine, other in zip(own, got):
        w = mine.shape[2]
        for k, out in enumerate(outs):
            for i in range(2):
                total = mine[2 * k + i].astype(f32) + other[2 * k + i].astype(f32)
                out[i, :, col : col + w] = total.astype(bf16)
        col += w


def pair_call(own, got, name):
    rows = own[0].shape[1]
    width = sum(a.shape[2] for a in own)
    return pl.pallas_call(
        pair_kernel,
        out_shape=[jax.ShapeDtypeStruct((2, rows, width), bf16)] * 2,
        compiler_params=pltpu.CompilerParams(vmem_limit_bytes=12 << 20),
        cost_estimate=cost(8 * rows * width, 24 * rows * width),
        name=name,
    )(*own, *got)


def exchange(a, reps, far, near):
    pairs = [(2 * i + c, 2 * (i ^ (near if c else far)) + c) for i in range(reps) for c in range(2)]
    return lax.ppermute(a, ("rep", "opt"), pairs)


def swap(a):
    return lax.ppermute(a, "opt", [(0, 1), (1, 0)])


def tie(value, *others):
    return lax.optimization_barrier((value, *others))[0]


def rest_bits(reps):
    return [1 << b for b in range(2, reps.bit_length() - 1)]


def spread(total, reps):
    return [total, exchange(total, reps, 2, 1), exchange(total, reps, 1, 2), exchange(total, reps, 3, 3)]


def adamw(grad, mean, square, weight):
    new_mean = BETA_ONE * mean + (1.0 - BETA_ONE) * grad
    new_square = BETA_TWO * square + (1.0 - BETA_TWO) * grad * grad
    step = -LEARN_RATE * (
        new_mean * (1.0 / FIX_ONE) / (jnp.sqrt(new_square * (1.0 / FIX_TWO)) + ADAM_EPS)
        + WEIGHT_DECAY * weight.astype(f32)
    )
    return step, new_mean, new_square


def pick(refs, which, cols, rows=slice(None)):
    out = refs[0][0, rows, cols]
    for k in range(1, len(refs)):
        out = jnp.where(which == k, refs[k][0, rows, cols], out)
    return out.astype(f32)


def adam_block(grad, m_ref, s_ref, w_ref, g_out, st_out, m_out, s_out, at):
    step, mean, square = adamw(grad, m_ref[at], s_ref[at], w_ref[at])
    g_out[at] = grad
    st_out[at] = step
    m_out[at] = mean
    s_out[at] = square


def adam_ff_kernel(meta, *refs):
    pieces, proj, fc, proj_out, fc_out = refs[:4], refs[4:7], refs[7:10], refs[10:14], refs[14:18]
    which = pl.program_id(0) ^ meta[1]
    quarter = fc[0].shape[0]
    for j in range(2):
        for k in range(2):
            at = (j, slice(k * quarter, (k + 1) * quarter), slice(None))
            col = 1024 * j + 512 * k
            adam_block(pick(pieces, which, slice(col, col + 512)), *proj, *proj_out, at)
            at = (slice(None), slice(col, col + 512))
            adam_block(pick(pieces, which, slice(2048 + col, 2048 + col + 512)), *fc, *fc_out, at)


def adam_qkv_kernel(meta, *refs):
    pieces, qkv, out, qkv_out, out_out = refs[:4], refs[4:7], refs[7:10], refs[10:14], refs[14:18]
    c = meta[0]
    which = pl.program_id(0) ^ meta[1]
    quarter = qkv[0].shape[0]
    hq = quarter // 2
    for j in range(2):
        for slot in range(2):
            for p in range(3):
                col = 384 * (2 * j + slot) + 128 * p
                grad = pick(pieces, which, slice(col, col + 128))
                lanes = pl.ds(pl.multiple_of((p * 4 + (slot ^ c) * 2 + j) * 128, 128), 128)
                adam_block(grad, *qkv, *qkv_out, (slice(None), lanes))
        for k in range(2):
            col = 1536 + 256 * j
            grad = pick(pieces, which, slice(col, col + 256), slice(k * hq, (k + 1) * hq))
            adam_block(grad, *out, *out_out, (j, slice(None), slice(256 * k, 256 * k + 256)))


def adam_call(kernel, meta, pieces, first, second, first_spec, second_spec, name):
    outs = [jax.ShapeDtypeStruct(first[0].shape, f32)] * 4 + [jax.ShapeDtypeStruct(second[0].shape, f32)] * 4
    grid_spec = pltpu.PrefetchScalarGridSpec(
        num_scalar_prefetch=1,
        grid=(4,),
        in_specs=[*[full_spec(a.shape) for a in pieces], *[first_spec] * 3, *[second_spec] * 3],
        out_specs=[*[first_spec] * 4, *[second_spec] * 4],
    )
    size = first[0].size + second[0].size
    return pl.pallas_call(
        kernel,
        grid_spec=grid_spec,
        out_shape=outs,
        compiler_params=pltpu.CompilerParams(vmem_limit_bytes=32 << 20),
        cost_estimate=cost(20 * size, 28 * size),
        name=name,
    )(meta, *pieces, *first, *second)


def body(
    tokens,
    out_grad,
    vectors,
    qkv_weight,
    qkv_bias,
    out_weight,
    fc_weight,
    fc_bias,
    proj_weight,
    mean_vectors,
    mean_qkv_weight,
    mean_qkv_bias,
    mean_out_weight,
    mean_fc_weight,
    mean_fc_bias,
    mean_proj_weight,
    square_vectors,
    square_qkv_weight,
    square_qkv_bias,
    square_out_weight,
    square_fc_weight,
    square_fc_bias,
    square_proj_weight,
):
    reps = lax.axis_size("rep")
    c = lax.axis_index("opt")
    place = lax.axis_index("rep")
    low, high = place & 1, (place >> 1) & 1
    ranks = jnp.stack([2 * low + high, 2 * high + low])
    meta = jnp.stack([c, ranks[c], ranks[1 - c]]).astype(jnp.int32)
    trig = jnp.asarray(trig_tables())

    packed = jnp.concatenate(
        [vectors.reshape(12, 128), qkv_bias.reshape(6, 128), fc_bias.reshape(8, 128)], 0
    )
    small = lax.all_gather(packed, "opt", axis=0, tiled=True).astype(f32).reshape(2 * SMALL_ROWS, 1, 128)
    fc_far = swap(fc_weight)
    proj_far = swap(proj_weight)
    qkv_far = swap(qkv_weight)
    out_far = swap(out_weight)

    first, second = norm_call(tokens, small)
    own, send, act, hg, fb = ff_call(meta, second, out_grad, fc_weight, fc_far, proj_weight, proj_far, small)

    ff_got = swap(send)
    att = {}
    last = own
    order = [(0, 1), (0, 0), (1, 1), (1, 0)]

    def attend(k, *wait):
        j, rel = order[k]
        out_w = out_far if rel else out_weight
        att[j, rel] = attention_call(
            j, rel, tie(meta, *wait), first, out_grad, qkv_weight, qkv_far, out_w, small, trig
        )
        return att[j, rel][5]

    mark = attend(0, own)
    keep, send = sum_call([tie(own, mark), ff_got], 2, "ff_pair")
    got = exchange(send, reps, 1, 2)
    mark = attend(1, keep)
    keep, send = sum_call([tie(keep, mark), got], 2, "ff_sum0")
    got = exchange(send, reps, 2, 1)
    mark = attend(2, keep)
    (ff_total,) = sum_call([tie(keep, mark), got], 1, "ff_sum1")
    bits = rest_bits(reps)
    got = exchange(ff_total, reps, bits[0], bits[0])
    mark = attend(3, ff_total)

    keys = [(0, 0), (0, 1), (1, 0), (1, 1)]
    q_own = [att[k][0] for k in keys]
    q_got = [swap(att[j, 1 - rel][1]) for j, rel in keys]
    o_own = [att[j, 0][2] for j in range(2)]
    o_got = [swap(att[j, 1][2]) for j in range(2)]
    (ff_total,) = sum_call([tie(ff_total, mark), got], 1, "ff_sum2")
    keep, send = pair_call([*q_own, *o_own], [*q_got, *o_got], "att_pair")
    att_got = exchange(send, reps, 1, 2)
    for bit in bits[1:]:
        got = exchange(ff_total, reps, bit, bit)
        (ff_total,) = sum_call([ff_total, got], 1, "ff_sum3")
    ff_pieces = spread(ff_total, reps)

    layer_out, tokens_grad, small_own, small_send = output_call(
        tie(meta, keep),
        tokens,
        out_grad,
        act,
        hg,
        [att[k][4] for k in keys],
        [att[k][3] for k in keys],
        (out_weight, out_far),
        (proj_weight, proj_far),
        (fc_weight, fc_far),
        (qkv_weight, qkv_far),
        small,
        [att[k][5] for k in keys],
        fb,
    )
    keep, send = sum_call([keep, att_got], 2, "att_sum0")
    got = exchange(send, reps, 2, 1)
    (att_total,) = sum_call([keep, got], 1, "att_sum1")
    for bit in bits:
        got = exchange(att_total, reps, bit, bit)
        (att_total,) = sum_call([att_total, got], 1, "att_sum2")
    att_pieces = spread(att_total, reps)

    (total,) = sum_call([small_own, swap(small_send)], 1, "small_pair")
    for bit in (1, 2, *bits):
        (total,) = sum_call([total, exchange(total, reps, bit, bit)], 1, "small_sum")
    flat = total.reshape(32, 128)
    g_vec = flat[:12].reshape(6, 256)
    g_qb = flat[12:18].reshape(768)
    g_fb = flat[18:26].reshape(1024)

    view = lambda a: a.reshape(2, 512, 512)
    proj_adam = adam_call(
        adam_ff_kernel,
        meta,
        ff_pieces,
        [view(a) for a in (mean_proj_weight, square_proj_weight, proj_weight)],
        [mean_fc_weight, square_fc_weight, fc_weight],
        pl.BlockSpec((2, 128, 512), lambda q, m: (0, q, 0)),
        pl.BlockSpec((64, 2048), lambda q, m: (q, 0)),
        "adam_ff",
    )
    a_proj = [a.reshape(1024, 512) for a in proj_adam[:4]]
    a_fc = proj_adam[4:]
    view_o = lambda a: a.reshape(2, 128, 512)
    qkv_adam = adam_call(
        adam_qkv_kernel,
        meta,
        att_pieces,
        [mean_qkv_weight, square_qkv_weight, qkv_weight],
        [view_o(a) for a in (mean_out_weight, square_out_weight, out_weight)],
        pl.BlockSpec((64, 1536), lambda q, m: (q, 0)),
        pl.BlockSpec((2, 32, 512), lambda q, m: (0, q, 0)),
        "adam_qkv",
    )
    a_qkv = qkv_adam[:4]
    a_out = [a.reshape(256, 512) for a in qkv_adam[4:]]
    a_vec = (g_vec, *adamw(g_vec, mean_vectors, square_vectors, vectors))
    a_qb = (g_qb, *adamw(g_qb, mean_qkv_bias, square_qkv_bias, qkv_bias))
    a_fb = (g_fb, *adamw(g_fb, mean_fc_bias, square_fc_bias, fc_bias))
    order = (a_vec, a_qkv, a_qb, a_out, a_fc, a_fb, a_proj)
    return (layer_out, tokens_grad, *[a[k] for k in range(4) for a in order])


def solution(mesh):
    rows = P(("rep", "opt"), None)
    weights = (P(None, "opt"), P("opt", None), P("opt"), P("opt", None), P("opt", None), P("opt"), P("opt", None))
    in_specs = (rows, rows, *weights, *weights, *weights)
    out_specs = (rows, rows, *weights, *weights, *weights, *weights)
    return jax.shard_map(body, mesh=mesh, in_specs=in_specs, out_specs=out_specs, check_vma=False)
```

```python
import functools

import jax
import jax.numpy as jnp
import numpy as np
from jax import lax
from jax.experimental import pallas as pl
from jax.experimental.pallas import tpu as pltpu
from jax.sharding import PartitionSpec as P

H = 8
ROT = 16
LEN = 512
ADAM_STEP = 10

LN_EPS = 1e-05
ADAM_EPS = 1e-08
BETA_ONE = 0.9
BETA_TWO = 0.95
LEARN_RATE = 0.02
WEIGHT_DECAY = 0.01
FIX_ONE = 1.0 - BETA_ONE**ADAM_STEP
FIX_TWO = 1.0 - BETA_TWO**ADAM_STEP
INV_ROOT_TWO = 0.7071067811865476
INV_ROOT_TWO_PI = 0.3989422804014327

bf16 = jnp.bfloat16
f32 = jnp.float32
PARTS = 2
SMALL_ROWS = 26


def dot_nn(a, b):
    return lax.dot_general(a, b, (((1,), (0,)), ((), ())), preferred_element_type=f32)


def dot_nt(a, b):
    return lax.dot_general(a, b, (((1,), (1,)), ((), ())), preferred_element_type=f32)


def dot_tn(a, b):
    return lax.dot_general(a, b, (((0,), (0,)), ((), ())), preferred_element_type=f32)


def full_spec(shape):
    zeros = (0,) * len(shape)
    return pl.BlockSpec(shape, lambda *_: zeros)


def cost(flops, moved, transcendentals=0):
    return pl.CostEstimate(
        flops=int(flops), bytes_accessed=int(moved), transcendentals=int(transcendentals)
    )


def vec_row(small_ref, i):
    n = SMALL_ROWS
    rows = [small_ref[o * n + 2 * i + k] for o in range(2) for k in range(2)]
    return jnp.concatenate(rows, 1)


def normalise(x):
    centre = x - jnp.mean(x, -1, keepdims=True)
    inv_dev = lax.rsqrt(jnp.mean(centre * centre, -1, keepdims=True) + LN_EPS)
    return centre * inv_dev, inv_dev


def norm_kernel(tok_ref, small_ref, first_ref, second_ref):
    normed, _ = normalise(tok_ref[...].astype(f32))
    first_ref[...] = (normed * vec_row(small_ref, 0) + vec_row(small_ref, 1)).astype(bf16)
    second_ref[...] = (normed * vec_row(small_ref, 2) + vec_row(small_ref, 3)).astype(bf16)


def norm_call(tokens, small):
    rows, width = tokens.shape
    tile = 512
    spec = pl.BlockSpec((tile, width), lambda i: (i, 0))
    out = jax.ShapeDtypeStruct((rows, width), bf16)
    return pl.pallas_call(
        norm_kernel,
        grid=(rows // tile,),
        in_specs=[spec, full_spec(small.shape)],
        out_specs=[spec, spec],
        out_shape=[out, out],
        cost_estimate=cost(20 * rows * width, 6 * rows * width),
        name="norm",
        compiler_params=pltpu.CompilerParams(vmem_limit_bytes=12 << 20),
    )(tokens, small)


def ff_kernel(meta, second_ref, grad_ref, fco_ref, fcx_ref, pro_ref, prx_ref, small_ref,
              send_ref, act_ref, hg_ref, bias_ref, fc_ref):
    j = pl.program_id(0)
    rel = pl.program_id(1)
    c = meta[0]
    far_rank = meta[2]
    o = rel ^ c
    rows, width = second_ref.shape
    half = width // 2
    cols = act_ref.shape[1]
    quarter = half // 4
    proj = jnp.where(rel == 0, pro_ref[...], prx_ref[...])
    own_lanes = pl.ds(pl.multiple_of(c * half, half), half)
    far_lanes = pl.ds(pl.multiple_of((1 - c) * half, half), half)
    fc_ref[own_lanes, :] = fco_ref[...]
    fc_ref[far_lanes, :] = fcx_ref[...]
    fc = fc_ref[...]
    base = o * SMALL_ROWS + 18 + 4 * j
    bias = jnp.concatenate([small_ref[base + k] for k in range(cols // 128)], 1)
    tile = 256

    def block(i, total):
        r = pl.ds(pl.multiple_of(i * tile, tile), tile)
        hidden = dot_nn(second_ref[r, :], fc) + bias
        act_grad = dot_nt(grad_ref[r, :], proj)
        phi_cap = 0.5 + 0.5 * lax.erf(hidden * INV_ROOT_TWO)
        slope = phi_cap + hidden * (jnp.exp(-0.5 * hidden * hidden) * INV_ROOT_TWO_PI)
        act_ref[r, :] = (hidden * phi_cap).astype(bf16)
        hg = (act_grad * slope).astype(bf16)
        hg_ref[r, :] = hg
        return total + jnp.sum(hg.astype(f32).reshape(tile // 8, 8, cols), 0)

    total = lax.fori_loop(0, rows // tile, block, jnp.zeros((8, cols), f32))
    bias_ref[...] = jnp.sum(total, 0, keepdims=True)[None]
    pl.when(rel == 1)(lambda: put_proj(send_ref, dot_tn(act_ref[...], grad_ref[...]), j, far_rank))
    put_fc(send_ref, dot_tn(second_ref[:, far_lanes], hg_ref[...]), o, j, far_rank)


def put_proj(ref, grad, j, rank):
    quarter = ref.shape[1]
    lanes = pl.ds(pl.multiple_of(j * 1024, 1024), 1024)
    for a in range(4):
        piece = grad[a * 2 * quarter : (a + 1) * 2 * quarter]
        ref[a ^ rank, :, lanes] = jnp.concatenate([piece[:quarter], piece[quarter:]], 1).astype(bf16)


def put_fc(ref, grad, o, j, rank):
    quarter = ref.shape[1]
    cols = grad.shape[1]
    lanes = pl.ds(pl.multiple_of(2048 + o * 1024 + j * cols, cols), cols)
    for a in range(4):
        ref[a ^ rank, :, lanes] = grad[a * quarter : (a + 1) * quarter].astype(bf16)


def ff_own_kernel(meta, second_ref, grad_ref, act_ref, hg_ref, own_ref):
    j = pl.program_id(0)
    rel = pl.program_id(1)
    c = meta[0]
    rank = meta[1]
    half = second_ref.shape[1] // 2
    own_lanes = pl.ds(pl.multiple_of(c * half, half), half)
    pl.when(rel == 0)(lambda: put_proj(own_ref, dot_tn(act_ref[...], grad_ref[...]), j, rank))
    put_fc(own_ref, dot_tn(second_ref[:, own_lanes], hg_ref[...]), rel ^ c, j, rank)


def ff_call(meta, second, grad, fc_own, fc_far, proj_own, proj_far, small):
    rows, width = second.shape
    ff = fc_own.shape[1]
    half = width // 2
    cols = ff // 4
    buf = (4, half // 4, 2 * ff)
    fc_spec = pl.BlockSpec((half, cols), lambda j, r, m: (0, (r ^ m[0]) * 2 + j))
    proj_spec = pl.BlockSpec((cols, width), lambda j, r, m: (j, 0))
    act_spec = pl.BlockSpec((rows, cols), lambda j, r, m: (0, 2 * j + r))
    grid_spec = pltpu.PrefetchScalarGridSpec(
        num_scalar_prefetch=1,
        grid=(2, 2),
        in_specs=[
            full_spec((rows, width)),
            full_spec((rows, width)),
            fc_spec,
            fc_spec,
            proj_spec,
            proj_spec,
            full_spec(small.shape),
        ],
        out_specs=[
            full_spec(buf),
            act_spec,
            act_spec,
            pl.BlockSpec((1, 1, cols), lambda j, r, m: (2 * j + r, 0, 0)),
        ],
        scratch_shapes=[pltpu.VMEM((width, cols), bf16)],
    )
    return pl.pallas_call(
        ff_kernel,
        grid_spec=grid_spec,
        out_shape=[
            jax.ShapeDtypeStruct(buf, bf16),
            jax.ShapeDtypeStruct((rows, ff), bf16),
            jax.ShapeDtypeStruct((rows, ff), bf16),
            jax.ShapeDtypeStruct((4, 1, cols), f32),
        ],
        cost_estimate=cost(6 * rows * width * ff, 4 * rows * width + 4 * rows * ff),
        name="feed_forward",
        compiler_params=pltpu.CompilerParams(vmem_limit_bytes=40 << 20),
    )(meta, second, grad, fc_own, fc_far, proj_own, proj_far, small)


def ff_own_call(meta, second, grad, act, hg):
    rows, width = second.shape
    ff = act.shape[1]
    cols = ff // 4
    buf = (4, width // 8, 2 * ff)
    grid_spec = pltpu.PrefetchScalarGridSpec(
        num_scalar_prefetch=1,
        grid=(2, 2),
        in_specs=[
            full_spec((rows, width)),
            full_spec((rows, width)),
            pl.BlockSpec((rows, cols), lambda j, r, m: (0, 2 * j)),
            pl.BlockSpec((rows, cols), lambda j, r, m: (0, 2 * j + r)),
        ],
        out_specs=full_spec(buf),
    )
    return pl.pallas_call(
        ff_own_kernel,
        grid_spec=grid_spec,
        out_shape=jax.ShapeDtypeStruct(buf, bf16),
        cost_estimate=cost(2 * rows * width * ff, 4 * rows * width + 3 * rows * ff),
        name="feed_forward_own",
        compiler_params=pltpu.CompilerParams(vmem_limit_bytes=30 << 20),
    )(meta, second, grad, act, hg)


def rotate_rows(x, cosine, sine):
    parts = []
    for h in range(2):
        low, high = x[64 * h : 64 * h + 8], x[64 * h + 8 : 64 * h + 16]
        parts += [low * cosine - high * sine, high * cosine + low * sine, x[64 * h + 16 : 64 * h + 64]]
    return jnp.concatenate(parts, 0)


def attention_kernel(j, rel, meta, first_ref, grad_ref, wq_ref, wk_ref, wv_ref, xq_ref, xk_ref, xv_ref,
                     ow_ref, small_ref, trig_ref, *refs):
    if rel == 0:
        own_first_ref, send_first_ref, refs = refs[0], refs[1], refs[2:]
    own_ref, send_ref, qg_ref, att_ref, bias_ref, wt_ref, bcol_ref, qgs_ref, attt_ref, btot_ref = refs
    s = pl.program_id(0)
    c = meta[0]
    rank, far_rank = meta[1], meta[2]
    o = rel ^ c
    rows, width = first_ref.shape
    half = width // 2
    quarter = half // 4
    own_lanes = pl.ds(pl.multiple_of(c * half, half), half)
    far_lanes = pl.ds(pl.multiple_of((1 - c) * half, half), half)

    @pl.when(s == 0)
    def _():
        for p, (own, far) in enumerate(((wq_ref, xq_ref), (wk_ref, xk_ref), (wv_ref, xv_ref))):
            wt_ref[128 * p : 128 * (p + 1), own_lanes] = own[...].T
            wt_ref[128 * p : 128 * (p + 1), far_lanes] = far[...].T
            row = p * 4 + o * 2 + j
            owner = row // 6
            bias = small_ref[owner * SMALL_ROWS + 12 + row - 6 * owner]
            bcol_ref[128 * p : 128 * (p + 1), :] = jnp.broadcast_to(bias, (128, 128)).T
        btot_ref[...] = jnp.zeros_like(btot_ref)

    seq = pl.ds(pl.multiple_of(s * LEN, LEN), LEN)
    first = first_ref[seq, :]
    grad = grad_ref[seq, :]
    mixed = dot_nt(wt_ref[...], first) + bcol_ref[:, :1]
    da_t = dot_nt(ow_ref[...], grad).astype(bf16)
    cosine, sine = trig_ref[0], trig_ref[1]
    q_t = rotate_rows(mixed[:128], cosine, sine).astype(bf16) * jnp.asarray(0.125, bf16)
    k_t = rotate_rows(mixed[128:256], cosine, sine).astype(bf16)
    v_t = mixed[256:].astype(bf16)
    k_tok = k_t.T
    v_tok = v_t.T
    hl = LEN // 2
    row_id = lax.broadcasted_iota(jnp.int32, (hl, hl), 0)
    col_id = lax.broadcasted_iota(jnp.int32, (hl, hl), 1)
    keep = row_id <= col_id
    zeros = jnp.zeros((64, LEN), bf16)
    att, dq, dk, dv = [], [], [], []
    for h in range(2):
        hs = slice(64 * h, 64 * h + 64)
        qh, kh, vh, dah = q_t[hs], k_t[hs], v_t[hs], da_t[hs]
        pad = (lambda u: jnp.concatenate([u, zeros], 0)) if h == 0 else (lambda u: jnp.concatenate([zeros, u], 0))
        qz, daz = pad(qh), pad(dah)
        att_h, dq_h = [], []
        dk_h = dv_h = None
        for t in range(2):
            ts = slice(hl * t, hl * t + hl)
            n = hl * (t + 1)
            score = dot_nn(k_tok[:n], qz[:, ts])
            diag = jnp.where(keep, score[n - hl :], -1e30)
            score = diag if t == 0 else jnp.concatenate([score[:hl], diag], 0)
            exps = jnp.exp(score - jnp.max(score, 0, keepdims=True))
            prob = exps * (1.0 / jnp.sum(exps, 0, keepdims=True))
            prob_b = prob.astype(bf16)
            att_h.append(dot_nn(vh[:, :n], prob_b))
            pg = dot_nn(v_tok[:n], daz[:, ts])
            sg = (prob * (pg - jnp.sum(pg * prob, 0, keepdims=True))).astype(bf16)
            dq_h.append(dot_nn(kh[:, :n], sg))
            dv_t = dot_nt(dah[:, ts], prob_b)
            dk_t = dot_nt(qh[:, ts], sg)
            if t == 0:
                dv_h, dk_h = dv_t, dk_t
            else:
                dv_h = jnp.concatenate([dv_h + dv_t[:, :hl], dv_t[:, hl:]], 1)
                dk_h = jnp.concatenate([dk_h + dk_t[:, :hl], dk_t[:, hl:]], 1)
        att.append(jnp.concatenate(att_h, 1))
        dq.append(jnp.concatenate(dq_h, 1) * 0.125)
        dk.append(dk_h)
        dv.append(dv_h)
    att_t = jnp.concatenate(att, 0).astype(bf16)
    dq_t = rotate_rows(jnp.concatenate(dq, 0), cosine, -sine)
    dk_t = rotate_rows(jnp.concatenate(dk, 0), cosine, -sine)
    qkv_t = jnp.concatenate([dq_t, dk_t, jnp.concatenate(dv, 0)], 0).astype(bf16)
    qkv_g = qkv_t.T
    qg_ref[...] = qkv_g
    qgs_ref[seq, :] = qkv_g
    att_ref[...] = att_t.T
    attt_ref[:, seq] = att_t
    btot_ref[...] += jnp.sum(qkv_g.astype(f32).reshape(LEN // 8, 8, 384), 0)

    @pl.when(s == pl.num_programs(0) - 1)
    def _():
        bias_ref[...] = jnp.sum(btot_ref[...], 0, keepdims=True)
        at_own, at_send = (0, 384) if rel == 0 else (0, 0)
        if rel == 0:
            own_ref[:, :, 384:768] = own_first_ref[...]
            send_ref[:, :, :384] = send_first_ref[:, :, :384]
            send_ref[:, :, 768:] = send_first_ref[:, :, 384:]
        for ref, side, number, at in ((own_ref, own_lanes, rank, at_own), (send_ref, far_lanes, far_rank, at_send)):
            gw = dot_tn(first_ref[:, side], qgs_ref[...])
            for a in range(4):
                ref[a ^ number, :, at : at + 384] = gw[a * quarter : (a + 1) * quarter].astype(bf16)
        go = dot_nn(attt_ref[...], grad_ref[...])
        hq = quarter // 2
        for a in range(4):
            piece = go[a * hq : (a + 1) * hq]
            piece = jnp.concatenate([piece[:, :256], piece[:, 256:]], 0).astype(bf16)
            if rel == 0:
                own_ref[a ^ rank, :, 768:] = piece
            else:
                send_ref[a ^ far_rank, :, 384:] = piece


def trig_tables():
    freqs = np.power(np.float32(10000.0), -np.arange(0, ROT, 2).astype(np.float32) / np.float32(ROT))
    angles = (np.arange(LEN).astype(np.float32)[None, :] * freqs[:, None]).astype(np.float32)
    return np.stack([np.cos(angles), np.sin(angles)]).astype(np.float32)


def attention_call(j, rel, meta, first, grad, qkv_own, qkv_far, out_w, small, trig, before=()):
    rows, width = first.shape
    half = width // 2
    bufs = [(4, half // 4, w) for w in ((1024, 1024) if rel == 0 else (384, 640))]
    w_specs = [
        pl.BlockSpec((half, 128), functools.partial(lambda p, s, m: (0, p * 4 + (rel ^ m[0]) * 2 + j), p))
        for p in range(3)
    ]
    grid_spec = pltpu.PrefetchScalarGridSpec(
        num_scalar_prefetch=1,
        grid=(rows // LEN,),
        in_specs=[
            full_spec((rows, width)),
            full_spec((rows, width)),
            *w_specs,
            *w_specs,
            pl.BlockSpec((128, width), lambda s, m: (j, 0)),
            full_spec(small.shape),
            full_spec(trig.shape),
            *[full_spec(a.shape) for a in before],
        ],
        out_specs=[
            *[full_spec(b) for b in bufs],
            pl.BlockSpec((LEN, 384), lambda s, m: (s, 0)),
            pl.BlockSpec((LEN, 128), lambda s, m: (s, 0)),
            full_spec((1, 384)),
        ],
        scratch_shapes=[
            pltpu.VMEM((384, width), bf16),
            pltpu.VMEM((384, 128), f32),
            pltpu.VMEM((rows, 384), bf16),
            pltpu.VMEM((128, rows), bf16),
            pltpu.VMEM((8, 384), f32),
        ],
    )
    flops = 2 * rows * width * (2 * 384 + 2 * 128) + 2 * 6 * 2 * rows * LEN * 128
    return pl.pallas_call(
        functools.partial(attention_kernel, j, rel),
        grid_spec=grid_spec,
        out_shape=[
            *[jax.ShapeDtypeStruct(b, bf16) for b in bufs],
            jax.ShapeDtypeStruct((rows, 384), bf16),
            jax.ShapeDtypeStruct((rows, 128), bf16),
            jax.ShapeDtypeStruct((1, 384), f32),
        ],
        cost_estimate=cost(flops, 4 * rows * width + 2 * rows * 512),
        name=f"attention_{j}{rel}",
        compiler_params=pltpu.CompilerParams(vmem_limit_bytes=26 << 20),
    )(meta, first, grad, *[qkv_own] * 3, *[qkv_far] * 3, out_w, small, trig, *before)


def output_kernel(part, parts, meta, tok_ref, grad_ref, act_ref, hg_ref, *refs):
    at_refs, qg_refs, refs = refs[0:4], refs[4:8], refs[8:]
    oo_ref, ox_ref, po_ref, px_ref, fo_ref, fx_ref, wo_ref, wx_ref, small_ref = refs[:9]
    qb_refs, fb_ref, refs = refs[9:13], refs[13], refs[14:]
    if part > 0:
        before_ref, refs = refs[0], refs[3:]
    lay_ref, tg_ref, refs = refs[0], refs[1], refs[2:]
    if part < parts - 1:
        tot_ref, wgo_ref, wgx_ref, sg_ref, fg_ref = refs
    else:
        own_ref, send_ref, wgo_ref, wgx_ref, sg_ref, fg_ref, tot_ref, qb_ref = refs
    i = pl.program_id(0)
    c = meta[0]
    tile, width = tok_ref.shape
    half = width // 2
    own_lanes = pl.ds(pl.multiple_of(c * half, half), half)
    far_lanes = pl.ds(pl.multiple_of((1 - c) * half, half), half)

    @pl.when(i == 0)
    def _():
        for w_ref, g_ref in ((wo_ref, wgo_ref), (wx_ref, wgx_ref)):
            for j in range(2):
                for rel in range(2):
                    for p in range(3):
                        src = pl.ds(pl.multiple_of((p * 4 + (rel ^ c) * 2 + j) * 128, 128), 128)
                        dst = (j * 6 + rel * 3 + p) * 128
                        g_ref[:, dst : dst + 128] = w_ref[:, src]
        tot_ref[...] = jnp.zeros_like(tot_ref) if part == 0 else before_ref[...]

    x = tok_ref[...].astype(f32)
    grad = grad_ref[...].astype(f32)
    normed, inv_dev = normalise(x)
    acc = dot_nn(jnp.concatenate([at_refs[0][...], at_refs[2][...]], 1), oo_ref[...])
    acc += dot_nn(jnp.concatenate([at_refs[1][...], at_refs[3][...]], 1), ox_ref[...])
    for j in range(2):
        for rel, p_ref in enumerate((po_ref, px_ref)):
            k = 512 * (2 * j + rel)
            acc += dot_nn(act_ref[:, k : k + 512], p_ref[512 * j : 512 * (j + 1), :])
    lay_ref[...] = (x + acc + (vec_row(small_ref, 4) + vec_row(small_ref, 5))).astype(bf16)

    for f_ref, wg_ref, lanes in ((fo_ref, wgo_ref, own_lanes), (fx_ref, wgx_ref, far_lanes)):
        total = None
        for j in range(2):
            for rel in range(2):
                k = 512 * (2 * j + rel)
                cols = pl.ds(pl.multiple_of((rel ^ c) * 1024 + 512 * j, 512), 512)
                term = dot_nt(hg_ref[:, k : k + 512], f_ref[:, cols])
                total = term if total is None else total + term
        sg_ref[:, lanes] = total
        qg = [jnp.concatenate([qg_refs[2 * j][...], qg_refs[2 * j + 1][...]], 1) for j in range(2)]
        fg_ref[:, lanes] = dot_nt(qg[0], wg_ref[:, :768]) + dot_nt(qg[1], wg_ref[:, 768:])
    second_g = sg_ref[...]
    first_g = fg_ref[...]
    e = first_g * vec_row(small_ref, 0) + second_g * vec_row(small_ref, 2)
    ln = inv_dev * (
        e - jnp.mean(e, -1, keepdims=True) - normed * jnp.mean(e * normed, -1, keepdims=True)
    )
    tg_ref[...] = (grad + ln).astype(bf16)
    for k, term in enumerate((first_g * normed, first_g, second_g * normed, second_g, grad)):
        tot_ref[k] += jnp.sum(term.reshape(tile // 8, 8, width), 0)

    if part < parts - 1:
        return

    @pl.when(i == pl.num_programs(0) - 1)
    def _():
        for j in range(2):
            for rel in range(2):
                for p in range(3):
                    qb_ref[p * 4 + (rel ^ c) * 2 + j] = qb_refs[2 * j + rel][:, 128 * p : 128 * (p + 1)]
        sums = [jnp.sum(tot_ref[k], 0, keepdims=True) for k in range(5)]
        sums.append(sums[4])
        for ref, rel in ((own_ref, 0), (send_ref, 1)):
            owner = rel ^ c
            for k in range(6):
                for part in range(2):
                    low = sums[k][:, 128 * part : 128 * (part + 1)]
                    high = sums[k][:, 256 + 128 * part : 256 + 128 * (part + 1)]
                    ref[2 * k + part] = jnp.where(owner == 0, low, high)
            for k in range(6):
                ref[12 + k] = qb_ref[owner * 6 + k]
            for j in range(2):
                for k in range(4):
                    ref[18 + 4 * j + k] = fb_ref[2 * j + rel][:, 128 * k : 128 * (k + 1)]
            for k in range(SMALL_ROWS, 32):
                ref[k] = jnp.zeros((1, 128), f32)


def output_call(part, parts, meta, tokens, grad, act, hg, atts, qgs, out_w, proj_w, fc_w, qkv_w, small, qbs, fb,
                before=None):
    rows, width = tokens.shape
    tile = 256
    tiles = rows // tile // parts
    blk = lambda n: pl.BlockSpec((tile, n), lambda i, m: (part * tiles + i, 0))
    weights = [*out_w, *proj_w, *fc_w, *qkv_w]
    tail = [small, *qbs, fb]
    sums = (5, 8, width)
    packed = (32, 1, 128)
    last = part == parts - 1
    extra, extra_specs, aliases = [], [], {}
    count = 5 + len(atts) + len(qgs) + len(weights) + len(tail)
    if before is not None:
        extra = [before[2], before[0], before[1]]
        extra_specs = [full_spec(sums), pl.BlockSpec(memory_space=pl.ANY), pl.BlockSpec(memory_space=pl.ANY)]
        aliases = {count + 1: 0, count + 2: 1}
    scratch = [
        pltpu.VMEM(qkv_w[0].shape, bf16),
        pltpu.VMEM(qkv_w[0].shape, bf16),
        pltpu.VMEM((tile, width), f32),
        pltpu.VMEM((tile, width), f32),
    ]
    if last:
        scratch += [pltpu.VMEM(sums, f32), pltpu.VMEM((12, 1, 128), f32)]
    given = [packed, packed] if last else [sums]
    grid_spec = pltpu.PrefetchScalarGridSpec(
        num_scalar_prefetch=1,
        grid=(tiles,),
        in_specs=[
            blk(width),
            blk(width),
            *[blk(a.shape[1]) for a in (act, hg, *atts, *qgs)],
            *[full_spec(w.shape) for w in weights],
            *[full_spec(w.shape) for w in tail],
            *extra_specs,
        ],
        out_specs=[blk(width), blk(width), *[full_spec(g) for g in given]],
        scratch_shapes=scratch,
    )
    return pl.pallas_call(
        functools.partial(output_kernel, part, parts),
        grid_spec=grid_spec,
        out_shape=[
            jax.ShapeDtypeStruct((rows, width), bf16),
            jax.ShapeDtypeStruct((rows, width), bf16),
            *[jax.ShapeDtypeStruct(g, f32) for g in given],
        ],
        input_output_aliases=aliases,
        cost_estimate=cost(
            2 * rows * width * (512 + 2048 * 2 + 1536) // parts, 2 * rows * (4 * 512 + 4 * 2048) // parts
        ),
        name=f"outputs_{part}",
        compiler_params=pltpu.CompilerParams(vmem_limit_bytes=44 << 20),
    )(meta, tokens, grad, act, hg, *atts, *qgs, *weights, *tail, *extra)


def sum_kernel(n_in, *refs):
    ins, outs = refs[:n_in], refs[n_in:]
    for k, out in enumerate(outs):
        rows = out.shape[0]
        for i in range(rows):
            total = ins[0][k * rows + i].astype(f32)
            for term in ins[1:]:
                total += term[k * rows + i].astype(f32)
            out[i] = total.astype(out.dtype)


def sum_call(terms, count, name):
    shape, dtype = terms[0].shape, terms[0].dtype
    moved = len(terms) * terms[0].size * terms[0].dtype.itemsize
    return pl.pallas_call(
        functools.partial(sum_kernel, len(terms)),
        out_shape=[jax.ShapeDtypeStruct((shape[0] // count, *shape[1:]), dtype)] * count,
        compiler_params=pltpu.CompilerParams(vmem_limit_bytes=(moved * 3) // 2 + (4 << 20)),
        cost_estimate=cost(moved, 2 * moved),
        name=name,
    )(*terms)


def along_kernel(n_in, meta, *refs):
    ins, outs = refs[:n_in], refs[n_in:]
    rows = outs[0].shape[1]
    for k, out in enumerate(outs):
        at = pl.ds(pl.multiple_of((meta[3] ^ k) * rows, rows), rows)
        total = ins[0][0, at, :].astype(f32)
        for term in ins[1:]:
            total += term[0, at, :].astype(f32)
        out[0] = total.astype(bf16)


def join_kernel(meta, *refs):
    ins, out = refs[:4], refs[4]
    rows = ins[0].shape[1]
    for k, piece in enumerate(ins):
        out[0, pl.ds(pl.multiple_of((meta[3] ^ k) * rows, rows), rows), :] = piece[0]


def along_call(kernel, meta, terms, outs, name):
    moved = 2 * sum(a.size for a in terms)
    whole = pl.BlockSpec(memory_space=pltpu.VMEM)
    return pl.pallas_call(
        kernel,
        in_specs=[pl.BlockSpec(memory_space=pltpu.SMEM), *[whole] * len(terms)],
        out_specs=[whole] * len(outs),
        out_shape=[jax.ShapeDtypeStruct(o, bf16) for o in outs],
        compiler_params=pltpu.CompilerParams(vmem_limit_bytes=(moved * 3) // 2 + (4 << 20)),
        cost_estimate=cost(moved, 2 * moved),
        name=name,
    )(meta, *terms)


def exchange(a, reps, far, near):
    pairs = [(2 * i + c, 2 * (i ^ (near if c else far)) + c) for i in range(reps) for c in range(2)]
    return lax.ppermute(a, ("rep", "opt"), pairs)


def swap(a):
    return lax.ppermute(a, "opt", [(0, 1), (1, 0)])


def tie(value, *others):
    return lax.optimization_barrier((value, *others))[0]


def rest_bits(reps):
    return [1 << b for b in range(2, reps.bit_length() - 1)]


def crosses(pieces, reps):
    steps = ((2, 1), (1, 2), (3, 3))
    return [exchange(a, reps, *step) for a, step in zip(pieces, steps)]


def along(pieces, reps):
    return [exchange(a, reps, 4 * k, 4 * k) for k, a in enumerate(pieces, 1)]


def adamw(grad, mean, square, weight):
    new_mean = BETA_ONE * mean + (1.0 - BETA_ONE) * grad
    new_square = BETA_TWO * square + (1.0 - BETA_TWO) * grad * grad
    step = -LEARN_RATE * (
        new_mean * (1.0 / FIX_ONE) / (jnp.sqrt(new_square * (1.0 / FIX_TWO)) + ADAM_EPS)
        + WEIGHT_DECAY * weight.astype(f32)
    )
    return step, new_mean, new_square


def pick(refs, which, cols, rows=slice(None)):
    out = refs[0][0, rows, cols]
    for k in range(1, len(refs)):
        out = jnp.where(which == k, refs[k][0, rows, cols], out)
    return out.astype(f32)


def adam_block(grad, m_ref, s_ref, w_ref, g_out, st_out, m_out, s_out, at):
    step, mean, square = adamw(grad, m_ref[at], s_ref[at], w_ref[at])
    g_out[at] = grad
    st_out[at] = step
    m_out[at] = mean
    s_out[at] = square


def adam_ff_kernel(meta, *refs):
    pieces, proj, fc, proj_out, fc_out = refs[:4], refs[4:7], refs[7:10], refs[10:14], refs[14:18]
    which = pl.program_id(0) ^ meta[1]
    quarter = fc[0].shape[0]
    for j in range(2):
        for k in range(2):
            at = (j, slice(k * quarter, (k + 1) * quarter), slice(None))
            col = 1024 * j + 512 * k
            adam_block(pick(pieces, which, slice(col, col + 512)), *proj, *proj_out, at)
            at = (slice(None), slice(col, col + 512))
            adam_block(pick(pieces, which, slice(2048 + col, 2048 + col + 512)), *fc, *fc_out, at)


def adam_qkv_kernel(meta, *refs):
    sets, qkv, out, qkv_out, out_out = (refs[:4], refs[4:8]), refs[8:11], refs[11:14], refs[14:18], refs[18:22]
    c = meta[0]
    which = pl.program_id(0) ^ meta[1]
    quarter = qkv[0].shape[0]
    hq = quarter // 2
    for j, pieces in enumerate(sets):
        for slot in range(2):
            for p in range(3):
                col = 384 * slot + 128 * p
                grad = pick(pieces, which, slice(col, col + 128))
                lanes = pl.ds(pl.multiple_of((p * 4 + (slot ^ c) * 2 + j) * 128, 128), 128)
                adam_block(grad, *qkv, *qkv_out, (slice(None), lanes))
        for k in range(2):
            grad = pick(pieces, which, slice(768, 1024), slice(k * hq, (k + 1) * hq))
            adam_block(grad, *out, *out_out, (j, slice(None), slice(256 * k, 256 * k + 256)))


def adam_call(kernel, meta, pieces, first, second, first_spec, second_spec, name):
    outs = [jax.ShapeDtypeStruct(first[0].shape, f32)] * 4 + [jax.ShapeDtypeStruct(second[0].shape, f32)] * 4
    grid_spec = pltpu.PrefetchScalarGridSpec(
        num_scalar_prefetch=1,
        grid=(4,),
        in_specs=[*[full_spec(a.shape) for a in pieces], *[first_spec] * 3, *[second_spec] * 3],
        out_specs=[*[first_spec] * 4, *[second_spec] * 4],
    )
    size = first[0].size + second[0].size
    return pl.pallas_call(
        kernel,
        grid_spec=grid_spec,
        out_shape=outs,
        compiler_params=pltpu.CompilerParams(vmem_limit_bytes=56 << 20),
        cost_estimate=cost(20 * size, 28 * size),
        name=name,
    )(meta, *pieces, *first, *second)


def body(
    tokens,
    out_grad,
    vectors,
    qkv_weight,
    qkv_bias,
    out_weight,
    fc_weight,
    fc_bias,
    proj_weight,
    mean_vectors,
    mean_qkv_weight,
    mean_qkv_bias,
    mean_out_weight,
    mean_fc_weight,
    mean_fc_bias,
    mean_proj_weight,
    square_vectors,
    square_qkv_weight,
    square_qkv_bias,
    square_out_weight,
    square_fc_weight,
    square_fc_bias,
    square_proj_weight,
):
    reps = lax.axis_size("rep")
    c = lax.axis_index("opt")
    place = lax.axis_index("rep")
    low, high = place & 1, (place >> 1) & 1
    ranks = jnp.stack([2 * low + high, 2 * high + low])
    meta = jnp.stack([c, ranks[c], ranks[1 - c], (place >> 2) & 3]).astype(jnp.int32)
    trig = jnp.asarray(trig_tables())

    packed = jnp.concatenate(
        [vectors.reshape(12, 128), qkv_bias.reshape(6, 128), fc_bias.reshape(8, 128)], 0
    )
    small = lax.all_gather(packed, "opt", axis=0, tiled=True).astype(f32).reshape(2 * SMALL_ROWS, 1, 128)
    fc_far = swap(fc_weight)
    proj_far = swap(proj_weight)
    qkv_far = swap(qkv_weight)
    out_far = swap(out_weight)

    first, second = norm_call(tokens, small)
    send, act, hg, fb = ff_call(meta, second, out_grad, fc_weight, fc_far, proj_weight, proj_far, small)
    got = swap(send)
    own = ff_own_call(tie(meta, send), second, out_grad, act, hg)

    att = {}
    sets = {}
    bits = rest_bits(reps)

    def attend(j, rel, *wait):
        out_w = out_far if rel else out_weight
        before = att[j, 1][:2] if rel == 0 else ()
        att[j, rel] = attention_call(
            j, rel, tie(meta, *wait), first, out_grad, qkv_weight, qkv_far, out_w, small, trig, before
        )
        return att[j, rel][4]

    def rest(total, name):
        for bit in bits[2:]:
            (total,) = sum_call([total, exchange(total, reps, bit, bit)], 1, name)
        return total

    keep, send = sum_call([own, got], 2, "ff_pair")
    got = exchange(send, reps, 1, 2)
    mark = attend(0, 1, keep)
    keep, send = sum_call([tie(keep, mark), got], 2, "ff_sum0")
    got = exchange(send, reps, 2, 1)
    mark = attend(0, 0, keep)
    rows = keep.shape[1]
    part = (1, rows // 4, keep.shape[2])
    pieces = along_call(functools.partial(along_kernel, 2), meta, [tie(keep, mark), got], [part] * 4, "ff_sum1")
    got = along(pieces[1:], reps)
    c_own, c_got = att[0, 0][0], swap(att[0, 0][1])
    mark = attend(1, 1, *pieces)
    (piece,) = sum_call([tie(pieces[0], mark), *got], 1, "ff_sum2")
    piece = rest(piece, "ff_sum3")
    pieces = [piece, *along([piece] * 3, reps)]
    c_keep, c_send = sum_call([tie(c_own, mark), c_got], 2, "att_pair")
    c_got = exchange(c_send, reps, 1, 2)
    mark = attend(1, 0, piece, c_keep)

    d_own, d_got = att[1, 0][0], swap(att[1, 0][1])
    (ff_total,) = along_call(join_kernel, meta, [tie(pieces[0], mark), *pieces[1:]], [keep[:1].shape], "ff_join")
    ff_pieces = [ff_total, exchange(ff_total, reps, 2, 1), exchange(ff_total, reps, 1, 2)]
    c_keep, c_send = sum_call([tie(c_keep, mark), c_got], 2, "att_sum0")
    c_got = exchange(c_send, reps, 2, 1)

    keys = [(0, 0), (0, 1), (1, 0), (1, 1)]
    give = lambda part, before, *wait: output_call(
        part,
        PARTS,
        tie(meta, *wait),
        tokens,
        out_grad,
        act,
        hg,
        [att[k][3] for k in keys],
        [att[k][2] for k in keys],
        (out_weight, out_far),
        (proj_weight, proj_far),
        (fc_weight, fc_far),
        (qkv_weight, qkv_far),
        small,
        [att[k][4] for k in keys],
        fb,
        before,
    )
    done = give(0, None, ff_total, c_keep)
    mark = done[2]
    d_keep, d_send = sum_call([tie(d_own, mark), d_got], 2, "att_pair")
    d_got = exchange(d_send, reps, 1, 2)
    (c_total,) = sum_call([tie(c_keep, mark), c_got], 1, "att_sum1")
    c_got = along([c_total] * 3, reps)
    ff_pieces.append(exchange(tie(ff_pieces[2], mark), reps, 2, 1))
    layer_out, tokens_grad, small_own, small_send = give(1, done, d_keep, c_total, *ff_pieces[1:3])

    (c_total,) = sum_call([tie(c_total, small_own), *c_got], 1, "att_sum2")
    c_total = rest(c_total, "att_sum3")
    d_keep, d_send = sum_call([tie(d_keep, c_total), d_got], 2, "att_sum0")
    d_got = exchange(d_send, reps, 2, 1)
    (total,) = sum_call([tie(small_own, d_keep), swap(small_send)], 1, "small_pair")
    (d_total,) = sum_call([tie(d_keep, total), d_got], 1, "att_sum1")
    d_got = along([d_total] * 3, reps)
    ff_last = tie(ff_pieces[3], d_total)
    c_pieces = [c_total, exchange(tie(c_total, ff_last), reps, 2, 1), exchange(tie(c_total, ff_last), reps, 1, 2)]

    view = lambda a: a.reshape(2, 512, 512)
    proj_adam = adam_call(
        adam_ff_kernel,
        tie(meta, total, d_total, ff_last),
        [*ff_pieces[:3], ff_last],
        [view(a) for a in (mean_proj_weight, square_proj_weight, proj_weight)],
        [mean_fc_weight, square_fc_weight, fc_weight],
        pl.BlockSpec((2, 128, 512), lambda q, m: (0, q, 0)),
        pl.BlockSpec((64, 2048), lambda q, m: (q, 0)),
        "adam_ff",
    )
    a_proj = [a.reshape(1024, 512) for a in proj_adam[:4]]
    a_fc = proj_adam[4:]

    (d_total,) = sum_call([tie(d_total, a_fc[0], *c_pieces[1:]), *d_got], 1, "att_sum4")
    d_total = rest(d_total, "att_sum5")
    d_pieces = [d_total, *crosses([d_total] * 3, reps)]
    c_pieces.append(exchange(tie(c_pieces[2], d_total), reps, 2, 1))
    total = tie(total, d_total)
    for bit in (1, 2, *bits):
        if bit == bits[-1]:
            total = tie(total, *c_pieces[1:], *d_pieces[1:])
        (total,) = sum_call([total, exchange(total, reps, bit, bit)], 1, "small_sum")
    flat = total.reshape(32, 128)
    g_vec = flat[:12].reshape(6, 256)
    g_qb = flat[12:18].reshape(768)
    g_fb = flat[18:26].reshape(1024)

    view_o = lambda a: a.reshape(2, 128, 512)
    qkv_adam = adam_call(
        adam_qkv_kernel,
        meta,
        [*c_pieces, *d_pieces],
        [mean_qkv_weight, square_qkv_weight, qkv_weight],
        [view_o(a) for a in (mean_out_weight, square_out_weight, out_weight)],
        pl.BlockSpec((64, 1536), lambda q, m: (q, 0)),
        pl.BlockSpec((2, 32, 512), lambda q, m: (0, q, 0)),
        "adam_qkv",
    )
    a_qkv = qkv_adam[:4]
    a_out = [a.reshape(256, 512) for a in qkv_adam[4:]]
    a_vec = (g_vec, *adamw(g_vec, mean_vectors, square_vectors, vectors))
    a_qb = (g_qb, *adamw(g_qb, mean_qkv_bias, square_qkv_bias, qkv_bias))
    a_fb = (g_fb, *adamw(g_fb, mean_fc_bias, square_fc_bias, fc_bias))
    order = (a_vec, a_qkv, a_qb, a_out, a_fc, a_fb, a_proj)
    return (layer_out, tokens_grad, *[a[k] for k in range(4) for a in order])


def solution(mesh):
    rows = P(("rep", "opt"), None)
    weights = (P(None, "opt"), P("opt", None), P("opt"), P("opt", None), P("opt", None), P("opt"), P("opt", None))
    in_specs = (rows, rows, *weights, *weights, *weights)
    out_specs = (rows, rows, *weights, *weights, *weights, *weights)
    return jax.shard_map(body, mesh=mesh, in_specs=in_specs, out_specs=out_specs, check_vma=False)
```

```python
import functools

import jax
import jax.numpy as jnp
import numpy as np
from jax import lax
from jax.experimental import pallas as pl
from jax.experimental.pallas import tpu as pltpu
from jax.sharding import PartitionSpec as P

H = 8
ROT = 16
LEN = 512
ADAM_STEP = 10

LN_EPS = 1e-05
ADAM_EPS = 1e-08
BETA_ONE = 0.9
BETA_TWO = 0.95
LEARN_RATE = 0.02
WEIGHT_DECAY = 0.01
FIX_ONE = 1.0 - BETA_ONE**ADAM_STEP
FIX_TWO = 1.0 - BETA_TWO**ADAM_STEP
INV_ROOT_TWO = 0.7071067811865476
INV_ROOT_TWO_PI = 0.3989422804014327

bf16 = jnp.bfloat16
f32 = jnp.float32
PARTS = 2
SMALL_ROWS = 26


def dot_nn(a, b):
    return lax.dot_general(a, b, (((1,), (0,)), ((), ())), preferred_element_type=f32)


def dot_nt(a, b):
    return lax.dot_general(a, b, (((1,), (1,)), ((), ())), preferred_element_type=f32)


def dot_tn(a, b):
    return lax.dot_general(a, b, (((0,), (0,)), ((), ())), preferred_element_type=f32)


def full_spec(shape):
    zeros = (0,) * len(shape)
    return pl.BlockSpec(shape, lambda *_: zeros)


def cost(flops, moved, transcendentals=0):
    return pl.CostEstimate(
        flops=int(flops), bytes_accessed=int(moved), transcendentals=int(transcendentals)
    )


def vec_row(small_ref, i):
    n = SMALL_ROWS
    rows = [small_ref[o * n + 2 * i + k] for o in range(2) for k in range(2)]
    return jnp.concatenate(rows, 1)


def normalise(x):
    centre = x - jnp.mean(x, -1, keepdims=True)
    inv_dev = lax.rsqrt(jnp.mean(centre * centre, -1, keepdims=True) + LN_EPS)
    return centre * inv_dev, inv_dev


def norm_kernel(tok_ref, small_ref, first_ref, second_ref):
    normed, _ = normalise(tok_ref[...].astype(f32))
    first_ref[...] = (normed * vec_row(small_ref, 0) + vec_row(small_ref, 1)).astype(bf16)
    second_ref[...] = (normed * vec_row(small_ref, 2) + vec_row(small_ref, 3)).astype(bf16)


def norm_call(tokens, small):
    rows, width = tokens.shape
    tile = 512
    spec = pl.BlockSpec((tile, width), lambda i: (i, 0))
    out = jax.ShapeDtypeStruct((rows, width), bf16)
    return pl.pallas_call(
        norm_kernel,
        grid=(rows // tile,),
        in_specs=[spec, full_spec(small.shape)],
        out_specs=[spec, spec],
        out_shape=[out, out],
        cost_estimate=cost(20 * rows * width, 6 * rows * width),
        name="norm",
        compiler_params=pltpu.CompilerParams(vmem_limit_bytes=12 << 20),
    )(tokens, small)


def ff_kernel(meta, second_ref, grad_ref, fco_ref, fcx_ref, pro_ref, prx_ref, small_ref,
              send_ref, act_ref, hg_ref, bias_ref, fc_ref):
    j = pl.program_id(0)
    rel = pl.program_id(1)
    c = meta[0]
    far_rank = meta[2]
    o = rel ^ c
    rows, width = second_ref.shape
    half = width // 2
    cols = act_ref.shape[1]
    quarter = half // 4
    proj = jnp.where(rel == 0, pro_ref[...], prx_ref[...])
    own_lanes = pl.ds(pl.multiple_of(c * half, half), half)
    far_lanes = pl.ds(pl.multiple_of((1 - c) * half, half), half)
    fc_ref[own_lanes, :] = fco_ref[...]
    fc_ref[far_lanes, :] = fcx_ref[...]
    fc = fc_ref[...]
    base = o * SMALL_ROWS + 18 + 4 * j
    bias = jnp.concatenate([small_ref[base + k] for k in range(cols // 128)], 1)
    tile = 256

    def block(i, total):
        r = pl.ds(pl.multiple_of(i * tile, tile), tile)
        hidden = dot_nn(second_ref[r, :], fc) + bias
        act_grad = dot_nt(grad_ref[r, :], proj)
        phi_cap = 0.5 + 0.5 * lax.erf(hidden * INV_ROOT_TWO)
        slope = phi_cap + hidden * (jnp.exp(-0.5 * hidden * hidden) * INV_ROOT_TWO_PI)
        act_ref[r, :] = (hidden * phi_cap).astype(bf16)
        hg = (act_grad * slope).astype(bf16)
        hg_ref[r, :] = hg
        return total + jnp.sum(hg.astype(f32).reshape(tile // 8, 8, cols), 0)

    total = lax.fori_loop(0, rows // tile, block, jnp.zeros((8, cols), f32))
    bias_ref[...] = jnp.sum(total, 0, keepdims=True)[None]
    pl.when(rel == 1)(lambda: put_proj(send_ref, dot_tn(act_ref[...], grad_ref[...]), j, far_rank))
    put_fc(send_ref, dot_tn(second_ref[:, far_lanes], hg_ref[...]), o, j, far_rank)


def put_proj(ref, grad, j, rank):
    quarter = ref.shape[1]
    lanes = pl.ds(pl.multiple_of(j * 1024, 1024), 1024)
    for a in range(4):
        piece = grad[a * 2 * quarter : (a + 1) * 2 * quarter]
        ref[a ^ rank, :, lanes] = jnp.concatenate([piece[:quarter], piece[quarter:]], 1).astype(bf16)


def put_fc(ref, grad, o, j, rank):
    quarter = ref.shape[1]
    cols = grad.shape[1]
    lanes = pl.ds(pl.multiple_of(2048 + o * 1024 + j * cols, cols), cols)
    for a in range(4):
        ref[a ^ rank, :, lanes] = grad[a * quarter : (a + 1) * quarter].astype(bf16)


def ff_own_kernel(meta, second_ref, grad_ref, act_ref, hg_ref, own_ref):
    j = pl.program_id(0)
    rel = pl.program_id(1)
    c = meta[0]
    rank = meta[1]
    half = second_ref.shape[1] // 2
    own_lanes = pl.ds(pl.multiple_of(c * half, half), half)
    pl.when(rel == 0)(lambda: put_proj(own_ref, dot_tn(act_ref[...], grad_ref[...]), j, rank))
    put_fc(own_ref, dot_tn(second_ref[:, own_lanes], hg_ref[...]), rel ^ c, j, rank)


def ff_call(meta, second, grad, fc_own, fc_far, proj_own, proj_far, small):
    rows, width = second.shape
    ff = fc_own.shape[1]
    half = width // 2
    cols = ff // 4
    buf = (4, half // 4, 2 * ff)
    fc_spec = pl.BlockSpec((half, cols), lambda j, r, m: (0, (r ^ m[0]) * 2 + j))
    proj_spec = pl.BlockSpec((cols, width), lambda j, r, m: (j, 0))
    act_spec = pl.BlockSpec((rows, cols), lambda j, r, m: (0, 2 * j + r))
    grid_spec = pltpu.PrefetchScalarGridSpec(
        num_scalar_prefetch=1,
        grid=(2, 2),
        in_specs=[
            full_spec((rows, width)),
            full_spec((rows, width)),
            fc_spec,
            fc_spec,
            proj_spec,
            proj_spec,
            full_spec(small.shape),
        ],
        out_specs=[
            full_spec(buf),
            act_spec,
            act_spec,
            pl.BlockSpec((1, 1, cols), lambda j, r, m: (2 * j + r, 0, 0)),
        ],
        scratch_shapes=[pltpu.VMEM((width, cols), bf16)],
    )
    return pl.pallas_call(
        ff_kernel,
        grid_spec=grid_spec,
        out_shape=[
            jax.ShapeDtypeStruct(buf, bf16),
            jax.ShapeDtypeStruct((rows, ff), bf16),
            jax.ShapeDtypeStruct((rows, ff), bf16),
            jax.ShapeDtypeStruct((4, 1, cols), f32),
        ],
        cost_estimate=cost(6 * rows * width * ff, 4 * rows * width + 4 * rows * ff),
        name="feed_forward",
        compiler_params=pltpu.CompilerParams(vmem_limit_bytes=40 << 20),
    )(meta, second, grad, fc_own, fc_far, proj_own, proj_far, small)


def ff_own_call(meta, second, grad, act, hg):
    rows, width = second.shape
    ff = act.shape[1]
    cols = ff // 4
    buf = (4, width // 8, 2 * ff)
    grid_spec = pltpu.PrefetchScalarGridSpec(
        num_scalar_prefetch=1,
        grid=(2, 2),
        in_specs=[
            full_spec((rows, width)),
            full_spec((rows, width)),
            pl.BlockSpec((rows, cols), lambda j, r, m: (0, 2 * j)),
            pl.BlockSpec((rows, cols), lambda j, r, m: (0, 2 * j + r)),
        ],
        out_specs=full_spec(buf),
    )
    return pl.pallas_call(
        ff_own_kernel,
        grid_spec=grid_spec,
        out_shape=jax.ShapeDtypeStruct(buf, bf16),
        cost_estimate=cost(2 * rows * width * ff, 4 * rows * width + 3 * rows * ff),
        name="feed_forward_own",
        compiler_params=pltpu.CompilerParams(vmem_limit_bytes=44 << 20),
    )(meta, second, grad, act, hg)


def rotate_rows(x, cosine, sine):
    parts = []
    for h in range(2):
        low, high = x[64 * h : 64 * h + 8], x[64 * h + 8 : 64 * h + 16]
        parts += [low * cosine - high * sine, high * cosine + low * sine, x[64 * h + 16 : 64 * h + 64]]
    return jnp.concatenate(parts, 0)


def attention_kernel(j, rel, meta, first_ref, grad_ref, wq_ref, wk_ref, wv_ref, xq_ref, xk_ref, xv_ref,
                     ow_ref, small_ref, trig_ref, *refs):
    if rel == 0:
        own_first_ref, send_first_ref, refs = refs[0], refs[1], refs[2:]
    own_ref, send_ref, qg_ref, att_ref, bias_ref, wt_ref, bcol_ref, qgs_ref, attt_ref, btot_ref = refs
    s = pl.program_id(0)
    c = meta[0]
    rank, far_rank = meta[1], meta[2]
    o = rel ^ c
    rows, width = first_ref.shape
    half = width // 2
    quarter = half // 4
    own_lanes = pl.ds(pl.multiple_of(c * half, half), half)
    far_lanes = pl.ds(pl.multiple_of((1 - c) * half, half), half)

    @pl.when(s == 0)
    def _():
        for p, (own, far) in enumerate(((wq_ref, xq_ref), (wk_ref, xk_ref), (wv_ref, xv_ref))):
            wt_ref[128 * p : 128 * (p + 1), own_lanes] = own[...].T
            wt_ref[128 * p : 128 * (p + 1), far_lanes] = far[...].T
            row = p * 4 + o * 2 + j
            owner = row // 6
            bias = small_ref[owner * SMALL_ROWS + 12 + row - 6 * owner]
            bcol_ref[128 * p : 128 * (p + 1), :] = jnp.broadcast_to(bias, (128, 128)).T
        btot_ref[...] = jnp.zeros_like(btot_ref)

    seq = pl.ds(pl.multiple_of(s * LEN, LEN), LEN)
    first = first_ref[seq, :]
    grad = grad_ref[seq, :]
    mixed = dot_nt(wt_ref[...], first) + bcol_ref[:, :1]
    da_t = dot_nt(ow_ref[...], grad).astype(bf16)
    cosine, sine = trig_ref[0], trig_ref[1]
    q_t = rotate_rows(mixed[:128], cosine, sine).astype(bf16) * jnp.asarray(0.125, bf16)
    k_t = rotate_rows(mixed[128:256], cosine, sine).astype(bf16)
    v_t = mixed[256:].astype(bf16)
    k_tok = k_t.T
    v_tok = v_t.T
    hl = LEN // 2
    row_id = lax.broadcasted_iota(jnp.int32, (hl, hl), 0)
    col_id = lax.broadcasted_iota(jnp.int32, (hl, hl), 1)
    keep = row_id <= col_id
    zeros = jnp.zeros((64, LEN), bf16)
    att, dq, dk, dv = [], [], [], []
    for h in range(2):
        hs = slice(64 * h, 64 * h + 64)
        qh, kh, vh, dah = q_t[hs], k_t[hs], v_t[hs], da_t[hs]
        pad = (lambda u: jnp.concatenate([u, zeros], 0)) if h == 0 else (lambda u: jnp.concatenate([zeros, u], 0))
        qz, daz = pad(qh), pad(dah)
        att_h, dq_h = [], []
        dk_h = dv_h = None
        for t in range(2):
            ts = slice(hl * t, hl * t + hl)
            n = hl * (t + 1)
            score = dot_nn(k_tok[:n], qz[:, ts])
            diag = jnp.where(keep, score[n - hl :], -1e30)
            score = diag if t == 0 else jnp.concatenate([score[:hl], diag], 0)
            exps = jnp.exp(score - jnp.max(score, 0, keepdims=True))
            prob = exps * (1.0 / jnp.sum(exps, 0, keepdims=True))
            prob_b = prob.astype(bf16)
            att_h.append(dot_nn(vh[:, :n], prob_b))
            pg = dot_nn(v_tok[:n], daz[:, ts])
            sg = (prob * (pg - jnp.sum(pg * prob, 0, keepdims=True))).astype(bf16)
            dq_h.append(dot_nn(kh[:, :n], sg))
            dv_t = dot_nt(dah[:, ts], prob_b)
            dk_t = dot_nt(qh[:, ts], sg)
            if t == 0:
                dv_h, dk_h = dv_t, dk_t
            else:
                dv_h = jnp.concatenate([dv_h + dv_t[:, :hl], dv_t[:, hl:]], 1)
                dk_h = jnp.concatenate([dk_h + dk_t[:, :hl], dk_t[:, hl:]], 1)
        att.append(jnp.concatenate(att_h, 1))
        dq.append(jnp.concatenate(dq_h, 1) * 0.125)
        dk.append(dk_h)
        dv.append(dv_h)
    att_t = jnp.concatenate(att, 0).astype(bf16)
    dq_t = rotate_rows(jnp.concatenate(dq, 0), cosine, -sine)
    dk_t = rotate_rows(jnp.concatenate(dk, 0), cosine, -sine)
    qkv_t = jnp.concatenate([dq_t, dk_t, jnp.concatenate(dv, 0)], 0).astype(bf16)
    qkv_g = qkv_t.T
    qg_ref[...] = qkv_g
    qgs_ref[seq, :] = qkv_g
    att_ref[...] = att_t.T
    attt_ref[:, seq] = att_t
    btot_ref[...] += jnp.sum(qkv_g.astype(f32).reshape(LEN // 8, 8, 384), 0)

    @pl.when(s == pl.num_programs(0) - 1)
    def _():
        bias_ref[...] = jnp.sum(btot_ref[...], 0, keepdims=True)
        at_own, at_send = (0, 384) if rel == 0 else (0, 0)
        if rel == 0:
            own_ref[:, :, 384:768] = own_first_ref[...]
            send_ref[:, :, :384] = send_first_ref[:, :, :384]
            send_ref[:, :, 768:] = send_first_ref[:, :, 384:]
        for ref, side, number, at in ((own_ref, own_lanes, rank, at_own), (send_ref, far_lanes, far_rank, at_send)):
            gw = dot_tn(first_ref[:, side], qgs_ref[...])
            for a in range(4):
                ref[a ^ number, :, at : at + 384] = gw[a * quarter : (a + 1) * quarter].astype(bf16)
        go = dot_nn(attt_ref[...], grad_ref[...])
        hq = quarter // 2
        for a in range(4):
            piece = go[a * hq : (a + 1) * hq]
            piece = jnp.concatenate([piece[:, :256], piece[:, 256:]], 0).astype(bf16)
            if rel == 0:
                own_ref[a ^ rank, :, 768:] = piece
            else:
                send_ref[a ^ far_rank, :, 384:] = piece


def trig_tables():
    freqs = np.power(np.float32(10000.0), -np.arange(0, ROT, 2).astype(np.float32) / np.float32(ROT))
    angles = (np.arange(LEN).astype(np.float32)[None, :] * freqs[:, None]).astype(np.float32)
    return np.stack([np.cos(angles), np.sin(angles)]).astype(np.float32)


def attention_call(j, rel, meta, first, grad, qkv_own, qkv_far, out_w, small, trig, before=()):
    rows, width = first.shape
    half = width // 2
    bufs = [(4, half // 4, w) for w in ((1024, 1024) if rel == 0 else (384, 640))]
    w_specs = [
        pl.BlockSpec((half, 128), functools.partial(lambda p, s, m: (0, p * 4 + (rel ^ m[0]) * 2 + j), p))
        for p in range(3)
    ]
    grid_spec = pltpu.PrefetchScalarGridSpec(
        num_scalar_prefetch=1,
        grid=(rows // LEN,),
        in_specs=[
            full_spec((rows, width)),
            full_spec((rows, width)),
            *w_specs,
            *w_specs,
            pl.BlockSpec((128, width), lambda s, m: (j, 0)),
            full_spec(small.shape),
            full_spec(trig.shape),
            *[full_spec(a.shape) for a in before],
        ],
        out_specs=[
            *[full_spec(b) for b in bufs],
            pl.BlockSpec((LEN, 384), lambda s, m: (s, 0)),
            pl.BlockSpec((LEN, 128), lambda s, m: (s, 0)),
            full_spec((1, 384)),
        ],
        scratch_shapes=[
            pltpu.VMEM((384, width), bf16),
            pltpu.VMEM((384, 128), f32),
            pltpu.VMEM((rows, 384), bf16),
            pltpu.VMEM((128, rows), bf16),
            pltpu.VMEM((8, 384), f32),
        ],
    )
    flops = 2 * rows * width * (2 * 384 + 2 * 128) + 2 * 6 * 2 * rows * LEN * 128
    return pl.pallas_call(
        functools.partial(attention_kernel, j, rel),
        grid_spec=grid_spec,
        out_shape=[
            *[jax.ShapeDtypeStruct(b, bf16) for b in bufs],
            jax.ShapeDtypeStruct((rows, 384), bf16),
            jax.ShapeDtypeStruct((rows, 128), bf16),
            jax.ShapeDtypeStruct((1, 384), f32),
        ],
        cost_estimate=cost(flops, 4 * rows * width + 2 * rows * 512),
        name=f"attention_{j}{rel}",
        compiler_params=pltpu.CompilerParams(vmem_limit_bytes=18 << 20),
    )(meta, first, grad, *[qkv_own] * 3, *[qkv_far] * 3, out_w, small, trig, *before)


def output_kernel(part, parts, meta, tok_ref, grad_ref, act_ref, hg_ref, *refs):
    at_refs, qg_refs, refs = refs[0:4], refs[4:8], refs[8:]
    oo_ref, ox_ref, po_ref, px_ref, fo_ref, fx_ref, wo_ref, wx_ref, small_ref = refs[:9]
    qb_refs, fb_ref, refs = refs[9:13], refs[13], refs[14:]
    if part > 0:
        before_ref, refs = refs[0], refs[3:]
    lay_ref, tg_ref, refs = refs[0], refs[1], refs[2:]
    if part < parts - 1:
        tot_ref, wgo_ref, wgx_ref, sg_ref, fg_ref = refs
    else:
        own_ref, send_ref, wgo_ref, wgx_ref, sg_ref, fg_ref, tot_ref, qb_ref = refs
    i = pl.program_id(0)
    c = meta[0]
    tile, width = tok_ref.shape
    half = width // 2
    own_lanes = pl.ds(pl.multiple_of(c * half, half), half)
    far_lanes = pl.ds(pl.multiple_of((1 - c) * half, half), half)

    @pl.when(i == 0)
    def _():
        for w_ref, g_ref in ((wo_ref, wgo_ref), (wx_ref, wgx_ref)):
            for j in range(2):
                for rel in range(2):
                    for p in range(3):
                        src = pl.ds(pl.multiple_of((p * 4 + (rel ^ c) * 2 + j) * 128, 128), 128)
                        dst = (j * 6 + rel * 3 + p) * 128
                        g_ref[:, dst : dst + 128] = w_ref[:, src]
        tot_ref[...] = jnp.zeros_like(tot_ref) if part == 0 else before_ref[...]

    x = tok_ref[...].astype(f32)
    grad = grad_ref[...].astype(f32)
    normed, inv_dev = normalise(x)
    acc = dot_nn(jnp.concatenate([at_refs[0][...], at_refs[2][...]], 1), oo_ref[...])
    acc += dot_nn(jnp.concatenate([at_refs[1][...], at_refs[3][...]], 1), ox_ref[...])
    for j in range(2):
        for rel, p_ref in enumerate((po_ref, px_ref)):
            k = 512 * (2 * j + rel)
            acc += dot_nn(act_ref[:, k : k + 512], p_ref[512 * j : 512 * (j + 1), :])
    lay_ref[...] = (x + acc + (vec_row(small_ref, 4) + vec_row(small_ref, 5))).astype(bf16)

    for f_ref, wg_ref, lanes in ((fo_ref, wgo_ref, own_lanes), (fx_ref, wgx_ref, far_lanes)):
        total = None
        for j in range(2):
            for rel in range(2):
                k = 512 * (2 * j + rel)
                cols = pl.ds(pl.multiple_of((rel ^ c) * 1024 + 512 * j, 512), 512)
                term = dot_nt(hg_ref[:, k : k + 512], f_ref[:, cols])
                total = term if total is None else total + term
        sg_ref[:, lanes] = total
        qg = [jnp.concatenate([qg_refs[2 * j][...], qg_refs[2 * j + 1][...]], 1) for j in range(2)]
        fg_ref[:, lanes] = dot_nt(qg[0], wg_ref[:, :768]) + dot_nt(qg[1], wg_ref[:, 768:])
    second_g = sg_ref[...]
    first_g = fg_ref[...]
    e = first_g * vec_row(small_ref, 0) + second_g * vec_row(small_ref, 2)
    ln = inv_dev * (
        e - jnp.mean(e, -1, keepdims=True) - normed * jnp.mean(e * normed, -1, keepdims=True)
    )
    tg_ref[...] = (grad + ln).astype(bf16)
    for k, term in enumerate((first_g * normed, first_g, second_g * normed, second_g, grad)):
        tot_ref[k] += jnp.sum(term.reshape(tile // 8, 8, width), 0)

    if part < parts - 1:
        return

    @pl.when(i == pl.num_programs(0) - 1)
    def _():
        for j in range(2):
            for rel in range(2):
                for p in range(3):
                    qb_ref[p * 4 + (rel ^ c) * 2 + j] = qb_refs[2 * j + rel][:, 128 * p : 128 * (p + 1)]
        sums = [jnp.sum(tot_ref[k], 0, keepdims=True) for k in range(5)]
        sums.append(sums[4])
        for ref, rel in ((own_ref, 0), (send_ref, 1)):
            owner = rel ^ c
            for k in range(6):
                for part in range(2):
                    low = sums[k][:, 128 * part : 128 * (part + 1)]
                    high = sums[k][:, 256 + 128 * part : 256 + 128 * (part + 1)]
                    ref[2 * k + part] = jnp.where(owner == 0, low, high)
            for k in range(6):
                ref[12 + k] = qb_ref[owner * 6 + k]
            for j in range(2):
                for k in range(4):
                    ref[18 + 4 * j + k] = fb_ref[2 * j + rel][:, 128 * k : 128 * (k + 1)]
            for k in range(SMALL_ROWS, 32):
                ref[k] = jnp.zeros((1, 128), f32)


def output_call(part, parts, meta, tokens, grad, act, hg, atts, qgs, out_w, proj_w, fc_w, qkv_w, small, qbs, fb,
                before=None):
    rows, width = tokens.shape
    tile = 256
    tiles = rows // tile // parts
    blk = lambda n: pl.BlockSpec((tile, n), lambda i, m: (part * tiles + i, 0))
    weights = [*out_w, *proj_w, *fc_w, *qkv_w]
    tail = [small, *qbs, fb]
    sums = (5, 8, width)
    packed = (32, 1, 128)
    last = part == parts - 1
    extra, extra_specs, aliases = [], [], {}
    count = 5 + len(atts) + len(qgs) + len(weights) + len(tail)
    if before is not None:
        extra = [before[2], before[0], before[1]]
        extra_specs = [full_spec(sums), pl.BlockSpec(memory_space=pl.ANY), pl.BlockSpec(memory_space=pl.ANY)]
        aliases = {count + 1: 0, count + 2: 1}
    scratch = [
        pltpu.VMEM(qkv_w[0].shape, bf16),
        pltpu.VMEM(qkv_w[0].shape, bf16),
        pltpu.VMEM((tile, width), f32),
        pltpu.VMEM((tile, width), f32),
    ]
    if last:
        scratch += [pltpu.VMEM(sums, f32), pltpu.VMEM((12, 1, 128), f32)]
    given = [packed, packed] if last else [sums]
    grid_spec = pltpu.PrefetchScalarGridSpec(
        num_scalar_prefetch=1,
        grid=(tiles,),
        in_specs=[
            blk(width),
            blk(width),
            *[blk(a.shape[1]) for a in (act, hg, *atts, *qgs)],
            *[full_spec(w.shape) for w in weights],
            *[full_spec(w.shape) for w in tail],
            *extra_specs,
        ],
        out_specs=[blk(width), blk(width), *[full_spec(g) for g in given]],
        scratch_shapes=scratch,
    )
    return pl.pallas_call(
        functools.partial(output_kernel, part, parts),
        grid_spec=grid_spec,
        out_shape=[
            jax.ShapeDtypeStruct((rows, width), bf16),
            jax.ShapeDtypeStruct((rows, width), bf16),
            *[jax.ShapeDtypeStruct(g, f32) for g in given],
        ],
        input_output_aliases=aliases,
        cost_estimate=cost(
            2 * rows * width * (512 + 2048 * 2 + 1536) // parts, 2 * rows * (4 * 512 + 4 * 2048) // parts
        ),
        name=f"outputs_{part}",
        compiler_params=pltpu.CompilerParams(vmem_limit_bytes=30 << 20),
    )(meta, tokens, grad, act, hg, *atts, *qgs, *weights, *tail, *extra)


def sum_kernel(n_in, *refs):
    ins, outs = refs[:n_in], refs[n_in:]
    for k, out in enumerate(outs):
        rows = out.shape[0]
        for i in range(rows):
            total = ins[0][k * rows + i].astype(f32)
            for term in ins[1:]:
                total += term[k * rows + i].astype(f32)
            out[i] = total.astype(out.dtype)


def sum_call(terms, count, name):
    shape, dtype = terms[0].shape, terms[0].dtype
    moved = len(terms) * terms[0].size * terms[0].dtype.itemsize
    return pl.pallas_call(
        functools.partial(sum_kernel, len(terms)),
        out_shape=[jax.ShapeDtypeStruct((shape[0] // count, *shape[1:]), dtype)] * count,
        compiler_params=pltpu.CompilerParams(vmem_limit_bytes=(moved * 3) // 2 + (4 << 20)),
        cost_estimate=cost(moved, 2 * moved),
        name=name,
    )(*terms)


def pair_kernel(*refs):
    own, got, outs = refs[:2], refs[2:4], refs[4:]
    for j, (mine, other) in enumerate(zip(own, got)):
        w = mine.shape[2]
        for k, out in enumerate(outs):
            total = mine[k].astype(f32) + other[k].astype(f32)
            out[0, :, j * w : (j + 1) * w] = total.astype(bf16)


def pair_call(own, got, name):
    rows, width = own[0].shape[1], 2 * own[0].shape[2]
    return pl.pallas_call(
        pair_kernel,
        out_shape=[jax.ShapeDtypeStruct((1, rows, width), bf16)] * 4,
        compiler_params=pltpu.CompilerParams(vmem_limit_bytes=12 << 20),
        cost_estimate=cost(8 * rows * width, 24 * rows * width),
        name=name,
    )(*own, *got)


def half_kernel(meta, mine_ref, got_ref, keep_ref, send_ref):
    rows = keep_ref.shape[1]
    for out, number in ((keep_ref, meta[3]), (send_ref, 1 - meta[3])):
        at = pl.ds(pl.multiple_of(number * rows, rows), rows)
        out[0] = (mine_ref[0, at, :].astype(f32) + got_ref[0, at, :].astype(f32)).astype(bf16)


def join_kernel(meta, mine_ref, got_ref, out_ref):
    rows = mine_ref.shape[1]
    for piece, number in ((mine_ref, meta[3]), (got_ref, 1 - meta[3])):
        out_ref[0, pl.ds(pl.multiple_of(number * rows, rows), rows), :] = piece[0]


def half_call(kernel, meta, terms, outs, name):
    moved = 2 * sum(a.size for a in terms)
    whole = pl.BlockSpec(memory_space=pltpu.VMEM)
    return pl.pallas_call(
        kernel,
        in_specs=[pl.BlockSpec(memory_space=pltpu.SMEM), whole, whole],
        out_specs=[whole] * len(outs),
        out_shape=[jax.ShapeDtypeStruct(o, bf16) for o in outs],
        compiler_params=pltpu.CompilerParams(vmem_limit_bytes=(moved * 3) // 2 + (4 << 20)),
        cost_estimate=cost(moved, 2 * moved),
        name=name,
    )(meta, *terms)


def exchange(a, reps, far, near):
    pairs = [(2 * i + c, 2 * (i ^ (near if c else far)) + c) for i in range(reps) for c in range(2)]
    return lax.ppermute(a, ("rep", "opt"), pairs)


def swap(a):
    return lax.ppermute(a, "opt", [(0, 1), (1, 0)])


def tie(value, *others):
    return lax.optimization_barrier((value, *others))[0]


def rest_bits(reps):
    return [1 << b for b in range(2, reps.bit_length() - 1)]


def crosses(pieces, reps):
    steps = ((2, 1), (1, 2), (3, 3))
    return [exchange(a, reps, *step) for a, step in zip(pieces, steps)]


def adamw(grad, mean, square, weight):
    new_mean = BETA_ONE * mean + (1.0 - BETA_ONE) * grad
    new_square = BETA_TWO * square + (1.0 - BETA_TWO) * grad * grad
    step = -LEARN_RATE * (
        new_mean * (1.0 / FIX_ONE) / (jnp.sqrt(new_square * (1.0 / FIX_TWO)) + ADAM_EPS)
        + WEIGHT_DECAY * weight.astype(f32)
    )
    return step, new_mean, new_square


def pick(refs, which, cols, rows=slice(None)):
    out = refs[0][0, rows, cols]
    for k in range(1, len(refs)):
        out = jnp.where(which == k, refs[k][0, rows, cols], out)
    return out.astype(f32)


def adam_block(grad, m_ref, s_ref, w_ref, g_out, st_out, m_out, s_out, at):
    step, mean, square = adamw(grad, m_ref[at], s_ref[at], w_ref[at])
    g_out[at] = grad
    st_out[at] = step
    m_out[at] = mean
    s_out[at] = square


def adam_ff_kernel(meta, *refs):
    pieces, proj, fc, proj_out, fc_out = refs[:-14], refs[-14:-11], refs[-11:-8], refs[-8:-4], refs[-4:]
    which = pl.program_id(0)
    quarter = fc[0].shape[0]
    for j in range(2):
        for k in range(2):
            at = (j, slice(k * quarter, (k + 1) * quarter), slice(None))
            col = 1024 * j + 512 * k
            adam_block(pick(pieces, which, slice(col, col + 512)), *proj, *proj_out, at)
            at = (slice(None), slice(col, col + 512))
            adam_block(pick(pieces, which, slice(2048 + col, 2048 + col + 512)), *fc, *fc_out, at)


def adam_qkv_kernel(meta, *refs):
    pieces, qkv, out, qkv_out, out_out = refs[:-14], refs[-14:-11], refs[-11:-8], refs[-8:-4], refs[-4:]
    c = meta[0]
    which = pl.program_id(0)
    quarter = qkv[0].shape[0]
    hq = quarter // 2
    for j in range(2):
        for slot in range(2):
            for p in range(3):
                col = 1024 * j + 384 * slot + 128 * p
                grad = pick(pieces, which, slice(col, col + 128))
                lanes = pl.ds(pl.multiple_of((p * 4 + (slot ^ c) * 2 + j) * 128, 128), 128)
                adam_block(grad, *qkv, *qkv_out, (slice(None), lanes))
        for k in range(2):
            col = 1024 * j + 768
            grad = pick(pieces, which, slice(col, col + 256), slice(k * hq, (k + 1) * hq))
            adam_block(grad, *out, *out_out, (j, slice(None), slice(256 * k, 256 * k + 256)))


def adam_call(kernel, meta, start, pieces, first, second, first_spec, second_spec, name, before=()):
    outs = [jax.ShapeDtypeStruct(first[0].shape, f32)] * 4 + [jax.ShapeDtypeStruct(second[0].shape, f32)] * 4
    specs = [
        pl.BlockSpec(shape, functools.partial(lambda at, i, m: at((start + i) ^ m[1]), at))
        for shape, at in (first_spec, second_spec)
    ]
    count = len(before)

    def run(meta_ref, *refs):
        kernel(meta_ref, *refs[count:])

    grid_spec = pltpu.PrefetchScalarGridSpec(
        num_scalar_prefetch=1,
        grid=(len(pieces),),
        in_specs=[
            *[pl.BlockSpec(memory_space=pl.ANY)] * count,
            *[full_spec(a.shape) for a in pieces],
            *[specs[0]] * 3,
            *[specs[1]] * 3,
        ],
        out_specs=[*[specs[0]] * 4, *[specs[1]] * 4],
    )
    size = (first[0].size + second[0].size) * len(pieces) // 4
    return pl.pallas_call(
        run,
        grid_spec=grid_spec,
        out_shape=outs,
        input_output_aliases={1 + k: k for k in range(count)},
        compiler_params=pltpu.CompilerParams(vmem_limit_bytes=56 << 20),
        cost_estimate=cost(20 * size, 28 * size),
        name=name,
    )(meta, *before, *pieces, *first, *second)


def body(
    tokens,
    out_grad,
    vectors,
    qkv_weight,
    qkv_bias,
    out_weight,
    fc_weight,
    fc_bias,
    proj_weight,
    mean_vectors,
    mean_qkv_weight,
    mean_qkv_bias,
    mean_out_weight,
    mean_fc_weight,
    mean_fc_bias,
    mean_proj_weight,
    square_vectors,
    square_qkv_weight,
    square_qkv_bias,
    square_out_weight,
    square_fc_weight,
    square_fc_bias,
    square_proj_weight,
):
    reps = lax.axis_size("rep")
    c = lax.axis_index("opt")
    place = lax.axis_index("rep")
    low, high = place & 1, (place >> 1) & 1
    slot = lax.iota(jnp.int32, 4)
    ranks = jnp.where((slot == 1) == (c == 0), 2 * low + high, 2 * high + low)
    meta = jnp.where(slot == 0, c, jnp.where(slot == 3, (place >> 2) & 1, ranks)).astype(jnp.int32)
    trig = jnp.asarray(trig_tables())

    packed = jnp.concatenate(
        [vectors.reshape(12, 128), qkv_bias.reshape(6, 128), fc_bias.reshape(8, 128)], 0
    )
    small = lax.all_gather(packed, "opt", axis=0, tiled=True).astype(f32).reshape(2 * SMALL_ROWS, 1, 128)
    fc_far = swap(fc_weight)
    proj_far = swap(proj_weight)
    qkv_far = swap(qkv_weight)
    out_far = swap(out_weight)

    first, second = norm_call(tokens, small)
    send, act, hg, fb = ff_call(
        meta, second, out_grad, fc_weight, fc_far, proj_weight, proj_far, small
    )
    ff_got = swap(send)
    own = ff_own_call(tie(meta, send), second, out_grad, act, hg)
    att = {}
    bits = rest_bits(reps)

    def attend(j, rel, *wait):
        out_w = out_far if rel else out_weight
        before = att[j, 1][:2] if rel == 0 else ()
        att[j, rel] = attention_call(
            j, rel, tie(meta, *wait), first, out_grad, qkv_weight, qkv_far, out_w, small, trig, before
        )
        return att[j, rel][4]

    def rest(total, start, name):
        for bit in bits[start:]:
            (total,) = sum_call([total, exchange(total, reps, bit, bit)], 1, name)
        return total

    keep, send = sum_call([own, ff_got], 2, "ff_pair")
    got = exchange(send, reps, 1, 2)
    mark = attend(0, 1, keep)
    keep, send = sum_call([tie(keep, mark), got], 2, "ff_sum0")
    got = exchange(send, reps, 2, 1)
    mark = attend(0, 0, keep)
    whole = keep.shape
    half = (1, whole[1] // 2, whole[2])
    keep, send = half_call(half_kernel, meta, [tie(keep, mark), got], [half] * 2, "ff_sum1")
    got = exchange(send, reps, bits[0], bits[0])
    own, others = [att[0, 0][0]], [swap(att[0, 0][1])]
    mark = attend(1, 1, keep)
    (piece,) = sum_call([tie(keep, mark), got], 1, "ff_sum2")
    ff_got = exchange(piece, reps, bits[1], bits[1])
    mark = attend(1, 0, piece, others[0])

    (piece,) = sum_call([tie(piece, mark), ff_got], 1, "ff_sum3")
    piece = rest(piece, 2, "ff_sum4")
    ff_got = exchange(piece, reps, bits[0], bits[0])
    own.append(att[1, 0][0])
    others.append(swap(tie(att[1, 0][1], piece)))
    chunks = pair_call(own, others, "att_pair")
    got = crosses(chunks[1:], reps)

    keys = [(0, 0), (0, 1), (1, 0), (1, 1)]
    give = lambda part, before, *wait: output_call(
        part,
        PARTS,
        tie(meta, *wait),
        tokens,
        out_grad,
        act,
        hg,
        [att[k][3] for k in keys],
        [att[k][2] for k in keys],
        (out_weight, out_far),
        (proj_weight, proj_far),
        (fc_weight, fc_far),
        (qkv_weight, qkv_far),
        small,
        [att[k][4] for k in keys],
        fb,
        before,
    )
    done = give(0, None, piece, chunks[0])
    (att_total,) = sum_call([tie(chunks[0], done[2]), *got], 1, "att_sum0")
    got = exchange(att_total, reps, bits[0], bits[0])
    (ff_total,) = half_call(join_kernel, meta, [tie(piece, att_total), ff_got], [whole], "ff_join")
    ff_pieces = [ff_total, exchange(ff_total, reps, 2, 1), exchange(ff_total, reps, 1, 2)]
    layer_out, tokens_grad, small_own, small_send = give(1, done, att_total, ff_total)

    (att_total,) = sum_call([tie(att_total, small_own, *ff_pieces[1:]), got], 1, "att_sum1")
    got = exchange(att_total, reps, bits[1], bits[1])
    ff_pieces.append(exchange(tie(ff_pieces[2], att_total), reps, 2, 1))
    (total,) = sum_call([tie(small_own, att_total), swap(small_send)], 1, "small_pair")
    small_got = exchange(total, reps, 1, 1)

    view = lambda a: a.reshape(2, 512, 512)
    adam_ff = lambda start, pieces, before, *wait: adam_call(
        adam_ff_kernel,
        tie(meta, *wait),
        start,
        pieces,
        [view(a) for a in (mean_proj_weight, square_proj_weight, proj_weight)],
        [mean_fc_weight, square_fc_weight, fc_weight],
        ((2, 128, 512), lambda q: (0, q, 0)),
        ((64, 2048), lambda q: (q, 0)),
        f"adam_ff_{start}",
        before,
    )
    a_ff = adam_ff(0, ff_pieces[:3], (), total, att_total)
    (total,) = sum_call([tie(total, a_ff[4]), small_got], 1, "small_sum")
    small_got = exchange(total, reps, 2, 2)
    (att_total,) = sum_call([tie(att_total, total), got], 1, "att_sum2")
    att_total = rest(att_total, 2, "att_sum3")
    att_pieces = [att_total, *crosses([att_total] * 3, reps)]
    a_ff = adam_ff(3, ff_pieces[3:], a_ff, att_total)
    (total,) = sum_call([tie(total, a_ff[4]), small_got], 1, "small_sum")
    (total,) = sum_call([total, exchange(total, reps, bits[0], bits[0])], 1, "small_sum")
    mark = tie(total, *att_pieces[1:])
    small_got = exchange(mark, reps, bits[1], bits[1])

    view_o = lambda a: a.reshape(2, 128, 512)
    qkv_adam = adam_call(
        adam_qkv_kernel,
        tie(meta, mark),
        0,
        att_pieces,
        [mean_qkv_weight, square_qkv_weight, qkv_weight],
        [view_o(a) for a in (mean_out_weight, square_out_weight, out_weight)],
        ((64, 1536), lambda q: (q, 0)),
        ((2, 32, 512), lambda q: (0, q, 0)),
        "adam_qkv",
    )
    a_proj = [a.reshape(1024, 512) for a in a_ff[:4]]
    a_fc = a_ff[4:]
    a_qkv = qkv_adam[:4]
    a_out = [a.reshape(256, 512) for a in qkv_adam[4:]]
    (total,) = sum_call([tie(mark, a_out[0]), small_got], 1, "small_sum")
    total = rest(total, 2, "small_sum")
    flat = total.reshape(32, 128)
    g_vec = flat[:12].reshape(6, 256)
    g_qb = flat[12:18].reshape(768)
    g_fb = flat[18:26].reshape(1024)

    a_vec = (g_vec, *adamw(g_vec, mean_vectors, square_vectors, vectors))
    a_qb = (g_qb, *adamw(g_qb, mean_qkv_bias, square_qkv_bias, qkv_bias))
    a_fb = (g_fb, *adamw(g_fb, mean_fc_bias, square_fc_bias, fc_bias))
    order = (a_vec, a_qkv, a_qb, a_out, a_fc, a_fb, a_proj)
    return (layer_out, tokens_grad, *[a[k] for k in range(4) for a in order])


def solution(mesh):
    rows = P(("rep", "opt"), None)
    weights = (P(None, "opt"), P("opt", None), P("opt"), P("opt", None), P("opt", None), P("opt"), P("opt", None))
    in_specs = (rows, rows, *weights, *weights, *weights)
    out_specs = (rows, rows, *weights, *weights, *weights, *weights)
    return jax.shard_map(body, mesh=mesh, in_specs=in_specs, out_specs=out_specs, check_vma=False)
```

```python
import functools

import jax
import jax.numpy as jnp
import numpy as np
from jax import lax
from jax.experimental import pallas as pl
from jax.experimental.pallas import tpu as pltpu
from jax.sharding import PartitionSpec as P

H = 8
ROT = 16
LEN = 512
ADAM_STEP = 10

LN_EPS = 1e-05
ADAM_EPS = 1e-08
BETA_ONE = 0.9
BETA_TWO = 0.95
LEARN_RATE = 0.02
WEIGHT_DECAY = 0.01
FIX_ONE = 1.0 - BETA_ONE**ADAM_STEP
FIX_TWO = 1.0 - BETA_TWO**ADAM_STEP
INV_ROOT_TWO = 0.7071067811865476
INV_ROOT_TWO_PI = 0.3989422804014327

bf16 = jnp.bfloat16
f32 = jnp.float32
PARTS = 2
SMALL_ROWS = 26


def dot_nn(a, b):
    return lax.dot_general(a, b, (((1,), (0,)), ((), ())), preferred_element_type=f32)


def dot_nt(a, b):
    return lax.dot_general(a, b, (((1,), (1,)), ((), ())), preferred_element_type=f32)


def dot_tn(a, b):
    return lax.dot_general(a, b, (((0,), (0,)), ((), ())), preferred_element_type=f32)


def full_spec(shape):
    zeros = (0,) * len(shape)
    return pl.BlockSpec(shape, lambda *_: zeros)


def cost(flops, moved, transcendentals=0):
    return pl.CostEstimate(
        flops=int(flops), bytes_accessed=int(moved), transcendentals=int(transcendentals)
    )


def vec_row(small_ref, i):
    n = SMALL_ROWS
    rows = [small_ref[o * n + 2 * i + k] for o in range(2) for k in range(2)]
    return jnp.concatenate(rows, 1)


def normalise(x):
    centre = x - jnp.mean(x, -1, keepdims=True)
    inv_dev = lax.rsqrt(jnp.mean(centre * centre, -1, keepdims=True) + LN_EPS)
    return centre * inv_dev, inv_dev


def norm_kernel(tok_ref, small_ref, first_ref, second_ref):
    normed, _ = normalise(tok_ref[...].astype(f32))
    first_ref[...] = (normed * vec_row(small_ref, 0) + vec_row(small_ref, 1)).astype(bf16)
    second_ref[...] = (normed * vec_row(small_ref, 2) + vec_row(small_ref, 3)).astype(bf16)


def norm_call(tokens, small):
    rows, width = tokens.shape
    tile = 512
    spec = pl.BlockSpec((tile, width), lambda i: (i, 0))
    out = jax.ShapeDtypeStruct((rows, width), bf16)
    return pl.pallas_call(
        norm_kernel,
        grid=(rows // tile,),
        in_specs=[spec, full_spec(small.shape)],
        out_specs=[spec, spec],
        out_shape=[out, out],
        cost_estimate=cost(20 * rows * width, 6 * rows * width),
        name="norm",
        compiler_params=pltpu.CompilerParams(vmem_limit_bytes=12 << 20),
    )(tokens, small)


def ff_kernel(meta, second_ref, grad_ref, fco_ref, fcx_ref, pro_ref, prx_ref, small_ref,
              send_ref, act_ref, hg_ref, bias_ref, fc_ref):
    j = pl.program_id(0)
    rel = pl.program_id(1)
    c = meta[0]
    far_rank = meta[2]
    o = rel ^ c
    rows, width = second_ref.shape
    half = width // 2
    cols = act_ref.shape[1]
    quarter = half // 4
    proj = jnp.where(rel == 0, pro_ref[...], prx_ref[...])
    own_lanes = pl.ds(pl.multiple_of(c * half, half), half)
    far_lanes = pl.ds(pl.multiple_of((1 - c) * half, half), half)
    fc_ref[own_lanes, :] = fco_ref[...]
    fc_ref[far_lanes, :] = fcx_ref[...]
    fc = fc_ref[...]
    base = o * SMALL_ROWS + 18 + 4 * j
    bias = jnp.concatenate([small_ref[base + k] for k in range(cols // 128)], 1)
    sub, parts = 256, 4
    tile = sub * parts

    def block(i, total):
        at = [pl.ds(pl.multiple_of(i * tile + k * sub, sub), sub) for k in range(parts)]
        products = [(dot_nn(second_ref[r, :], fc), dot_nt(grad_ref[r, :], proj)) for r in at]
        for r, (product, act_grad) in zip(at, products):
            hidden = product + bias
            phi_cap = 0.5 + 0.5 * lax.erf(hidden * INV_ROOT_TWO)
            slope = phi_cap + hidden * (jnp.exp(-0.5 * hidden * hidden) * INV_ROOT_TWO_PI)
            act_ref[r, :] = (hidden * phi_cap).astype(bf16)
            hg = (act_grad * slope).astype(bf16)
            hg_ref[r, :] = hg
            total += jnp.sum(hg.astype(f32).reshape(sub // 8, 8, cols), 0)
        return total

    total = lax.fori_loop(0, rows // tile, block, jnp.zeros((8, cols), f32))
    bias_ref[...] = jnp.sum(total, 0, keepdims=True)[None]
    pl.when(rel == 1)(lambda: put_proj(send_ref, dot_tn(act_ref[...], grad_ref[...]), j, far_rank))
    put_fc(send_ref, dot_tn(second_ref[:, far_lanes], hg_ref[...]), o, j, far_rank)


def put_proj(ref, grad, j, rank):
    quarter = ref.shape[1]
    lanes = pl.ds(pl.multiple_of(j * 1024, 1024), 1024)
    for a in range(4):
        piece = grad[a * 2 * quarter : (a + 1) * 2 * quarter]
        ref[a ^ rank, :, lanes] = jnp.concatenate([piece[:quarter], piece[quarter:]], 1).astype(bf16)


def put_fc(ref, grad, o, j, rank):
    quarter = ref.shape[1]
    cols = grad.shape[1]
    lanes = pl.ds(pl.multiple_of(2048 + o * 1024 + j * cols, cols), cols)
    for a in range(4):
        ref[a ^ rank, :, lanes] = grad[a * quarter : (a + 1) * quarter].astype(bf16)


def ff_own_kernel(meta, second_ref, grad_ref, act_ref, hg_ref, own_ref):
    j = pl.program_id(0)
    rel = pl.program_id(1)
    c = meta[0]
    rank = meta[1]
    half = second_ref.shape[1] // 2
    own_lanes = pl.ds(pl.multiple_of(c * half, half), half)
    pl.when(rel == 0)(lambda: put_proj(own_ref, dot_tn(act_ref[...], grad_ref[...]), j, rank))
    put_fc(own_ref, dot_tn(second_ref[:, own_lanes], hg_ref[...]), rel ^ c, j, rank)


def ff_call(meta, second, grad, fc_own, fc_far, proj_own, proj_far, small):
    rows, width = second.shape
    ff = fc_own.shape[1]
    half = width // 2
    cols = ff // 4
    buf = (4, half // 4, 2 * ff)
    fc_spec = pl.BlockSpec((half, cols), lambda j, r, m: (0, (r ^ m[0]) * 2 + j))
    proj_spec = pl.BlockSpec((cols, width), lambda j, r, m: (j, 0))
    act_spec = pl.BlockSpec((rows, cols), lambda j, r, m: (0, 2 * j + r))
    grid_spec = pltpu.PrefetchScalarGridSpec(
        num_scalar_prefetch=1,
        grid=(2, 2),
        in_specs=[
            full_spec((rows, width)),
            full_spec((rows, width)),
            fc_spec,
            fc_spec,
            proj_spec,
            proj_spec,
            full_spec(small.shape),
        ],
        out_specs=[
            full_spec(buf),
            act_spec,
            act_spec,
            pl.BlockSpec((1, 1, cols), lambda j, r, m: (2 * j + r, 0, 0)),
        ],
        scratch_shapes=[pltpu.VMEM((width, cols), bf16)],
    )
    return pl.pallas_call(
        ff_kernel,
        grid_spec=grid_spec,
        out_shape=[
            jax.ShapeDtypeStruct(buf, bf16),
            jax.ShapeDtypeStruct((rows, ff), bf16),
            jax.ShapeDtypeStruct((rows, ff), bf16),
            jax.ShapeDtypeStruct((4, 1, cols), f32),
        ],
        cost_estimate=cost(6 * rows * width * ff, 4 * rows * width + 4 * rows * ff),
        name="feed_forward",
        compiler_params=pltpu.CompilerParams(vmem_limit_bytes=40 << 20),
    )(meta, second, grad, fc_own, fc_far, proj_own, proj_far, small)


def ff_own_call(meta, second, grad, act, hg):
    rows, width = second.shape
    ff = act.shape[1]
    cols = ff // 4
    buf = (4, width // 8, 2 * ff)
    grid_spec = pltpu.PrefetchScalarGridSpec(
        num_scalar_prefetch=1,
        grid=(2, 2),
        in_specs=[
            full_spec((rows, width)),
            full_spec((rows, width)),
            pl.BlockSpec((rows, cols), lambda j, r, m: (0, 2 * j)),
            pl.BlockSpec((rows, cols), lambda j, r, m: (0, 2 * j + r)),
        ],
        out_specs=full_spec(buf),
    )
    return pl.pallas_call(
        ff_own_kernel,
        grid_spec=grid_spec,
        out_shape=jax.ShapeDtypeStruct(buf, bf16),
        cost_estimate=cost(2 * rows * width * ff, 4 * rows * width + 3 * rows * ff),
        name="feed_forward_own",
        compiler_params=pltpu.CompilerParams(vmem_limit_bytes=44 << 20),
    )(meta, second, grad, act, hg)


def rotate_rows(x, cosine, sine):
    parts = []
    for h in range(2):
        low, high = x[64 * h : 64 * h + 8], x[64 * h + 8 : 64 * h + 16]
        parts += [low * cosine - high * sine, high * cosine + low * sine, x[64 * h + 16 : 64 * h + 64]]
    return jnp.concatenate(parts, 0)


def attention_kernel(j, rel, meta, first_ref, grad_ref, wq_ref, wk_ref, wv_ref, xq_ref, xk_ref, xv_ref,
                     ow_ref, small_ref, trig_ref, *refs):
    if rel == 0:
        own_first_ref, send_first_ref, refs = refs[0], refs[1], refs[2:]
    own_ref, send_ref, qg_ref, att_ref, bias_ref, wt_ref, bcol_ref, qgs_ref, attt_ref, btot_ref = refs
    s = pl.program_id(0)
    c = meta[0]
    rank, far_rank = meta[1], meta[2]
    o = rel ^ c
    rows, width = first_ref.shape
    half = width // 2
    quarter = half // 4
    own_lanes = pl.ds(pl.multiple_of(c * half, half), half)
    far_lanes = pl.ds(pl.multiple_of((1 - c) * half, half), half)

    @pl.when(s == 0)
    def _():
        for p, (own, far) in enumerate(((wq_ref, xq_ref), (wk_ref, xk_ref), (wv_ref, xv_ref))):
            wt_ref[128 * p : 128 * (p + 1), own_lanes] = own[...].T
            wt_ref[128 * p : 128 * (p + 1), far_lanes] = far[...].T
            row = p * 4 + o * 2 + j
            owner = row // 6
            bias = small_ref[owner * SMALL_ROWS + 12 + row - 6 * owner]
            bcol_ref[128 * p : 128 * (p + 1), :] = jnp.broadcast_to(bias, (128, 128)).T
        btot_ref[...] = jnp.zeros_like(btot_ref)

    seq = pl.ds(pl.multiple_of(s * LEN, LEN), LEN)
    first = first_ref[seq, :]
    grad = grad_ref[seq, :]
    mixed = dot_nt(wt_ref[...], first) + bcol_ref[:, :1]
    da_t = dot_nt(ow_ref[...], grad).astype(bf16)
    cosine, sine = trig_ref[0], trig_ref[1]
    q_t = rotate_rows(mixed[:128], cosine, sine).astype(bf16) * jnp.asarray(0.125, bf16)
    k_t = rotate_rows(mixed[128:256], cosine, sine).astype(bf16)
    v_t = mixed[256:].astype(bf16)
    k_tok = k_t.T
    v_tok = v_t.T
    hl = LEN // 2
    row_id = lax.broadcasted_iota(jnp.int32, (hl, hl), 0)
    col_id = lax.broadcasted_iota(jnp.int32, (hl, hl), 1)
    keep = row_id <= col_id
    zeros = jnp.zeros((64, LEN), bf16)
    def pad(u, h):
        return jnp.concatenate([u, zeros], 0) if h == 0 else jnp.concatenate([zeros, u], 0)

    def open_chunk(h, t):
        hs, ts, n = slice(64 * h, 64 * h + 64), slice(hl * t, hl * t + hl), hl * (t + 1)
        return dot_nn(k_tok[:n], pad(q_t[hs], h)[:, ts]), dot_nn(v_tok[:n], pad(da_t[hs], h)[:, ts])

    def close_chunk(h, t, score, pg):
        hs, ts, n = slice(64 * h, 64 * h + 64), slice(hl * t, hl * t + hl), hl * (t + 1)
        qh, kh, vh, dah = q_t[hs], k_t[hs], v_t[hs], da_t[hs]
        diag = jnp.where(keep, score[n - hl :], -1e30)
        score = diag if t == 0 else jnp.concatenate([score[:hl], diag], 0)
        exps = jnp.exp(score - jnp.max(score, 0, keepdims=True))
        prob = exps * (1.0 / jnp.sum(exps, 0, keepdims=True))
        prob_b = prob.astype(bf16)
        sg = (prob * (pg - jnp.sum(pg * prob, 0, keepdims=True))).astype(bf16)
        return (
            dot_nn(vh[:, :n], prob_b),
            dot_nn(kh[:, :n], sg),
            dot_nt(dah[:, ts], prob_b),
            dot_nt(qh[:, ts], sg),
        )

    chunks = [(h, t) for h in range(2) for t in range(2)]
    ahead = 4
    opened = [open_chunk(*k) for k in chunks[:ahead]]
    closed = {}
    for i, k in enumerate(chunks):
        if i + ahead < len(chunks):
            opened.append(open_chunk(*chunks[i + ahead]))
        closed[k] = close_chunk(*k, *opened[i])
    att, dq, dk, dv = [], [], [], []
    for h in range(2):
        (a0, q0, v0, k0), (a1, q1, v1, k1) = closed[h, 0], closed[h, 1]
        att.append(jnp.concatenate([a0, a1], 1))
        dq.append(jnp.concatenate([q0, q1], 1) * 0.125)
        dk.append(jnp.concatenate([k0 + k1[:, :hl], k1[:, hl:]], 1))
        dv.append(jnp.concatenate([v0 + v1[:, :hl], v1[:, hl:]], 1))
    att_t = jnp.concatenate(att, 0).astype(bf16)
    dq_t = rotate_rows(jnp.concatenate(dq, 0), cosine, -sine)
    dk_t = rotate_rows(jnp.concatenate(dk, 0), cosine, -sine)
    qkv_t = jnp.concatenate([dq_t, dk_t, jnp.concatenate(dv, 0)], 0).astype(bf16)
    qkv_g = qkv_t.T
    qg_ref[...] = qkv_g
    qgs_ref[seq, :] = qkv_g
    att_ref[...] = att_t.T
    attt_ref[:, seq] = att_t
    btot_ref[...] += jnp.sum(qkv_g.astype(f32).reshape(LEN // 8, 8, 384), 0)

    @pl.when(s == pl.num_programs(0) - 1)
    def _():
        bias_ref[...] = jnp.sum(btot_ref[...], 0, keepdims=True)
        at_own, at_send = (0, 384) if rel == 0 else (0, 0)
        if rel == 0:
            own_ref[:, :, 384:768] = own_first_ref[...]
            send_ref[:, :, :384] = send_first_ref[:, :, :384]
            send_ref[:, :, 768:] = send_first_ref[:, :, 384:]
        for ref, side, number, at in ((own_ref, own_lanes, rank, at_own), (send_ref, far_lanes, far_rank, at_send)):
            gw = dot_tn(first_ref[:, side], qgs_ref[...])
            for a in range(4):
                ref[a ^ number, :, at : at + 384] = gw[a * quarter : (a + 1) * quarter].astype(bf16)
        go = dot_nn(attt_ref[...], grad_ref[...])
        hq = quarter // 2
        for a in range(4):
            piece = go[a * hq : (a + 1) * hq]
            piece = jnp.concatenate([piece[:, :256], piece[:, 256:]], 0).astype(bf16)
            if rel == 0:
                own_ref[a ^ rank, :, 768:] = piece
            else:
                send_ref[a ^ far_rank, :, 384:] = piece


def trig_tables():
    freqs = np.power(np.float32(10000.0), -np.arange(0, ROT, 2).astype(np.float32) / np.float32(ROT))
    angles = (np.arange(LEN).astype(np.float32)[None, :] * freqs[:, None]).astype(np.float32)
    return np.stack([np.cos(angles), np.sin(angles)]).astype(np.float32)


def attention_call(j, rel, meta, first, grad, qkv_own, qkv_far, out_w, small, trig, before=()):
    rows, width = first.shape
    half = width // 2
    bufs = [(4, half // 4, w) for w in ((1024, 1024) if rel == 0 else (384, 640))]
    w_specs = [
        pl.BlockSpec((half, 128), functools.partial(lambda p, s, m: (0, p * 4 + (rel ^ m[0]) * 2 + j), p))
        for p in range(3)
    ]
    grid_spec = pltpu.PrefetchScalarGridSpec(
        num_scalar_prefetch=1,
        grid=(rows // LEN,),
        in_specs=[
            full_spec((rows, width)),
            full_spec((rows, width)),
            *w_specs,
            *w_specs,
            pl.BlockSpec((128, width), lambda s, m: (j, 0)),
            full_spec(small.shape),
            full_spec(trig.shape),
            *[full_spec(a.shape) for a in before],
        ],
        out_specs=[
            *[full_spec(b) for b in bufs],
            pl.BlockSpec((LEN, 384), lambda s, m: (s, 0)),
            pl.BlockSpec((LEN, 128), lambda s, m: (s, 0)),
            full_spec((1, 384)),
        ],
        scratch_shapes=[
            pltpu.VMEM((384, width), bf16),
            pltpu.VMEM((384, 128), f32),
            pltpu.VMEM((rows, 384), bf16),
            pltpu.VMEM((128, rows), bf16),
            pltpu.VMEM((8, 384), f32),
        ],
    )
    flops = 2 * rows * width * (2 * 384 + 2 * 128) + 2 * 6 * 2 * rows * LEN * 128
    return pl.pallas_call(
        functools.partial(attention_kernel, j, rel),
        grid_spec=grid_spec,
        out_shape=[
            *[jax.ShapeDtypeStruct(b, bf16) for b in bufs],
            jax.ShapeDtypeStruct((rows, 384), bf16),
            jax.ShapeDtypeStruct((rows, 128), bf16),
            jax.ShapeDtypeStruct((1, 384), f32),
        ],
        cost_estimate=cost(flops, 4 * rows * width + 2 * rows * 512),
        name=f"attention_{j}{rel}",
        compiler_params=pltpu.CompilerParams(vmem_limit_bytes=18 << 20),
    )(meta, first, grad, *[qkv_own] * 3, *[qkv_far] * 3, out_w, small, trig, *before)


def output_kernel(part, parts, meta, tok_ref, grad_ref, act_ref, hg_ref, *refs):
    at_refs, qg_refs, refs = refs[0:4], refs[4:8], refs[8:]
    oo_ref, ox_ref, po_ref, px_ref, fo_ref, fx_ref, wo_ref, wx_ref, small_ref = refs[:9]
    qb_refs, fb_ref, refs = refs[9:13], refs[13], refs[14:]
    if part > 0:
        before_ref, refs = refs[0], refs[3:]
    lay_ref, tg_ref, refs = refs[0], refs[1], refs[2:]
    if part < parts - 1:
        tot_ref, wgo_ref, wgx_ref, sg_ref, fg_ref = refs
    else:
        own_ref, send_ref, wgo_ref, wgx_ref, sg_ref, fg_ref, tot_ref, qb_ref = refs
    i = pl.program_id(0)
    c = meta[0]
    tile, width = tok_ref.shape
    half = width // 2
    own_lanes = pl.ds(pl.multiple_of(c * half, half), half)
    far_lanes = pl.ds(pl.multiple_of((1 - c) * half, half), half)

    @pl.when(i == 0)
    def _():
        for w_ref, g_ref in ((wo_ref, wgo_ref), (wx_ref, wgx_ref)):
            for j in range(2):
                for rel in range(2):
                    for p in range(3):
                        src = pl.ds(pl.multiple_of((p * 4 + (rel ^ c) * 2 + j) * 128, 128), 128)
                        dst = (j * 6 + rel * 3 + p) * 128
                        g_ref[:, dst : dst + 128] = w_ref[:, src]
        tot_ref[...] = jnp.zeros_like(tot_ref) if part == 0 else before_ref[...]

    x = tok_ref[...].astype(f32)
    grad = grad_ref[...].astype(f32)
    normed, inv_dev = normalise(x)
    acc = dot_nn(jnp.concatenate([at_refs[0][...], at_refs[2][...]], 1), oo_ref[...])
    acc += dot_nn(jnp.concatenate([at_refs[1][...], at_refs[3][...]], 1), ox_ref[...])
    for j in range(2):
        for rel, p_ref in enumerate((po_ref, px_ref)):
            k = 512 * (2 * j + rel)
            acc += dot_nn(act_ref[:, k : k + 512], p_ref[512 * j : 512 * (j + 1), :])
    lay_ref[...] = (x + acc + (vec_row(small_ref, 4) + vec_row(small_ref, 5))).astype(bf16)

    for f_ref, wg_ref, lanes in ((fo_ref, wgo_ref, own_lanes), (fx_ref, wgx_ref, far_lanes)):
        total = None
        for j in range(2):
            for rel in range(2):
                k = 512 * (2 * j + rel)
                cols = pl.ds(pl.multiple_of((rel ^ c) * 1024 + 512 * j, 512), 512)
                term = dot_nt(hg_ref[:, k : k + 512], f_ref[:, cols])
                total = term if total is None else total + term
        sg_ref[:, lanes] = total
        qg = [jnp.concatenate([qg_refs[2 * j][...], qg_refs[2 * j + 1][...]], 1) for j in range(2)]
        fg_ref[:, lanes] = dot_nt(qg[0], wg_ref[:, :768]) + dot_nt(qg[1], wg_ref[:, 768:])
    second_g = sg_ref[...]
    first_g = fg_ref[...]
    e = first_g * vec_row(small_ref, 0) + second_g * vec_row(small_ref, 2)
    ln = inv_dev * (
        e - jnp.mean(e, -1, keepdims=True) - normed * jnp.mean(e * normed, -1, keepdims=True)
    )
    tg_ref[...] = (grad + ln).astype(bf16)
    for k, term in enumerate((first_g * normed, first_g, second_g * normed, second_g, grad)):
        tot_ref[k] += jnp.sum(term.reshape(tile // 8, 8, width), 0)

    if part < parts - 1:
        return

    @pl.when(i == pl.num_programs(0) - 1)
    def _():
        for j in range(2):
            for rel in range(2):
                for p in range(3):
                    qb_ref[p * 4 + (rel ^ c) * 2 + j] = qb_refs[2 * j + rel][:, 128 * p : 128 * (p + 1)]
        sums = [jnp.sum(tot_ref[k], 0, keepdims=True) for k in range(5)]
        sums.append(sums[4])
        for ref, rel in ((own_ref, 0), (send_ref, 1)):
            owner = rel ^ c
            for k in range(6):
                for part in range(2):
                    low = sums[k][:, 128 * part : 128 * (part + 1)]
                    high = sums[k][:, 256 + 128 * part : 256 + 128 * (part + 1)]
                    ref[2 * k + part] = jnp.where(owner == 0, low, high)
            for k in range(6):
                ref[12 + k] = qb_ref[owner * 6 + k]
            for j in range(2):
                for k in range(4):
                    ref[18 + 4 * j + k] = fb_ref[2 * j + rel][:, 128 * k : 128 * (k + 1)]
            for k in range(SMALL_ROWS, 32):
                ref[k] = jnp.zeros((1, 128), f32)


def output_call(part, parts, meta, tokens, grad, act, hg, atts, qgs, out_w, proj_w, fc_w, qkv_w, small, qbs, fb,
                before=None):
    rows, width = tokens.shape
    tile = 256
    tiles = rows // tile // parts
    blk = lambda n: pl.BlockSpec((tile, n), lambda i, m: (part * tiles + i, 0))
    weights = [*out_w, *proj_w, *fc_w, *qkv_w]
    tail = [small, *qbs, fb]
    sums = (5, 8, width)
    packed = (32, 1, 128)
    last = part == parts - 1
    extra, extra_specs, aliases = [], [], {}
    count = 5 + len(atts) + len(qgs) + len(weights) + len(tail)
    if before is not None:
        extra = [before[2], before[0], before[1]]
        extra_specs = [full_spec(sums), pl.BlockSpec(memory_space=pl.ANY), pl.BlockSpec(memory_space=pl.ANY)]
        aliases = {count + 1: 0, count + 2: 1}
    scratch = [
        pltpu.VMEM(qkv_w[0].shape, bf16),
        pltpu.VMEM(qkv_w[0].shape, bf16),
        pltpu.VMEM((tile, width), f32),
        pltpu.VMEM((tile, width), f32),
    ]
    if last:
        scratch += [pltpu.VMEM(sums, f32), pltpu.VMEM((12, 1, 128), f32)]
    given = [packed, packed] if last else [sums]
    grid_spec = pltpu.PrefetchScalarGridSpec(
        num_scalar_prefetch=1,
        grid=(tiles,),
        in_specs=[
            blk(width),
            blk(width),
            *[blk(a.shape[1]) for a in (act, hg, *atts, *qgs)],
            *[full_spec(w.shape) for w in weights],
            *[full_spec(w.shape) for w in tail],
            *extra_specs,
        ],
        out_specs=[blk(width), blk(width), *[full_spec(g) for g in given]],
        scratch_shapes=scratch,
    )
    return pl.pallas_call(
        functools.partial(output_kernel, part, parts),
        grid_spec=grid_spec,
        out_shape=[
            jax.ShapeDtypeStruct((rows, width), bf16),
            jax.ShapeDtypeStruct((rows, width), bf16),
            *[jax.ShapeDtypeStruct(g, f32) for g in given],
        ],
        input_output_aliases=aliases,
        cost_estimate=cost(
            2 * rows * width * (512 + 2048 * 2 + 1536) // parts, 2 * rows * (4 * 512 + 4 * 2048) // parts
        ),
        name=f"outputs_{part}",
        compiler_params=pltpu.CompilerParams(vmem_limit_bytes=30 << 20),
    )(meta, tokens, grad, act, hg, *atts, *qgs, *weights, *tail, *extra)


def sum_kernel(n_in, *refs):
    ins, outs = refs[:n_in], refs[n_in:]
    for k, out in enumerate(outs):
        rows = out.shape[0]
        for i in range(rows):
            total = ins[0][k * rows + i].astype(f32)
            for term in ins[1:]:
                total += term[k * rows + i].astype(f32)
            out[i] = total.astype(out.dtype)


def sum_call(terms, count, name):
    shape, dtype = terms[0].shape, terms[0].dtype
    moved = len(terms) * terms[0].size * terms[0].dtype.itemsize
    return pl.pallas_call(
        functools.partial(sum_kernel, len(terms)),
        out_shape=[jax.ShapeDtypeStruct((shape[0] // count, *shape[1:]), dtype)] * count,
        compiler_params=pltpu.CompilerParams(vmem_limit_bytes=(moved * 3) // 2 + (4 << 20)),
        cost_estimate=cost(moved, 2 * moved),
        name=name,
    )(*terms)


def pair_kernel(*refs):
    own, got, outs = refs[:2], refs[2:4], refs[4:]
    for j, (mine, other) in enumerate(zip(own, got)):
        w = mine.shape[2]
        for k, out in enumerate(outs):
            total = mine[k].astype(f32) + other[k].astype(f32)
            out[0, :, j * w : (j + 1) * w] = total.astype(bf16)


def pair_call(own, got, name):
    rows, width = own[0].shape[1], 2 * own[0].shape[2]
    return pl.pallas_call(
        pair_kernel,
        out_shape=[jax.ShapeDtypeStruct((1, rows, width), bf16)] * 4,
        compiler_params=pltpu.CompilerParams(vmem_limit_bytes=12 << 20),
        cost_estimate=cost(8 * rows * width, 24 * rows * width),
        name=name,
    )(*own, *got)


def half_kernel(meta, mine_ref, got_ref, keep_ref, send_ref):
    rows = keep_ref.shape[1]
    for out, number in ((keep_ref, meta[3]), (send_ref, 1 - meta[3])):
        at = pl.ds(pl.multiple_of(number * rows, rows), rows)
        out[0] = (mine_ref[0, at, :].astype(f32) + got_ref[0, at, :].astype(f32)).astype(bf16)


def join_kernel(meta, mine_ref, got_ref, out_ref):
    rows = mine_ref.shape[1]
    for piece, number in ((mine_ref, meta[3]), (got_ref, 1 - meta[3])):
        out_ref[0, pl.ds(pl.multiple_of(number * rows, rows), rows), :] = piece[0]


def half_call(kernel, meta, terms, outs, name):
    moved = 2 * sum(a.size for a in terms)
    whole = pl.BlockSpec(memory_space=pltpu.VMEM)
    return pl.pallas_call(
        kernel,
        in_specs=[pl.BlockSpec(memory_space=pltpu.SMEM), whole, whole],
        out_specs=[whole] * len(outs),
        out_shape=[jax.ShapeDtypeStruct(o, bf16) for o in outs],
        compiler_params=pltpu.CompilerParams(vmem_limit_bytes=(moved * 3) // 2 + (4 << 20)),
        cost_estimate=cost(moved, 2 * moved),
        name=name,
    )(meta, *terms)


def exchange(a, reps, far, near):
    pairs = [(2 * i + c, 2 * (i ^ (near if c else far)) + c) for i in range(reps) for c in range(2)]
    return lax.ppermute(a, ("rep", "opt"), pairs)


def swap(a):
    return lax.ppermute(a, "opt", [(0, 1), (1, 0)])


def tie(value, *others):
    return lax.optimization_barrier((value, *others))[0]


def rest_bits(reps):
    return [1 << b for b in range(2, reps.bit_length() - 1)]


def crosses(pieces, reps):
    steps = ((2, 1), (1, 2), (3, 3))
    return [exchange(a, reps, *step) for a, step in zip(pieces, steps)]


def adamw(grad, mean, square, weight):
    new_mean = BETA_ONE * mean + (1.0 - BETA_ONE) * grad
    new_square = BETA_TWO * square + (1.0 - BETA_TWO) * grad * grad
    step = -LEARN_RATE * (
        new_mean * (1.0 / FIX_ONE) / (jnp.sqrt(new_square * (1.0 / FIX_TWO)) + ADAM_EPS)
        + WEIGHT_DECAY * weight.astype(f32)
    )
    return step, new_mean, new_square


def pick(refs, which, cols, rows=slice(None)):
    out = refs[0][0, rows, cols]
    for k in range(1, len(refs)):
        out = jnp.where(which == k, refs[k][0, rows, cols], out)
    return out.astype(f32)


def adam_block(grad, m_ref, s_ref, w_ref, g_out, st_out, m_out, s_out, at):
    step, mean, square = adamw(grad, m_ref[at], s_ref[at], w_ref[at])
    g_out[at] = grad
    st_out[at] = step
    m_out[at] = mean
    s_out[at] = square


def adam_ff_kernel(meta, *refs):
    pieces, proj, fc, proj_out, fc_out = refs[:-14], refs[-14:-11], refs[-11:-8], refs[-8:-4], refs[-4:]
    which = pl.program_id(0)
    n = fc[0].shape[0]
    rows = pl.ds(pl.multiple_of(pl.program_id(1) * n, n), n)
    for j in range(2):
        for k in range(2):
            col = 1024 * j + 512 * k
            at = (j, 0, k, slice(None), slice(None))
            adam_block(pick(pieces, which, slice(col, col + 512), rows), *proj, *proj_out, at)
            at = (slice(None), slice(col, col + 512))
            adam_block(pick(pieces, which, slice(2048 + col, 2048 + col + 512), rows), *fc, *fc_out, at)


def adam_qkv_kernel(meta, *refs):
    pieces, qkv, out, qkv_out, out_out = refs[:-14], refs[-14:-11], refs[-11:-8], refs[-8:-4], refs[-4:]
    c = meta[0]
    which = pl.program_id(0)
    sub = pl.program_id(1)
    n = qkv[0].shape[0]
    h = out[0].shape[1]
    rows = pl.ds(pl.multiple_of(sub * n, n), n)
    for j in range(2):
        for slot in range(2):
            for p in range(3):
                col = 1024 * j + 384 * slot + 128 * p
                grad = pick(pieces, which, slice(col, col + 128), rows)
                lanes = pl.ds(pl.multiple_of((p * 4 + (slot ^ c) * 2 + j) * 128, 128), 128)
                adam_block(grad, *qkv, *qkv_out, (slice(None), lanes))
        for k in range(2):
            col = 1024 * j + 768
            half = pl.ds(pl.multiple_of(k * (pieces[0].shape[1] // 2) + sub * h, h), h)
            grad = pick(pieces, which, slice(col, col + 256), half)
            adam_block(grad, *out, *out_out, (j, slice(None), slice(256 * k, 256 * k + 256)))


def adam_call(kernel, meta, start, pieces, first, second, first_spec, second_spec, subs, name, before=()):
    outs = [jax.ShapeDtypeStruct(first[0].shape, f32)] * 4 + [jax.ShapeDtypeStruct(second[0].shape, f32)] * 4
    specs = [
        pl.BlockSpec(shape, functools.partial(lambda at, i, k, m: at((start + i) ^ m[1], k), at))
        for shape, at in (first_spec, second_spec)
    ]
    count = len(before)

    def run(meta_ref, *refs):
        kernel(meta_ref, *refs[count:])

    grid_spec = pltpu.PrefetchScalarGridSpec(
        num_scalar_prefetch=1,
        grid=(len(pieces), subs),
        in_specs=[
            *[pl.BlockSpec(memory_space=pl.ANY)] * count,
            *[full_spec(a.shape) for a in pieces],
            *[specs[0]] * 3,
            *[specs[1]] * 3,
        ],
        out_specs=[*[specs[0]] * 4, *[specs[1]] * 4],
    )
    size = (first[0].size + second[0].size) * len(pieces) // 4
    return pl.pallas_call(
        run,
        grid_spec=grid_spec,
        out_shape=outs,
        input_output_aliases={1 + k: k for k in range(count)},
        compiler_params=pltpu.CompilerParams(vmem_limit_bytes=56 << 20),
        cost_estimate=cost(20 * size, 28 * size),
        name=name,
    )(meta, *before, *pieces, *first, *second)


def body(
    tokens,
    out_grad,
    vectors,
    qkv_weight,
    qkv_bias,
    out_weight,
    fc_weight,
    fc_bias,
    proj_weight,
    mean_vectors,
    mean_qkv_weight,
    mean_qkv_bias,
    mean_out_weight,
    mean_fc_weight,
    mean_fc_bias,
    mean_proj_weight,
    square_vectors,
    square_qkv_weight,
    square_qkv_bias,
    square_out_weight,
    square_fc_weight,
    square_fc_bias,
    square_proj_weight,
):
    reps = lax.axis_size("rep")
    c = lax.axis_index("opt")
    place = lax.axis_index("rep")
    low, high = place & 1, (place >> 1) & 1
    slot = lax.iota(jnp.int32, 4)
    ranks = jnp.where((slot == 1) == (c == 0), 2 * low + high, 2 * high + low)
    meta = jnp.where(slot == 0, c, jnp.where(slot == 3, (place >> 2) & 1, ranks)).astype(jnp.int32)
    trig = jnp.asarray(trig_tables())

    packed = jnp.concatenate(
        [vectors.reshape(12, 128), qkv_bias.reshape(6, 128), fc_bias.reshape(8, 128)], 0
    )
    small = lax.all_gather(packed, "opt", axis=0, tiled=True).astype(f32).reshape(2 * SMALL_ROWS, 1, 128)
    fc_far = swap(fc_weight)
    proj_far = swap(proj_weight)
    qkv_far = swap(qkv_weight)
    out_far = swap(out_weight)

    first, second = norm_call(tokens, small)
    send, act, hg, fb = ff_call(
        meta, second, out_grad, fc_weight, fc_far, proj_weight, proj_far, small
    )
    ff_got = swap(send)
    own = ff_own_call(tie(meta, send), second, out_grad, act, hg)
    att = {}
    bits = rest_bits(reps)

    def attend(j, rel, *wait):
        out_w = out_far if rel else out_weight
        before = att[j, 1][:2] if rel == 0 else ()
        att[j, rel] = attention_call(
            j, rel, tie(meta, *wait), first, out_grad, qkv_weight, qkv_far, out_w, small, trig, before
        )
        return att[j, rel][4]

    def rest(total, start, name):
        for bit in bits[start:]:
            (total,) = sum_call([total, exchange(total, reps, bit, bit)], 1, name)
        return total

    keep, send = sum_call([own, ff_got], 2, "ff_pair")
    got = exchange(send, reps, 1, 2)
    mark = attend(0, 1, keep)
    keep, send = sum_call([tie(keep, mark), got], 2, "ff_sum0")
    got = exchange(send, reps, 2, 1)
    mark = attend(0, 0, keep)
    whole = keep.shape
    half = (1, whole[1] // 2, whole[2])
    keep, send = half_call(half_kernel, meta, [tie(keep, mark), got], [half] * 2, "ff_sum1")
    got = exchange(send, reps, bits[0], bits[0])
    own, others = [att[0, 0][0]], [swap(att[0, 0][1])]
    mark = attend(1, 1, keep)
    (piece,) = sum_call([tie(keep, mark), got], 1, "ff_sum2")
    ff_got = exchange(piece, reps, bits[1], bits[1])
    mark = attend(1, 0, piece, others[0])

    (piece,) = sum_call([tie(piece, mark), ff_got], 1, "ff_sum3")
    piece = rest(piece, 2, "ff_sum4")
    ff_got = exchange(piece, reps, bits[0], bits[0])
    own.append(att[1, 0][0])
    others.append(swap(tie(att[1, 0][1], piece)))
    chunks = pair_call(own, others, "att_pair")
    got = crosses(chunks[1:], reps)

    keys = [(0, 0), (0, 1), (1, 0), (1, 1)]
    give = lambda part, before, *wait: output_call(
        part,
        PARTS,
        tie(meta, *wait),
        tokens,
        out_grad,
        act,
        hg,
        [att[k][3] for k in keys],
        [att[k][2] for k in keys],
        (out_weight, out_far),
        (proj_weight, proj_far),
        (fc_weight, fc_far),
        (qkv_weight, qkv_far),
        small,
        [att[k][4] for k in keys],
        fb,
        before,
    )
    done = give(0, None, piece, chunks[0])
    (att_total,) = sum_call([tie(chunks[0], done[2]), *got], 1, "att_sum0")
    got = exchange(att_total, reps, bits[0], bits[0])
    (ff_total,) = half_call(join_kernel, meta, [tie(piece, att_total), ff_got], [whole], "ff_join")
    ff_pieces = [ff_total, exchange(ff_total, reps, 2, 1), exchange(ff_total, reps, 1, 2)]
    layer_out, tokens_grad, small_own, small_send = give(1, done, att_total, ff_total)

    (att_total,) = sum_call([tie(att_total, small_own, *ff_pieces[1:]), got], 1, "att_sum1")
    got = exchange(att_total, reps, bits[1], bits[1])
    ff_pieces.append(exchange(tie(ff_pieces[2], att_total), reps, 2, 1))
    (total,) = sum_call([tie(small_own, att_total), swap(small_send)], 1, "small_pair")
    small_got = exchange(total, reps, 1, 1)

    view = lambda a: a.reshape(2, 4, 2, 64, 512)
    adam_ff = lambda start, pieces, before, *wait: adam_call(
        adam_ff_kernel,
        tie(meta, *wait),
        start,
        pieces,
        [view(a) for a in (mean_proj_weight, square_proj_weight, proj_weight)],
        [mean_fc_weight, square_fc_weight, fc_weight],
        ((2, 1, 2, 64, 512), lambda q, k: (0, q, 0, k, 0)),
        ((64, 2048), lambda q, k: (q + k, 0)),
        1,
        f"adam_ff_{start}",
        before,
    )
    view_o = lambda a: a.reshape(2, 128, 512)
    adam_qkv = lambda start, pieces, before, *wait: adam_call(
        adam_qkv_kernel,
        tie(meta, *wait),
        start,
        pieces,
        [mean_qkv_weight, square_qkv_weight, qkv_weight],
        [view_o(a) for a in (mean_out_weight, square_out_weight, out_weight)],
        ((64, 1536), lambda q, k: (q + k, 0)),
        ((2, 32, 512), lambda q, k: (0, q + k, 0)),
        1,
        f"adam_qkv_{start}",
        before,
    )
    a_ff = adam_ff(0, ff_pieces[:3], (), total, att_total)
    (total,) = sum_call([tie(total, a_ff[4]), small_got], 1, "small_sum")
    small_got = exchange(total, reps, 2, 2)
    (att_total,) = sum_call([tie(att_total, total), got], 1, "att_sum2")
    att_total = rest(att_total, 2, "att_sum3")
    att_pieces = [att_total, *crosses([att_total] * 3, reps)]
    a_ff = adam_ff(3, ff_pieces[3:], a_ff, att_total)
    (total,) = sum_call([tie(total, a_ff[4]), small_got], 1, "small_sum")
    small_got = exchange(total, reps, bits[0], bits[0])
    a_qkv = adam_qkv(0, att_pieces[:1], (), total)
    (total,) = sum_call([tie(total, a_qkv[0]), small_got], 1, "small_sum")
    mark = tie(total, *att_pieces[1:])
    small_got = exchange(mark, reps, bits[1], bits[1])

    a_qkv = adam_qkv(1, att_pieces[1:], a_qkv, mark)
    a_proj = [a.reshape(1024, 512) for a in a_ff[:4]]
    a_fc = a_ff[4:]
    a_out = [a.reshape(256, 512) for a in a_qkv[4:]]
    a_qkv = a_qkv[:4]
    (total,) = sum_call([tie(mark, a_out[0]), small_got], 1, "small_sum")
    total = rest(total, 2, "small_sum")
    flat = total.reshape(32, 128)
    g_vec = flat[:12].reshape(6, 256)
    g_qb = flat[12:18].reshape(768)
    g_fb = flat[18:26].reshape(1024)

    a_vec = (g_vec, *adamw(g_vec, mean_vectors, square_vectors, vectors))
    a_qb = (g_qb, *adamw(g_qb, mean_qkv_bias, square_qkv_bias, qkv_bias))
    a_fb = (g_fb, *adamw(g_fb, mean_fc_bias, square_fc_bias, fc_bias))
    order = (a_vec, a_qkv, a_qb, a_out, a_fc, a_fb, a_proj)
    return (layer_out, tokens_grad, *[a[k] for k in range(4) for a in order])


def solution(mesh):
    rows = P(("rep", "opt"), None)
    weights = (P(None, "opt"), P("opt", None), P("opt"), P("opt", None), P("opt", None), P("opt"), P("opt", None))
    in_specs = (rows, rows, *weights, *weights, *weights)
    out_specs = (rows, rows, *weights, *weights, *weights, *weights)
    return jax.shard_map(body, mesh=mesh, in_specs=in_specs, out_specs=out_specs, check_vma=False)
```

```python
import functools

import jax
import jax.numpy as jnp
import numpy as np
from jax import lax
from jax.experimental import pallas as pl
from jax.experimental.pallas import tpu as pltpu
from jax.sharding import PartitionSpec as P

H = 8
ROT = 16
LEN = 512
ADAM_STEP = 10

LN_EPS = 1e-05
ADAM_EPS = 1e-08
BETA_ONE = 0.9
BETA_TWO = 0.95
LEARN_RATE = 0.02
WEIGHT_DECAY = 0.01
FIX_ONE = 1.0 - BETA_ONE**ADAM_STEP
FIX_TWO = 1.0 - BETA_TWO**ADAM_STEP
INV_ROOT_TWO = 0.7071067811865476
INV_ROOT_TWO_PI = 0.3989422804014327

bf16 = jnp.bfloat16
f32 = jnp.float32
PARTS = 2
SMALL_ROWS = 26


def dot_nn(a, b):
    return lax.dot_general(a, b, (((1,), (0,)), ((), ())), preferred_element_type=f32)


def dot_nt(a, b):
    return lax.dot_general(a, b, (((1,), (1,)), ((), ())), preferred_element_type=f32)


def dot_tn(a, b):
    return lax.dot_general(a, b, (((0,), (0,)), ((), ())), preferred_element_type=f32)


def full_spec(shape):
    zeros = (0,) * len(shape)
    return pl.BlockSpec(shape, lambda *_: zeros)


def cost(flops, moved, transcendentals=0):
    return pl.CostEstimate(
        flops=int(flops), bytes_accessed=int(moved), transcendentals=int(transcendentals)
    )


def vec_row(small_ref, i):
    n = SMALL_ROWS
    rows = [small_ref[o * n + 2 * i + k] for o in range(2) for k in range(2)]
    return jnp.concatenate(rows, 1)


def normalise(x):
    centre = x - jnp.mean(x, -1, keepdims=True)
    inv_dev = lax.rsqrt(jnp.mean(centre * centre, -1, keepdims=True) + LN_EPS)
    return centre * inv_dev, inv_dev


def norm_kernel(tok_ref, small_ref, first_ref, second_ref):
    normed, _ = normalise(tok_ref[...].astype(f32))
    first_ref[...] = (normed * vec_row(small_ref, 0) + vec_row(small_ref, 1)).astype(bf16)
    second_ref[...] = (normed * vec_row(small_ref, 2) + vec_row(small_ref, 3)).astype(bf16)


def norm_call(tokens, small):
    rows, width = tokens.shape
    tile = 512
    spec = pl.BlockSpec((tile, width), lambda i: (i, 0))
    out = jax.ShapeDtypeStruct((rows, width), bf16)
    return pl.pallas_call(
        norm_kernel,
        grid=(rows // tile,),
        in_specs=[spec, full_spec(small.shape)],
        out_specs=[spec, spec],
        out_shape=[out, out],
        cost_estimate=cost(20 * rows * width, 6 * rows * width),
        name="norm",
        compiler_params=pltpu.CompilerParams(vmem_limit_bytes=12 << 20),
    )(tokens, small)


def ff_kernel(meta, second_ref, grad_ref, fco_ref, fcx_ref, pro_ref, prx_ref, small_ref,
              send_ref, act_ref, hg_ref, bias_ref, fc_ref):
    j = pl.program_id(0)
    rel = pl.program_id(1)
    c = meta[0]
    far_rank = meta[2]
    o = rel ^ c
    rows, width = second_ref.shape
    half = width // 2
    cols = act_ref.shape[1]
    quarter = half // 4
    proj = jnp.where(rel == 0, pro_ref[...], prx_ref[...])
    own_lanes = pl.ds(pl.multiple_of(c * half, half), half)
    far_lanes = pl.ds(pl.multiple_of((1 - c) * half, half), half)
    fc_ref[own_lanes, :] = fco_ref[...]
    fc_ref[far_lanes, :] = fcx_ref[...]
    fc = fc_ref[...]
    base = o * SMALL_ROWS + 18 + 4 * j
    bias = jnp.concatenate([small_ref[base + k] for k in range(cols // 128)], 1)
    sub, parts = 256, 4
    tile = sub * parts

    def block(i, total):
        at = [pl.ds(pl.multiple_of(i * tile + k * sub, sub), sub) for k in range(parts)]
        products = [(dot_nn(second_ref[r, :], fc), dot_nt(grad_ref[r, :], proj)) for r in at]
        for r, (product, act_grad) in zip(at, products):
            hidden = product + bias
            phi_cap = 0.5 + 0.5 * lax.erf(hidden * INV_ROOT_TWO)
            slope = phi_cap + hidden * (jnp.exp(-0.5 * hidden * hidden) * INV_ROOT_TWO_PI)
            act_ref[r, :] = (hidden * phi_cap).astype(bf16)
            hg = (act_grad * slope).astype(bf16)
            hg_ref[r, :] = hg
            total += jnp.sum(hg.astype(f32).reshape(sub // 8, 8, cols), 0)
        return total

    total = lax.fori_loop(0, rows // tile, block, jnp.zeros((8, cols), f32))
    bias_ref[...] = jnp.sum(total, 0, keepdims=True)[None]
    pl.when(rel == 1)(lambda: put_proj(send_ref, dot_tn(act_ref[...], grad_ref[...]), j, far_rank))
    put_fc(send_ref, dot_tn(second_ref[:, far_lanes], hg_ref[...]), o, j, far_rank)


def put_proj(ref, grad, j, rank):
    quarter = ref.shape[1]
    lanes = pl.ds(pl.multiple_of(j * 1024, 1024), 1024)
    for a in range(4):
        piece = grad[a * 2 * quarter : (a + 1) * 2 * quarter]
        ref[a ^ rank, :, lanes] = jnp.concatenate([piece[:quarter], piece[quarter:]], 1).astype(bf16)


def put_fc(ref, grad, o, j, rank):
    quarter = ref.shape[1]
    cols = grad.shape[1]
    lanes = pl.ds(pl.multiple_of(2048 + o * 1024 + j * cols, cols), cols)
    for a in range(4):
        ref[a ^ rank, :, lanes] = grad[a * quarter : (a + 1) * quarter].astype(bf16)


def ff_own_kernel(meta, second_ref, grad_ref, act_ref, hg_ref, own_ref):
    j = pl.program_id(0)
    rel = pl.program_id(1)
    c = meta[0]
    rank = meta[1]
    half = second_ref.shape[1] // 2
    own_lanes = pl.ds(pl.multiple_of(c * half, half), half)
    pl.when(rel == 0)(lambda: put_proj(own_ref, dot_tn(act_ref[...], grad_ref[...]), j, rank))
    put_fc(own_ref, dot_tn(second_ref[:, own_lanes], hg_ref[...]), rel ^ c, j, rank)


def ff_call(meta, second, grad, fc_own, fc_far, proj_own, proj_far, small):
    rows, width = second.shape
    ff = fc_own.shape[1]
    half = width // 2
    cols = ff // 4
    buf = (4, half // 4, 2 * ff)
    fc_spec = pl.BlockSpec((half, cols), lambda j, r, m: (0, (r ^ m[0]) * 2 + j))
    proj_spec = pl.BlockSpec((cols, width), lambda j, r, m: (j, 0))
    act_spec = pl.BlockSpec((rows, cols), lambda j, r, m: (0, 2 * j + r))
    grid_spec = pltpu.PrefetchScalarGridSpec(
        num_scalar_prefetch=1,
        grid=(2, 2),
        in_specs=[
            full_spec((rows, width)),
            full_spec((rows, width)),
            fc_spec,
            fc_spec,
            proj_spec,
            proj_spec,
            full_spec(small.shape),
        ],
        out_specs=[
            full_spec(buf),
            act_spec,
            act_spec,
            pl.BlockSpec((1, 1, cols), lambda j, r, m: (2 * j + r, 0, 0)),
        ],
        scratch_shapes=[pltpu.VMEM((width, cols), bf16)],
    )
    return pl.pallas_call(
        ff_kernel,
        grid_spec=grid_spec,
        out_shape=[
            jax.ShapeDtypeStruct(buf, bf16),
            jax.ShapeDtypeStruct((rows, ff), bf16),
            jax.ShapeDtypeStruct((rows, ff), bf16),
            jax.ShapeDtypeStruct((4, 1, cols), f32),
        ],
        cost_estimate=cost(6 * rows * width * ff, 4 * rows * width + 4 * rows * ff),
        name="feed_forward",
        compiler_params=pltpu.CompilerParams(vmem_limit_bytes=40 << 20),
    )(meta, second, grad, fc_own, fc_far, proj_own, proj_far, small)


def ff_own_call(meta, second, grad, act, hg):
    rows, width = second.shape
    ff = act.shape[1]
    cols = ff // 4
    buf = (4, width // 8, 2 * ff)
    grid_spec = pltpu.PrefetchScalarGridSpec(
        num_scalar_prefetch=1,
        grid=(2, 2),
        in_specs=[
            full_spec((rows, width)),
            full_spec((rows, width)),
            pl.BlockSpec((rows, cols), lambda j, r, m: (0, 2 * j)),
            pl.BlockSpec((rows, cols), lambda j, r, m: (0, 2 * j + r)),
        ],
        out_specs=full_spec(buf),
    )
    return pl.pallas_call(
        ff_own_kernel,
        grid_spec=grid_spec,
        out_shape=jax.ShapeDtypeStruct(buf, bf16),
        cost_estimate=cost(2 * rows * width * ff, 4 * rows * width + 3 * rows * ff),
        name="feed_forward_own",
        compiler_params=pltpu.CompilerParams(vmem_limit_bytes=44 << 20),
    )(meta, second, grad, act, hg)


def rotate_rows(x, cosine, sine):
    parts = []
    for h in range(2):
        low, high = x[64 * h : 64 * h + 8], x[64 * h + 8 : 64 * h + 16]
        parts += [low * cosine - high * sine, high * cosine + low * sine, x[64 * h + 16 : 64 * h + 64]]
    return jnp.concatenate(parts, 0)


def attention_kernel(j, rel, meta, first_ref, grad_ref, wq_ref, wk_ref, wv_ref, xq_ref, xk_ref, xv_ref,
                     ow_ref, small_ref, trig_ref, *refs):
    if rel == 0:
        own_first_ref, send_first_ref, refs = refs[0], refs[1], refs[2:]
    own_ref, send_ref, qg_ref, att_ref, bias_ref, wt_ref, bcol_ref, qgs_ref, attt_ref, btot_ref = refs
    s = pl.program_id(0)
    c = meta[0]
    rank, far_rank = meta[1], meta[2]
    o = rel ^ c
    rows, width = first_ref.shape
    half = width // 2
    quarter = half // 4
    own_lanes = pl.ds(pl.multiple_of(c * half, half), half)
    far_lanes = pl.ds(pl.multiple_of((1 - c) * half, half), half)

    @pl.when(s == 0)
    def _():
        for p, (own, far) in enumerate(((wq_ref, xq_ref), (wk_ref, xk_ref), (wv_ref, xv_ref))):
            wt_ref[128 * p : 128 * (p + 1), own_lanes] = own[...].T
            wt_ref[128 * p : 128 * (p + 1), far_lanes] = far[...].T
            row = p * 4 + o * 2 + j
            owner = row // 6
            bias = small_ref[owner * SMALL_ROWS + 12 + row - 6 * owner]
            bcol_ref[128 * p : 128 * (p + 1), :] = jnp.broadcast_to(bias, (128, 128)).T
        btot_ref[...] = jnp.zeros_like(btot_ref)

    seq = pl.ds(pl.multiple_of(s * LEN, LEN), LEN)
    first = first_ref[seq, :]
    grad = grad_ref[seq, :]
    mixed = dot_nt(wt_ref[...], first) + bcol_ref[:, :1]
    da_t = dot_nt(ow_ref[...], grad).astype(bf16)
    cosine, sine = trig_ref[0], trig_ref[1]
    q_t = rotate_rows(mixed[:128], cosine, sine).astype(bf16) * jnp.asarray(0.125, bf16)
    k_t = rotate_rows(mixed[128:256], cosine, sine).astype(bf16)
    v_t = mixed[256:].astype(bf16)
    k_tok = k_t.T
    v_tok = v_t.T
    hl = LEN // 2
    row_id = lax.broadcasted_iota(jnp.int32, (hl, hl), 0)
    col_id = lax.broadcasted_iota(jnp.int32, (hl, hl), 1)
    keep = row_id <= col_id
    zeros = jnp.zeros((64, LEN), bf16)
    def pad(u, h):
        return jnp.concatenate([u, zeros], 0) if h == 0 else jnp.concatenate([zeros, u], 0)

    def open_chunk(h, t):
        hs, ts, n = slice(64 * h, 64 * h + 64), slice(hl * t, hl * t + hl), hl * (t + 1)
        return dot_nn(k_tok[:n], pad(q_t[hs], h)[:, ts]), dot_nn(v_tok[:n], pad(da_t[hs], h)[:, ts])

    def close_chunk(h, t, score, pg):
        hs, ts, n = slice(64 * h, 64 * h + 64), slice(hl * t, hl * t + hl), hl * (t + 1)
        qh, kh, vh, dah = q_t[hs], k_t[hs], v_t[hs], da_t[hs]
        diag = jnp.where(keep, score[n - hl :], -1e30)
        score = diag if t == 0 else jnp.concatenate([score[:hl], diag], 0)
        exps = jnp.exp(score - jnp.max(score, 0, keepdims=True))
        prob = exps * (1.0 / jnp.sum(exps, 0, keepdims=True))
        prob_b = prob.astype(bf16)
        sg = (prob * (pg - jnp.sum(pg * prob, 0, keepdims=True))).astype(bf16)
        return (
            dot_nn(vh[:, :n], prob_b),
            dot_nn(kh[:, :n], sg),
            dot_nt(dah[:, ts], prob_b),
            dot_nt(qh[:, ts], sg),
        )

    chunks = [(h, t) for h in range(2) for t in range(2)]
    ahead = 4
    opened = [open_chunk(*k) for k in chunks[:ahead]]
    closed = {}
    for i, k in enumerate(chunks):
        if i + ahead < len(chunks):
            opened.append(open_chunk(*chunks[i + ahead]))
        closed[k] = close_chunk(*k, *opened[i])
    att, dq, dk, dv = [], [], [], []
    for h in range(2):
        (a0, q0, v0, k0), (a1, q1, v1, k1) = closed[h, 0], closed[h, 1]
        att.append(jnp.concatenate([a0, a1], 1))
        dq.append(jnp.concatenate([q0, q1], 1) * 0.125)
        dk.append(jnp.concatenate([k0 + k1[:, :hl], k1[:, hl:]], 1))
        dv.append(jnp.concatenate([v0 + v1[:, :hl], v1[:, hl:]], 1))
    att_t = jnp.concatenate(att, 0).astype(bf16)
    dq_t = rotate_rows(jnp.concatenate(dq, 0), cosine, -sine)
    dk_t = rotate_rows(jnp.concatenate(dk, 0), cosine, -sine)
    qkv_t = jnp.concatenate([dq_t, dk_t, jnp.concatenate(dv, 0)], 0).astype(bf16)
    qkv_g = qkv_t.T
    qg_ref[...] = qkv_g
    qgs_ref[seq, :] = qkv_g
    att_ref[...] = att_t.T
    attt_ref[:, seq] = att_t
    btot_ref[...] += jnp.sum(qkv_g.astype(f32).reshape(LEN // 8, 8, 384), 0)

    @pl.when(s == pl.num_programs(0) - 1)
    def _():
        bias_ref[...] = jnp.sum(btot_ref[...], 0, keepdims=True)
        at_own, at_send = (0, 384) if rel == 0 else (0, 0)
        if rel == 0:
            own_ref[:, :, 384:768] = own_first_ref[...]
            send_ref[:, :, :384] = send_first_ref[:, :, :384]
            send_ref[:, :, 768:] = send_first_ref[:, :, 384:]
        for ref, side, number, at in ((own_ref, own_lanes, rank, at_own), (send_ref, far_lanes, far_rank, at_send)):
            gw = dot_tn(first_ref[:, side], qgs_ref[...])
            for a in range(4):
                ref[a ^ number, :, at : at + 384] = gw[a * quarter : (a + 1) * quarter].astype(bf16)
        go = dot_nn(attt_ref[...], grad_ref[...])
        hq = quarter // 2
        for a in range(4):
            piece = go[a * hq : (a + 1) * hq]
            piece = jnp.concatenate([piece[:, :256], piece[:, 256:]], 0).astype(bf16)
            if rel == 0:
                own_ref[a ^ rank, :, 768:] = piece
            else:
                send_ref[a ^ far_rank, :, 384:] = piece


def trig_tables():
    freqs = np.power(np.float32(10000.0), -np.arange(0, ROT, 2).astype(np.float32) / np.float32(ROT))
    angles = (np.arange(LEN).astype(np.float32)[None, :] * freqs[:, None]).astype(np.float32)
    return np.stack([np.cos(angles), np.sin(angles)]).astype(np.float32)


def attention_call(j, rel, meta, first, grad, qkv_own, qkv_far, out_w, small, trig, before=()):
    rows, width = first.shape
    half = width // 2
    bufs = [(4, half // 4, w) for w in ((1024, 1024) if rel == 0 else (384, 640))]
    w_specs = [
        pl.BlockSpec((half, 128), functools.partial(lambda p, s, m: (0, p * 4 + (rel ^ m[0]) * 2 + j), p))
        for p in range(3)
    ]
    grid_spec = pltpu.PrefetchScalarGridSpec(
        num_scalar_prefetch=1,
        grid=(rows // LEN,),
        in_specs=[
            full_spec((rows, width)),
            full_spec((rows, width)),
            *w_specs,
            *w_specs,
            pl.BlockSpec((128, width), lambda s, m: (j, 0)),
            full_spec(small.shape),
            full_spec(trig.shape),
            *[full_spec(a.shape) for a in before],
        ],
        out_specs=[
            *[full_spec(b) for b in bufs],
            pl.BlockSpec((LEN, 384), lambda s, m: (s, 0)),
            pl.BlockSpec((LEN, 128), lambda s, m: (s, 0)),
            full_spec((1, 384)),
        ],
        scratch_shapes=[
            pltpu.VMEM((384, width), bf16),
            pltpu.VMEM((384, 128), f32),
            pltpu.VMEM((rows, 384), bf16),
            pltpu.VMEM((128, rows), bf16),
            pltpu.VMEM((8, 384), f32),
        ],
    )
    flops = 2 * rows * width * (2 * 384 + 2 * 128) + 2 * 6 * 2 * rows * LEN * 128
    return pl.pallas_call(
        functools.partial(attention_kernel, j, rel),
        grid_spec=grid_spec,
        out_shape=[
            *[jax.ShapeDtypeStruct(b, bf16) for b in bufs],
            jax.ShapeDtypeStruct((rows, 384), bf16),
            jax.ShapeDtypeStruct((rows, 128), bf16),
            jax.ShapeDtypeStruct((1, 384), f32),
        ],
        cost_estimate=cost(flops, 4 * rows * width + 2 * rows * 512),
        name=f"attention_{j}{rel}",
        compiler_params=pltpu.CompilerParams(vmem_limit_bytes=18 << 20),
    )(meta, first, grad, *[qkv_own] * 3, *[qkv_far] * 3, out_w, small, trig, *before)


def output_kernel(part, parts, meta, tok_ref, grad_ref, act_ref, hg_ref, *refs):
    at_refs, qg_refs, refs = refs[0:4], refs[4:8], refs[8:]
    oo_ref, ox_ref, po_ref, px_ref, fo_ref, fx_ref, wo_ref, wx_ref, small_ref = refs[:9]
    qb_refs, fb_ref, refs = refs[9:13], refs[13], refs[14:]
    if part > 0:
        before_ref, refs = refs[0], refs[3:]
    lay_ref, tg_ref, refs = refs[0], refs[1], refs[2:]
    if part < parts - 1:
        tot_ref, wgo_ref, wgx_ref, sg_ref, fg_ref = refs
    else:
        own_ref, send_ref, wgo_ref, wgx_ref, sg_ref, fg_ref, tot_ref, qb_ref = refs
    i = pl.program_id(0)
    c = meta[0]
    tile, width = tok_ref.shape
    half = width // 2
    own_lanes = pl.ds(pl.multiple_of(c * half, half), half)
    far_lanes = pl.ds(pl.multiple_of((1 - c) * half, half), half)

    @pl.when(i == 0)
    def _():
        for w_ref, g_ref in ((wo_ref, wgo_ref), (wx_ref, wgx_ref)):
            for j in range(2):
                for rel in range(2):
                    for p in range(3):
                        src = pl.ds(pl.multiple_of((p * 4 + (rel ^ c) * 2 + j) * 128, 128), 128)
                        dst = (j * 6 + rel * 3 + p) * 128
                        g_ref[:, dst : dst + 128] = w_ref[:, src]
        tot_ref[...] = jnp.zeros_like(tot_ref) if part == 0 else before_ref[...]

    x = tok_ref[...].astype(f32)
    grad = grad_ref[...].astype(f32)
    normed, inv_dev = normalise(x)
    acc = dot_nn(jnp.concatenate([at_refs[0][...], at_refs[2][...]], 1), oo_ref[...])
    acc += dot_nn(jnp.concatenate([at_refs[1][...], at_refs[3][...]], 1), ox_ref[...])
    for j in range(2):
        for rel, p_ref in enumerate((po_ref, px_ref)):
            k = 512 * (2 * j + rel)
            acc += dot_nn(act_ref[:, k : k + 512], p_ref[512 * j : 512 * (j + 1), :])
    lay_ref[...] = (x + acc + (vec_row(small_ref, 4) + vec_row(small_ref, 5))).astype(bf16)

    for f_ref, wg_ref, lanes in ((fo_ref, wgo_ref, own_lanes), (fx_ref, wgx_ref, far_lanes)):
        total = None
        for j in range(2):
            for rel in range(2):
                k = 512 * (2 * j + rel)
                cols = pl.ds(pl.multiple_of((rel ^ c) * 1024 + 512 * j, 512), 512)
                term = dot_nt(hg_ref[:, k : k + 512], f_ref[:, cols])
                total = term if total is None else total + term
        sg_ref[:, lanes] = total
        qg = [jnp.concatenate([qg_refs[2 * j][...], qg_refs[2 * j + 1][...]], 1) for j in range(2)]
        fg_ref[:, lanes] = dot_nt(qg[0], wg_ref[:, :768]) + dot_nt(qg[1], wg_ref[:, 768:])
    second_g = sg_ref[...]
    first_g = fg_ref[...]
    e = first_g * vec_row(small_ref, 0) + second_g * vec_row(small_ref, 2)
    ln = inv_dev * (
        e - jnp.mean(e, -1, keepdims=True) - normed * jnp.mean(e * normed, -1, keepdims=True)
    )
    tg_ref[...] = (grad + ln).astype(bf16)
    for k, term in enumerate((first_g * normed, first_g, second_g * normed, second_g, grad)):
        tot_ref[k] += jnp.sum(term.reshape(tile // 8, 8, width), 0)

    if part < parts - 1:
        return

    @pl.when(i == pl.num_programs(0) - 1)
    def _():
        for j in range(2):
            for rel in range(2):
                for p in range(3):
                    qb_ref[p * 4 + (rel ^ c) * 2 + j] = qb_refs[2 * j + rel][:, 128 * p : 128 * (p + 1)]
        sums = [jnp.sum(tot_ref[k], 0, keepdims=True) for k in range(5)]
        sums.append(sums[4])
        for ref, rel in ((own_ref, 0), (send_ref, 1)):
            owner = rel ^ c
            for k in range(6):
                for part in range(2):
                    low = sums[k][:, 128 * part : 128 * (part + 1)]
                    high = sums[k][:, 256 + 128 * part : 256 + 128 * (part + 1)]
                    ref[2 * k + part] = jnp.where(owner == 0, low, high)
            for k in range(6):
                ref[12 + k] = qb_ref[owner * 6 + k]
            for j in range(2):
                for k in range(4):
                    ref[18 + 4 * j + k] = fb_ref[2 * j + rel][:, 128 * k : 128 * (k + 1)]
            for k in range(SMALL_ROWS, 32):
                ref[k] = jnp.zeros((1, 128), f32)


def output_call(part, parts, meta, tokens, grad, act, hg, atts, qgs, out_w, proj_w, fc_w, qkv_w, small, qbs, fb,
                before=None):
    rows, width = tokens.shape
    tile = 256
    tiles = rows // tile // parts
    blk = lambda n: pl.BlockSpec((tile, n), lambda i, m: (part * tiles + i, 0))
    weights = [*out_w, *proj_w, *fc_w, *qkv_w]
    tail = [small, *qbs, fb]
    sums = (5, 8, width)
    packed = (32, 1, 128)
    last = part == parts - 1
    extra, extra_specs, aliases = [], [], {}
    count = 5 + len(atts) + len(qgs) + len(weights) + len(tail)
    if before is not None:
        extra = [before[2], before[0], before[1]]
        extra_specs = [full_spec(sums), pl.BlockSpec(memory_space=pl.ANY), pl.BlockSpec(memory_space=pl.ANY)]
        aliases = {count + 1: 0, count + 2: 1}
    scratch = [
        pltpu.VMEM(qkv_w[0].shape, bf16),
        pltpu.VMEM(qkv_w[0].shape, bf16),
        pltpu.VMEM((tile, width), f32),
        pltpu.VMEM((tile, width), f32),
    ]
    if last:
        scratch += [pltpu.VMEM(sums, f32), pltpu.VMEM((12, 1, 128), f32)]
    given = [packed, packed] if last else [sums]
    grid_spec = pltpu.PrefetchScalarGridSpec(
        num_scalar_prefetch=1,
        grid=(tiles,),
        in_specs=[
            blk(width),
            blk(width),
            *[blk(a.shape[1]) for a in (act, hg, *atts, *qgs)],
            *[full_spec(w.shape) for w in weights],
            *[full_spec(w.shape) for w in tail],
            *extra_specs,
        ],
        out_specs=[blk(width), blk(width), *[full_spec(g) for g in given]],
        scratch_shapes=scratch,
    )
    return pl.pallas_call(
        functools.partial(output_kernel, part, parts),
        grid_spec=grid_spec,
        out_shape=[
            jax.ShapeDtypeStruct((rows, width), bf16),
            jax.ShapeDtypeStruct((rows, width), bf16),
            *[jax.ShapeDtypeStruct(g, f32) for g in given],
        ],
        input_output_aliases=aliases,
        cost_estimate=cost(
            2 * rows * width * (512 + 2048 * 2 + 1536) // parts, 2 * rows * (4 * 512 + 4 * 2048) // parts
        ),
        name=f"outputs_{part}",
        compiler_params=pltpu.CompilerParams(vmem_limit_bytes=30 << 20),
    )(meta, tokens, grad, act, hg, *atts, *qgs, *weights, *tail, *extra)


def sum_kernel(n_in, *refs):
    ins, outs = refs[:n_in], refs[n_in:]
    for k, out in enumerate(outs):
        rows = out.shape[0]
        for i in range(rows):
            total = ins[0][k * rows + i].astype(f32)
            for term in ins[1:]:
                total += term[k * rows + i].astype(f32)
            out[i] = total.astype(out.dtype)


def sum_call(terms, count, name):
    shape, dtype = terms[0].shape, terms[0].dtype
    moved = len(terms) * terms[0].size * terms[0].dtype.itemsize
    return pl.pallas_call(
        functools.partial(sum_kernel, len(terms)),
        out_shape=[jax.ShapeDtypeStruct((shape[0] // count, *shape[1:]), dtype)] * count,
        compiler_params=pltpu.CompilerParams(vmem_limit_bytes=(moved * 3) // 2 + (4 << 20)),
        cost_estimate=cost(moved, 2 * moved),
        name=name,
    )(*terms)


def pair_kernel(*refs):
    own, got, outs = refs[:2], refs[2:4], refs[4:]
    for j, (mine, other) in enumerate(zip(own, got)):
        w = mine.shape[2]
        for k, out in enumerate(outs):
            total = mine[k].astype(f32) + other[k].astype(f32)
            out[0, :, j * w : (j + 1) * w] = total.astype(bf16)


def pair_call(own, got, name):
    rows, width = own[0].shape[1], 2 * own[0].shape[2]
    return pl.pallas_call(
        pair_kernel,
        out_shape=[jax.ShapeDtypeStruct((1, rows, width), bf16)] * 4,
        compiler_params=pltpu.CompilerParams(vmem_limit_bytes=12 << 20),
        cost_estimate=cost(8 * rows * width, 24 * rows * width),
        name=name,
    )(*own, *got)


def half_kernel(meta, mine_ref, got_ref, keep_ref, send_ref):
    rows = keep_ref.shape[1]
    for out, number in ((keep_ref, meta[3]), (send_ref, 1 - meta[3])):
        at = pl.ds(pl.multiple_of(number * rows, rows), rows)
        out[0] = (mine_ref[0, at, :].astype(f32) + got_ref[0, at, :].astype(f32)).astype(bf16)


def join_kernel(meta, mine_ref, got_ref, out_ref):
    rows = mine_ref.shape[1]
    for piece, number in ((mine_ref, meta[3]), (got_ref, 1 - meta[3])):
        out_ref[0, pl.ds(pl.multiple_of(number * rows, rows), rows), :] = piece[0]


def half_call(kernel, meta, terms, outs, name):
    moved = 2 * sum(a.size for a in terms)
    whole = pl.BlockSpec(memory_space=pltpu.VMEM)
    return pl.pallas_call(
        kernel,
        in_specs=[pl.BlockSpec(memory_space=pltpu.SMEM), whole, whole],
        out_specs=[whole] * len(outs),
        out_shape=[jax.ShapeDtypeStruct(o, bf16) for o in outs],
        compiler_params=pltpu.CompilerParams(vmem_limit_bytes=(moved * 3) // 2 + (4 << 20)),
        cost_estimate=cost(moved, 2 * moved),
        name=name,
    )(meta, *terms)


def exchange(a, reps, far, near):
    pairs = [(2 * i + c, 2 * (i ^ (near if c else far)) + c) for i in range(reps) for c in range(2)]
    return lax.ppermute(a, ("rep", "opt"), pairs)


def swap(a):
    return lax.ppermute(a, "opt", [(0, 1), (1, 0)])


def tie(value, *others):
    return lax.optimization_barrier((value, *others))[0]


def rest_bits(reps):
    return [1 << b for b in range(2, reps.bit_length() - 1)]


def crosses(pieces, reps):
    steps = ((2, 1), (1, 2), (3, 3))
    return [exchange(a, reps, *step) for a, step in zip(pieces, steps)]


def adamw(grad, mean, square, weight):
    new_mean = BETA_ONE * mean + (1.0 - BETA_ONE) * grad
    new_square = BETA_TWO * square + (1.0 - BETA_TWO) * grad * grad
    step = -LEARN_RATE * (
        new_mean * (1.0 / FIX_ONE) / (jnp.sqrt(new_square * (1.0 / FIX_TWO)) + ADAM_EPS)
        + WEIGHT_DECAY * weight.astype(f32)
    )
    return step, new_mean, new_square


def pick(refs, which, cols, rows=slice(None)):
    out = refs[0][0, rows, cols]
    for k in range(1, len(refs)):
        out = jnp.where(which == k, refs[k][0, rows, cols], out)
    return out.astype(f32)


def adam_block(grad, m_ref, s_ref, w_ref, g_out, st_out, m_out, s_out, at):
    step, mean, square = adamw(grad, m_ref[at], s_ref[at], w_ref[at])
    g_out[at] = grad
    st_out[at] = step
    m_out[at] = mean
    s_out[at] = square


def adam_ff_kernel(meta, *refs):
    pieces, proj, fc, proj_out, fc_out = refs[:-14], refs[-14:-11], refs[-11:-8], refs[-8:-4], refs[-4:]
    which = pl.program_id(0)
    n = fc[0].shape[0]
    rows = pl.ds(pl.multiple_of(pl.program_id(1) * n, n), n)
    for j in range(2):
        for k in range(2):
            col = 1024 * j + 512 * k
            at = (j, 0, k, slice(None), slice(None))
            adam_block(pick(pieces, which, slice(col, col + 512), rows), *proj, *proj_out, at)
            at = (slice(None), slice(col, col + 512))
            adam_block(pick(pieces, which, slice(2048 + col, 2048 + col + 512), rows), *fc, *fc_out, at)


def adam_qkv_kernel(meta, *refs):
    pieces, qkv, out, qkv_out, out_out = refs[:-14], refs[-14:-11], refs[-11:-8], refs[-8:-4], refs[-4:]
    c = meta[0]
    which = pl.program_id(0)
    sub = pl.program_id(1)
    n = qkv[0].shape[0]
    h = out[0].shape[1]
    rows = pl.ds(pl.multiple_of(sub * n, n), n)
    for j in range(2):
        for slot in range(2):
            for p in range(3):
                col = 1024 * j + 384 * slot + 128 * p
                grad = pick(pieces, which, slice(col, col + 128), rows)
                lanes = pl.ds(pl.multiple_of((p * 4 + (slot ^ c) * 2 + j) * 128, 128), 128)
                adam_block(grad, *qkv, *qkv_out, (slice(None), lanes))
        for k in range(2):
            col = 1024 * j + 768
            half = pl.ds(pl.multiple_of(k * (pieces[0].shape[1] // 2) + sub * h, h), h)
            grad = pick(pieces, which, slice(col, col + 256), half)
            adam_block(grad, *out, *out_out, (j, slice(None), slice(256 * k, 256 * k + 256)))


def adam_call(kernel, meta, start, pieces, first, second, first_spec, second_spec, subs, name, before=()):
    outs = [jax.ShapeDtypeStruct(first[0].shape, f32)] * 4 + [jax.ShapeDtypeStruct(second[0].shape, f32)] * 4
    specs = [
        pl.BlockSpec(shape, functools.partial(lambda at, i, k, m: at((start + i) ^ m[1], k), at))
        for shape, at in (first_spec, second_spec)
    ]
    count = len(before)

    def run(meta_ref, *refs):
        kernel(meta_ref, *refs[count:])

    grid_spec = pltpu.PrefetchScalarGridSpec(
        num_scalar_prefetch=1,
        grid=(len(pieces), subs),
        in_specs=[
            *[pl.BlockSpec(memory_space=pl.ANY)] * count,
            *[full_spec(a.shape) for a in pieces],
            *[specs[0]] * 3,
            *[specs[1]] * 3,
        ],
        out_specs=[*[specs[0]] * 4, *[specs[1]] * 4],
    )
    size = (first[0].size + second[0].size) * len(pieces) // 4
    return pl.pallas_call(
        run,
        grid_spec=grid_spec,
        out_shape=outs,
        input_output_aliases={1 + k: k for k in range(count)},
        compiler_params=pltpu.CompilerParams(vmem_limit_bytes=56 << 20),
        cost_estimate=cost(20 * size, 28 * size),
        name=name,
    )(meta, *before, *pieces, *first, *second)


def body(
    tokens,
    out_grad,
    vectors,
    qkv_weight,
    qkv_bias,
    out_weight,
    fc_weight,
    fc_bias,
    proj_weight,
    mean_vectors,
    mean_qkv_weight,
    mean_qkv_bias,
    mean_out_weight,
    mean_fc_weight,
    mean_fc_bias,
    mean_proj_weight,
    square_vectors,
    square_qkv_weight,
    square_qkv_bias,
    square_out_weight,
    square_fc_weight,
    square_fc_bias,
    square_proj_weight,
):
    reps = lax.axis_size("rep")
    c = lax.axis_index("opt")
    place = lax.axis_index("rep")
    low, high = place & 1, (place >> 1) & 1
    slot = lax.iota(jnp.int32, 4)
    ranks = jnp.where((slot == 1) == (c == 0), 2 * low + high, 2 * high + low)
    meta = jnp.where(slot == 0, c, jnp.where(slot == 3, (place >> 2) & 1, ranks)).astype(jnp.int32)
    trig = jnp.asarray(trig_tables())

    packed = jnp.concatenate(
        [vectors.reshape(12, 128), qkv_bias.reshape(6, 128), fc_bias.reshape(8, 128)], 0
    )
    small = lax.all_gather(packed, "opt", axis=0, tiled=True).astype(f32).reshape(2 * SMALL_ROWS, 1, 128)
    fc_far = swap(fc_weight)
    proj_far = swap(proj_weight)
    qkv_far = swap(qkv_weight)
    out_far = swap(out_weight)

    first, second = norm_call(tokens, small)
    send, act, hg, fb = ff_call(
        meta, second, out_grad, fc_weight, fc_far, proj_weight, proj_far, small
    )
    ff_got = swap(send)
    own = ff_own_call(tie(meta, send), second, out_grad, act, hg)
    att = {}
    bits = rest_bits(reps)

    def attend(j, rel, *wait):
        out_w = out_far if rel else out_weight
        before = att[j, 1][:2] if rel == 0 else ()
        att[j, rel] = attention_call(
            j, rel, tie(meta, *wait), first, out_grad, qkv_weight, qkv_far, out_w, small, trig, before
        )
        return att[j, rel][4]

    def rest(total, start, name):
        for bit in bits[start:]:
            (total,) = sum_call([total, exchange(total, reps, bit, bit)], 1, name)
        return total

    keep, send = sum_call([own, ff_got], 2, "ff_pair")
    got = exchange(send, reps, 1, 2)
    mark = attend(0, 1, keep)
    keep, send = sum_call([tie(keep, mark), got], 2, "ff_sum0")
    got = exchange(send, reps, 2, 1)
    mark = attend(0, 0, keep)
    whole = keep.shape
    half = (1, whole[1] // 2, whole[2])
    keep, send = half_call(half_kernel, meta, [tie(keep, mark), got], [half] * 2, "ff_sum1")
    got = exchange(send, reps, bits[0], bits[0])
    own, others = [att[0, 0][0]], [swap(att[0, 0][1])]
    mark = attend(1, 1, keep)
    (piece,) = sum_call([tie(keep, mark), got], 1, "ff_sum2")
    ff_got = exchange(piece, reps, bits[1], bits[1])
    mark = attend(1, 0, piece, others[0])

    (piece,) = sum_call([tie(piece, mark), ff_got], 1, "ff_sum3")
    piece = rest(piece, 2, "ff_sum4")
    ff_got = exchange(piece, reps, bits[0], bits[0])
    own.append(att[1, 0][0])
    others.append(swap(tie(att[1, 0][1], piece)))
    chunks = pair_call(own, others, "att_pair")
    got = crosses(chunks[1:], reps)

    keys = [(0, 0), (0, 1), (1, 0), (1, 1)]
    give = lambda part, before, *wait: output_call(
        part,
        PARTS,
        tie(meta, *wait),
        tokens,
        out_grad,
        act,
        hg,
        [att[k][3] for k in keys],
        [att[k][2] for k in keys],
        (out_weight, out_far),
        (proj_weight, proj_far),
        (fc_weight, fc_far),
        (qkv_weight, qkv_far),
        small,
        [att[k][4] for k in keys],
        fb,
        before,
    )
    done = give(0, None, piece, chunks[0])
    (att_total,) = sum_call([tie(chunks[0], done[2]), *got], 1, "att_sum0")
    got = exchange(att_total, reps, bits[0], bits[0])
    (ff_total,) = half_call(join_kernel, meta, [tie(piece, att_total), ff_got], [whole], "ff_join")
    ff_pieces = [ff_total, exchange(ff_total, reps, 2, 1), exchange(ff_total, reps, 1, 2)]
    layer_out, tokens_grad, small_own, small_send = give(1, done, att_total, ff_total)

    (att_total,) = sum_call([tie(att_total, small_own, *ff_pieces[1:]), got], 1, "att_sum1")
    got = exchange(att_total, reps, bits[1], bits[1])
    ff_pieces.append(exchange(tie(ff_pieces[2], att_total), reps, 2, 1))
    (total,) = sum_call([tie(small_own, att_total), swap(small_send)], 1, "small_pair")
    small_got = exchange(total, reps, 1, 1)

    view = lambda a: a.reshape(2, 4, 2, 64, 512)
    adam_ff = lambda start, pieces, before, *wait: adam_call(
        adam_ff_kernel,
        tie(meta, *wait),
        start,
        pieces,
        [view(a) for a in (mean_proj_weight, square_proj_weight, proj_weight)],
        [mean_fc_weight, square_fc_weight, fc_weight],
        ((2, 1, 2, 64, 512), lambda q, k: (0, q, 0, k, 0)),
        ((64, 2048), lambda q, k: (q + k, 0)),
        1,
        f"adam_ff_{start}",
        before,
    )
    view_o = lambda a: a.reshape(2, 128, 512)
    adam_qkv = lambda start, pieces, before, *wait: adam_call(
        adam_qkv_kernel,
        tie(meta, *wait),
        start,
        pieces,
        [mean_qkv_weight, square_qkv_weight, qkv_weight],
        [view_o(a) for a in (mean_out_weight, square_out_weight, out_weight)],
        ((64, 1536), lambda q, k: (q + k, 0)),
        ((2, 32, 512), lambda q, k: (0, q + k, 0)),
        1,
        f"adam_qkv_{start}",
        before,
    )
    a_ff = adam_ff(0, ff_pieces[:3], (), total, att_total)
    (total,) = sum_call([tie(total, a_ff[4]), small_got], 1, "small_sum")
    small_got = exchange(total, reps, bits[0], bits[0])
    (att_total,) = sum_call([tie(att_total, total), got], 1, "att_sum2")
    att_total = rest(att_total, 2, "att_sum3")
    att_pieces = [att_total, *crosses([att_total] * 3, reps)]
    a_ff = adam_ff(3, ff_pieces[3:], a_ff, att_total)
    (total,) = sum_call([tie(total, a_ff[4]), small_got], 1, "small_sum")
    small_got = exchange(total, reps, bits[1], bits[1])
    a_qkv = adam_qkv(0, att_pieces[:1], (), total)
    (total,) = sum_call([tie(total, a_qkv[0]), small_got], 1, "small_sum")
    mark = tie(total, *att_pieces[1:])
    small_got = exchange(mark, reps, 2, 2)

    a_qkv = adam_qkv(1, att_pieces[1:], a_qkv, mark)
    a_proj = [a.reshape(1024, 512) for a in a_ff[:4]]
    a_fc = a_ff[4:]
    a_out = [a.reshape(256, 512) for a in a_qkv[4:]]
    a_qkv = a_qkv[:4]
    (total,) = sum_call([tie(mark, a_out[0]), small_got], 1, "small_sum")
    total = rest(total, 2, "small_sum")
    flat = total.reshape(32, 128)
    g_vec = flat[:12].reshape(6, 256)
    g_qb = flat[12:18].reshape(768)
    g_fb = flat[18:26].reshape(1024)

    a_vec = (g_vec, *adamw(g_vec, mean_vectors, square_vectors, vectors))
    a_qb = (g_qb, *adamw(g_qb, mean_qkv_bias, square_qkv_bias, qkv_bias))
    a_fb = (g_fb, *adamw(g_fb, mean_fc_bias, square_fc_bias, fc_bias))
    order = (a_vec, a_qkv, a_qb, a_out, a_fc, a_fb, a_proj)
    return (layer_out, tokens_grad, *[a[k] for k in range(4) for a in order])


def solution(mesh):
    rows = P(("rep", "opt"), None)
    weights = (P(None, "opt"), P("opt", None), P("opt"), P("opt", None), P("opt", None), P("opt"), P("opt", None))
    in_specs = (rows, rows, *weights, *weights, *weights)
    out_specs = (rows, rows, *weights, *weights, *weights, *weights)
    return jax.shard_map(body, mesh=mesh, in_specs=in_specs, out_specs=out_specs, check_vma=False)
```

```python
import functools

import jax
import jax.numpy as jnp
import numpy as np
from jax import lax
from jax.experimental import pallas as pl
from jax.experimental.pallas import tpu as pltpu
from jax.sharding import PartitionSpec as P

H = 8
ROT = 16
LEN = 512
ADAM_STEP = 10

LN_EPS = 1e-05
ADAM_EPS = 1e-08
BETA_ONE = 0.9
BETA_TWO = 0.95
LEARN_RATE = 0.02
WEIGHT_DECAY = 0.01
FIX_ONE = 1.0 - BETA_ONE**ADAM_STEP
FIX_TWO = 1.0 - BETA_TWO**ADAM_STEP
INV_ROOT_TWO = 0.7071067811865476
INV_ROOT_TWO_PI = 0.3989422804014327

bf16 = jnp.bfloat16
f32 = jnp.float32
PARTS = 2
SMALL_ROWS = 26


def dot_nn(a, b):
    return lax.dot_general(a, b, (((1,), (0,)), ((), ())), preferred_element_type=f32)


def dot_nt(a, b):
    return lax.dot_general(a, b, (((1,), (1,)), ((), ())), preferred_element_type=f32)


def dot_tn(a, b):
    return lax.dot_general(a, b, (((0,), (0,)), ((), ())), preferred_element_type=f32)


def full_spec(shape):
    zeros = (0,) * len(shape)
    return pl.BlockSpec(shape, lambda *_: zeros)


def cost(flops, moved, transcendentals=0):
    return pl.CostEstimate(
        flops=int(flops), bytes_accessed=int(moved), transcendentals=int(transcendentals)
    )


def vec_row(small_ref, i):
    n = SMALL_ROWS
    rows = [small_ref[o * n + 2 * i + k] for o in range(2) for k in range(2)]
    return jnp.concatenate(rows, 1)


def normalise(x):
    centre = x - jnp.mean(x, -1, keepdims=True)
    inv_dev = lax.rsqrt(jnp.mean(centre * centre, -1, keepdims=True) + LN_EPS)
    return centre * inv_dev, inv_dev


def norm_kernel(tok_ref, small_ref, first_ref, second_ref):
    normed, _ = normalise(tok_ref[...].astype(f32))
    first_ref[...] = (normed * vec_row(small_ref, 0) + vec_row(small_ref, 1)).astype(bf16)
    second_ref[...] = (normed * vec_row(small_ref, 2) + vec_row(small_ref, 3)).astype(bf16)


def norm_call(tokens, small):
    rows, width = tokens.shape
    tile = 512
    spec = pl.BlockSpec((tile, width), lambda i: (i, 0))
    out = jax.ShapeDtypeStruct((rows, width), bf16)
    return pl.pallas_call(
        norm_kernel,
        grid=(rows // tile,),
        in_specs=[spec, full_spec(small.shape)],
        out_specs=[spec, spec],
        out_shape=[out, out],
        cost_estimate=cost(20 * rows * width, 6 * rows * width),
        name="norm",
        compiler_params=pltpu.CompilerParams(vmem_limit_bytes=12 << 20),
    )(tokens, small)


def ff_kernel(meta, second_ref, grad_ref, fco_ref, fcx_ref, pro_ref, prx_ref, small_ref,
              send_ref, act_ref, hg_ref, bias_ref, fc_ref):
    j = pl.program_id(0)
    rel = pl.program_id(1)
    c = meta[0]
    far_rank = meta[2]
    o = rel ^ c
    rows, width = second_ref.shape
    half = width // 2
    cols = act_ref.shape[1]
    quarter = half // 4
    proj = jnp.where(rel == 0, pro_ref[...], prx_ref[...])
    own_lanes = pl.ds(pl.multiple_of(c * half, half), half)
    far_lanes = pl.ds(pl.multiple_of((1 - c) * half, half), half)
    fc_ref[own_lanes, :] = fco_ref[...]
    fc_ref[far_lanes, :] = fcx_ref[...]
    fc = fc_ref[...]
    base = o * SMALL_ROWS + 18 + 4 * j
    bias = jnp.concatenate([small_ref[base + k] for k in range(cols // 128)], 1)
    sub, parts = 256, 4
    tile = sub * parts

    def block(i, total):
        at = [pl.ds(pl.multiple_of(i * tile + k * sub, sub), sub) for k in range(parts)]
        products = [(dot_nn(second_ref[r, :], fc), dot_nt(grad_ref[r, :], proj)) for r in at]
        for r, (product, act_grad) in zip(at, products):
            hidden = product + bias
            phi_cap = 0.5 + 0.5 * lax.erf(hidden * INV_ROOT_TWO)
            slope = phi_cap + hidden * (jnp.exp(-0.5 * hidden * hidden) * INV_ROOT_TWO_PI)
            act_ref[r, :] = (hidden * phi_cap).astype(bf16)
            hg = (act_grad * slope).astype(bf16)
            hg_ref[r, :] = hg
            total += jnp.sum(hg.astype(f32).reshape(sub // 8, 8, cols), 0)
        return total

    total = lax.fori_loop(0, rows // tile, block, jnp.zeros((8, cols), f32))
    bias_ref[...] = jnp.sum(total, 0, keepdims=True)[None]
    pl.when(rel == 1)(lambda: put_proj(send_ref, dot_tn(act_ref[...], grad_ref[...]), j, far_rank))
    put_fc(send_ref, dot_tn(second_ref[:, far_lanes], hg_ref[...]), o, j, far_rank)


def put_proj(ref, grad, j, rank):
    quarter = ref.shape[1]
    lanes = pl.ds(pl.multiple_of(j * 1024, 1024), 1024)
    for a in range(4):
        piece = grad[a * 2 * quarter : (a + 1) * 2 * quarter]
        ref[a ^ rank, :, lanes] = jnp.concatenate([piece[:quarter], piece[quarter:]], 1).astype(bf16)


def put_fc(ref, grad, o, j, rank):
    quarter = ref.shape[1]
    cols = grad.shape[1]
    lanes = pl.ds(pl.multiple_of(2048 + o * 1024 + j * cols, cols), cols)
    for a in range(4):
        ref[a ^ rank, :, lanes] = grad[a * quarter : (a + 1) * quarter].astype(bf16)


def ff_own_kernel(meta, second_ref, grad_ref, act_ref, hg_ref, own_ref):
    j = pl.program_id(0)
    rel = pl.program_id(1)
    c = meta[0]
    rank = meta[1]
    half = second_ref.shape[1] // 2
    own_lanes = pl.ds(pl.multiple_of(c * half, half), half)
    pl.when(rel == 0)(lambda: put_proj(own_ref, dot_tn(act_ref[...], grad_ref[...]), j, rank))
    put_fc(own_ref, dot_tn(second_ref[:, own_lanes], hg_ref[...]), rel ^ c, j, rank)


def ff_call(meta, second, grad, fc_own, fc_far, proj_own, proj_far, small):
    rows, width = second.shape
    ff = fc_own.shape[1]
    half = width // 2
    cols = ff // 4
    buf = (4, half // 4, 2 * ff)
    fc_spec = pl.BlockSpec((half, cols), lambda j, r, m: (0, (r ^ m[0]) * 2 + j))
    proj_spec = pl.BlockSpec((cols, width), lambda j, r, m: (j, 0))
    act_spec = pl.BlockSpec((rows, cols), lambda j, r, m: (0, 2 * j + r))
    grid_spec = pltpu.PrefetchScalarGridSpec(
        num_scalar_prefetch=1,
        grid=(2, 2),
        in_specs=[
            full_spec((rows, width)),
            full_spec((rows, width)),
            fc_spec,
            fc_spec,
            proj_spec,
            proj_spec,
            full_spec(small.shape),
        ],
        out_specs=[
            full_spec(buf),
            act_spec,
            act_spec,
            pl.BlockSpec((1, 1, cols), lambda j, r, m: (2 * j + r, 0, 0)),
        ],
        scratch_shapes=[pltpu.VMEM((width, cols), bf16)],
    )
    return pl.pallas_call(
        ff_kernel,
        grid_spec=grid_spec,
        out_shape=[
            jax.ShapeDtypeStruct(buf, bf16),
            jax.ShapeDtypeStruct((rows, ff), bf16),
            jax.ShapeDtypeStruct((rows, ff), bf16),
            jax.ShapeDtypeStruct((4, 1, cols), f32),
        ],
        cost_estimate=cost(6 * rows * width * ff, 4 * rows * width + 4 * rows * ff),
        name="feed_forward",
        compiler_params=pltpu.CompilerParams(vmem_limit_bytes=40 << 20),
    )(meta, second, grad, fc_own, fc_far, proj_own, proj_far, small)


def ff_own_call(meta, second, grad, act, hg):
    rows, width = second.shape
    ff = act.shape[1]
    cols = ff // 4
    buf = (4, width // 8, 2 * ff)
    grid_spec = pltpu.PrefetchScalarGridSpec(
        num_scalar_prefetch=1,
        grid=(2, 2),
        in_specs=[
            full_spec((rows, width)),
            full_spec((rows, width)),
            pl.BlockSpec((rows, cols), lambda j, r, m: (0, 2 * j)),
            pl.BlockSpec((rows, cols), lambda j, r, m: (0, 2 * j + r)),
        ],
        out_specs=full_spec(buf),
    )
    return pl.pallas_call(
        ff_own_kernel,
        grid_spec=grid_spec,
        out_shape=jax.ShapeDtypeStruct(buf, bf16),
        cost_estimate=cost(2 * rows * width * ff, 4 * rows * width + 3 * rows * ff),
        name="feed_forward_own",
        compiler_params=pltpu.CompilerParams(vmem_limit_bytes=44 << 20),
    )(meta, second, grad, act, hg)


def rotate_rows(x, cosine, sine):
    parts = []
    for h in range(2):
        low, high = x[64 * h : 64 * h + 8], x[64 * h + 8 : 64 * h + 16]
        parts += [low * cosine - high * sine, high * cosine + low * sine, x[64 * h + 16 : 64 * h + 64]]
    return jnp.concatenate(parts, 0)


def attention_kernel(j, rel, meta, first_ref, grad_ref, wq_ref, wk_ref, wv_ref, xq_ref, xk_ref, xv_ref,
                     ow_ref, small_ref, trig_ref, *refs):
    if rel == 0:
        own_first_ref, send_first_ref, refs = refs[0], refs[1], refs[2:]
    own_ref, send_ref, qg_ref, att_ref, bias_ref, wt_ref, bcol_ref, qgs_ref, attt_ref, btot_ref = refs
    s = pl.program_id(0)
    c = meta[0]
    rank, far_rank = meta[1], meta[2]
    o = rel ^ c
    rows, width = first_ref.shape
    half = width // 2
    quarter = half // 4
    own_lanes = pl.ds(pl.multiple_of(c * half, half), half)
    far_lanes = pl.ds(pl.multiple_of((1 - c) * half, half), half)

    @pl.when(s == 0)
    def _():
        for p, (own, far) in enumerate(((wq_ref, xq_ref), (wk_ref, xk_ref), (wv_ref, xv_ref))):
            wt_ref[128 * p : 128 * (p + 1), own_lanes] = own[...].T
            wt_ref[128 * p : 128 * (p + 1), far_lanes] = far[...].T
            row = p * 4 + o * 2 + j
            owner = row // 6
            bias = small_ref[owner * SMALL_ROWS + 12 + row - 6 * owner]
            bcol_ref[128 * p : 128 * (p + 1), :] = jnp.broadcast_to(bias, (128, 128)).T
        btot_ref[...] = jnp.zeros_like(btot_ref)

    seq = pl.ds(pl.multiple_of(s * LEN, LEN), LEN)
    first = first_ref[seq, :]
    grad = grad_ref[seq, :]
    mixed = dot_nt(wt_ref[...], first) + bcol_ref[:, :1]
    da_t = dot_nt(ow_ref[...], grad).astype(bf16)
    cosine, sine = trig_ref[0], trig_ref[1]
    q_t = rotate_rows(mixed[:128], cosine, sine).astype(bf16) * jnp.asarray(0.125, bf16)
    k_t = rotate_rows(mixed[128:256], cosine, sine).astype(bf16)
    v_t = mixed[256:].astype(bf16)
    k_tok = k_t.T
    v_tok = v_t.T
    hl = LEN // 2
    row_id = lax.broadcasted_iota(jnp.int32, (hl, hl), 0)
    col_id = lax.broadcasted_iota(jnp.int32, (hl, hl), 1)
    keep = row_id <= col_id
    zeros = jnp.zeros((64, LEN), bf16)
    def pad(u, h):
        return jnp.concatenate([u, zeros], 0) if h == 0 else jnp.concatenate([zeros, u], 0)

    def open_chunk(h, t):
        hs, ts, n = slice(64 * h, 64 * h + 64), slice(hl * t, hl * t + hl), hl * (t + 1)
        return dot_nn(k_tok[:n], pad(q_t[hs], h)[:, ts]), dot_nn(v_tok[:n], pad(da_t[hs], h)[:, ts])

    def close_chunk(h, t, score, pg):
        hs, ts, n = slice(64 * h, 64 * h + 64), slice(hl * t, hl * t + hl), hl * (t + 1)
        qh, kh, vh, dah = q_t[hs], k_t[hs], v_t[hs], da_t[hs]
        diag = jnp.where(keep, score[n - hl :], -1e30)
        score = diag if t == 0 else jnp.concatenate([score[:hl], diag], 0)
        exps = jnp.exp(score - jnp.max(score, 0, keepdims=True))
        prob = exps * (1.0 / jnp.sum(exps, 0, keepdims=True))
        prob_b = prob.astype(bf16)
        sg = (prob * (pg - jnp.sum(pg * prob, 0, keepdims=True))).astype(bf16)
        return (
            dot_nn(vh[:, :n], prob_b),
            dot_nn(kh[:, :n], sg),
            dot_nt(dah[:, ts], prob_b),
            dot_nt(qh[:, ts], sg),
        )

    chunks = [(h, t) for h in range(2) for t in range(2)]
    ahead = 4
    opened = [open_chunk(*k) for k in chunks[:ahead]]
    closed = {}
    for i, k in enumerate(chunks):
        if i + ahead < len(chunks):
            opened.append(open_chunk(*chunks[i + ahead]))
        closed[k] = close_chunk(*k, *opened[i])
    att, dq, dk, dv = [], [], [], []
    for h in range(2):
        (a0, q0, v0, k0), (a1, q1, v1, k1) = closed[h, 0], closed[h, 1]
        att.append(jnp.concatenate([a0, a1], 1))
        dq.append(jnp.concatenate([q0, q1], 1) * 0.125)
        dk.append(jnp.concatenate([k0 + k1[:, :hl], k1[:, hl:]], 1))
        dv.append(jnp.concatenate([v0 + v1[:, :hl], v1[:, hl:]], 1))
    att_t = jnp.concatenate(att, 0).astype(bf16)
    dq_t = rotate_rows(jnp.concatenate(dq, 0), cosine, -sine)
    dk_t = rotate_rows(jnp.concatenate(dk, 0), cosine, -sine)
    qkv_t = jnp.concatenate([dq_t, dk_t, jnp.concatenate(dv, 0)], 0).astype(bf16)
    qkv_g = qkv_t.T
    qg_ref[...] = qkv_g
    qgs_ref[seq, :] = qkv_g
    att_ref[...] = att_t.T
    attt_ref[:, seq] = att_t
    btot_ref[...] += jnp.sum(qkv_g.astype(f32).reshape(LEN // 8, 8, 384), 0)

    @pl.when(s == pl.num_programs(0) - 1)
    def _():
        bias_ref[...] = jnp.sum(btot_ref[...], 0, keepdims=True)
        at_own, at_send = (0, 384) if rel == 0 else (0, 0)
        if rel == 0:
            own_ref[:, :, 384:768] = own_first_ref[...]
            send_ref[:, :, :384] = send_first_ref[:, :, :384]
            send_ref[:, :, 768:] = send_first_ref[:, :, 384:]
        for ref, side, number, at in ((own_ref, own_lanes, rank, at_own), (send_ref, far_lanes, far_rank, at_send)):
            gw = dot_tn(first_ref[:, side], qgs_ref[...])
            for a in range(4):
                ref[a ^ number, :, at : at + 384] = gw[a * quarter : (a + 1) * quarter].astype(bf16)
        go = dot_nn(attt_ref[...], grad_ref[...])
        hq = quarter // 2
        for a in range(4):
            piece = go[a * hq : (a + 1) * hq]
            piece = jnp.concatenate([piece[:, :256], piece[:, 256:]], 0).astype(bf16)
            if rel == 0:
                own_ref[a ^ rank, :, 768:] = piece
            else:
                send_ref[a ^ far_rank, :, 384:] = piece


def trig_tables():
    freqs = np.power(np.float32(10000.0), -np.arange(0, ROT, 2).astype(np.float32) / np.float32(ROT))
    angles = (np.arange(LEN).astype(np.float32)[None, :] * freqs[:, None]).astype(np.float32)
    return np.stack([np.cos(angles), np.sin(angles)]).astype(np.float32)


def attention_call(j, rel, meta, first, grad, qkv_own, qkv_far, out_w, small, trig, before=()):
    rows, width = first.shape
    half = width // 2
    bufs = [(4, half // 4, w) for w in ((1024, 1024) if rel == 0 else (384, 640))]
    w_specs = [
        pl.BlockSpec((half, 128), functools.partial(lambda p, s, m: (0, p * 4 + (rel ^ m[0]) * 2 + j), p))
        for p in range(3)
    ]
    grid_spec = pltpu.PrefetchScalarGridSpec(
        num_scalar_prefetch=1,
        grid=(rows // LEN,),
        in_specs=[
            full_spec((rows, width)),
            full_spec((rows, width)),
            *w_specs,
            *w_specs,
            pl.BlockSpec((128, width), lambda s, m: (j, 0)),
            full_spec(small.shape),
            full_spec(trig.shape),
            *[full_spec(a.shape) for a in before],
        ],
        out_specs=[
            *[full_spec(b) for b in bufs],
            pl.BlockSpec((LEN, 384), lambda s, m: (s, 0)),
            pl.BlockSpec((LEN, 128), lambda s, m: (s, 0)),
            full_spec((1, 384)),
        ],
        scratch_shapes=[
            pltpu.VMEM((384, width), bf16),
            pltpu.VMEM((384, 128), f32),
            pltpu.VMEM((rows, 384), bf16),
            pltpu.VMEM((128, rows), bf16),
            pltpu.VMEM((8, 384), f32),
        ],
    )
    flops = 2 * rows * width * (2 * 384 + 2 * 128) + 2 * 6 * 2 * rows * LEN * 128
    return pl.pallas_call(
        functools.partial(attention_kernel, j, rel),
        grid_spec=grid_spec,
        out_shape=[
            *[jax.ShapeDtypeStruct(b, bf16) for b in bufs],
            jax.ShapeDtypeStruct((rows, 384), bf16),
            jax.ShapeDtypeStruct((rows, 128), bf16),
            jax.ShapeDtypeStruct((1, 384), f32),
        ],
        cost_estimate=cost(flops, 4 * rows * width + 2 * rows * 512),
        name=f"attention_{j}{rel}",
        compiler_params=pltpu.CompilerParams(vmem_limit_bytes=18 << 20),
    )(meta, first, grad, *[qkv_own] * 3, *[qkv_far] * 3, out_w, small, trig, *before)


def output_kernel(part, parts, meta, tok_ref, grad_ref, act_ref, hg_ref, *refs):
    at_refs, qg_refs, refs = refs[0:4], refs[4:8], refs[8:]
    oo_ref, ox_ref, po_ref, px_ref, fo_ref, fx_ref, wo_ref, wx_ref, small_ref = refs[:9]
    qb_refs, fb_ref, refs = refs[9:13], refs[13], refs[14:]
    if part > 0:
        before_ref, refs = refs[0], refs[3:]
    lay_ref, tg_ref, refs = refs[0], refs[1], refs[2:]
    if part < parts - 1:
        tot_ref, wgo_ref, wgx_ref, sg_ref, fg_ref = refs
    else:
        own_ref, send_ref, wgo_ref, wgx_ref, sg_ref, fg_ref, tot_ref, qb_ref = refs
    i = pl.program_id(0)
    c = meta[0]
    tile, width = tok_ref.shape
    half = width // 2
    own_lanes = pl.ds(pl.multiple_of(c * half, half), half)
    far_lanes = pl.ds(pl.multiple_of((1 - c) * half, half), half)

    @pl.when(i == 0)
    def _():
        for w_ref, g_ref in ((wo_ref, wgo_ref), (wx_ref, wgx_ref)):
            for j in range(2):
                for rel in range(2):
                    for p in range(3):
                        src = pl.ds(pl.multiple_of((p * 4 + (rel ^ c) * 2 + j) * 128, 128), 128)
                        dst = (j * 6 + rel * 3 + p) * 128
                        g_ref[:, dst : dst + 128] = w_ref[:, src]
        tot_ref[...] = jnp.zeros_like(tot_ref) if part == 0 else before_ref[...]

    x = tok_ref[...].astype(f32)
    grad = grad_ref[...].astype(f32)
    normed, inv_dev = normalise(x)
    acc = dot_nn(jnp.concatenate([at_refs[0][...], at_refs[2][...]], 1), oo_ref[...])
    acc += dot_nn(jnp.concatenate([at_refs[1][...], at_refs[3][...]], 1), ox_ref[...])
    for j in range(2):
        for rel, p_ref in enumerate((po_ref, px_ref)):
            k = 512 * (2 * j + rel)
            acc += dot_nn(act_ref[:, k : k + 512], p_ref[512 * j : 512 * (j + 1), :])
    lay_ref[...] = (x + acc + (vec_row(small_ref, 4) + vec_row(small_ref, 5))).astype(bf16)

    for f_ref, wg_ref, lanes in ((fo_ref, wgo_ref, own_lanes), (fx_ref, wgx_ref, far_lanes)):
        total = None
        for j in range(2):
            for rel in range(2):
                k = 512 * (2 * j + rel)
                cols = pl.ds(pl.multiple_of((rel ^ c) * 1024 + 512 * j, 512), 512)
                term = dot_nt(hg_ref[:, k : k + 512], f_ref[:, cols])
                total = term if total is None else total + term
        sg_ref[:, lanes] = total
        qg = [jnp.concatenate([qg_refs[2 * j][...], qg_refs[2 * j + 1][...]], 1) for j in range(2)]
        fg_ref[:, lanes] = dot_nt(qg[0], wg_ref[:, :768]) + dot_nt(qg[1], wg_ref[:, 768:])
    second_g = sg_ref[...]
    first_g = fg_ref[...]
    e = first_g * vec_row(small_ref, 0) + second_g * vec_row(small_ref, 2)
    ln = inv_dev * (
        e - jnp.mean(e, -1, keepdims=True) - normed * jnp.mean(e * normed, -1, keepdims=True)
    )
    tg_ref[...] = (grad + ln).astype(bf16)
    for k, term in enumerate((first_g * normed, first_g, second_g * normed, second_g, grad)):
        tot_ref[k] += jnp.sum(term.reshape(tile // 8, 8, width), 0)

    if part < parts - 1:
        return

    @pl.when(i == pl.num_programs(0) - 1)
    def _():
        for j in range(2):
            for rel in range(2):
                for p in range(3):
                    qb_ref[p * 4 + (rel ^ c) * 2 + j] = qb_refs[2 * j + rel][:, 128 * p : 128 * (p + 1)]
        sums = [jnp.sum(tot_ref[k], 0, keepdims=True) for k in range(5)]
        sums.append(sums[4])
        for ref, rel in ((own_ref, 0), (send_ref, 1)):
            owner = rel ^ c
            for k in range(6):
                for part in range(2):
                    low = sums[k][:, 128 * part : 128 * (part + 1)]
                    high = sums[k][:, 256 + 128 * part : 256 + 128 * (part + 1)]
                    ref[2 * k + part] = jnp.where(owner == 0, low, high)
            for k in range(6):
                ref[12 + k] = qb_ref[owner * 6 + k]
            for j in range(2):
                for k in range(4):
                    ref[18 + 4 * j + k] = fb_ref[2 * j + rel][:, 128 * k : 128 * (k + 1)]
            for k in range(SMALL_ROWS, 32):
                ref[k] = jnp.zeros((1, 128), f32)


def output_call(part, parts, meta, tokens, grad, act, hg, atts, qgs, out_w, proj_w, fc_w, qkv_w, small, qbs, fb,
                before=None):
    rows, width = tokens.shape
    tile = 256
    tiles = rows // tile // parts
    blk = lambda n: pl.BlockSpec((tile, n), lambda i, m: (part * tiles + i, 0))
    weights = [*out_w, *proj_w, *fc_w, *qkv_w]
    tail = [small, *qbs, fb]
    sums = (5, 8, width)
    packed = (32, 1, 128)
    last = part == parts - 1
    extra, extra_specs, aliases = [], [], {}
    count = 5 + len(atts) + len(qgs) + len(weights) + len(tail)
    if before is not None:
        extra = [before[2], before[0], before[1]]
        extra_specs = [full_spec(sums), pl.BlockSpec(memory_space=pl.ANY), pl.BlockSpec(memory_space=pl.ANY)]
        aliases = {count + 1: 0, count + 2: 1}
    scratch = [
        pltpu.VMEM(qkv_w[0].shape, bf16),
        pltpu.VMEM(qkv_w[0].shape, bf16),
        pltpu.VMEM((tile, width), f32),
        pltpu.VMEM((tile, width), f32),
    ]
    if last:
        scratch += [pltpu.VMEM(sums, f32), pltpu.VMEM((12, 1, 128), f32)]
    given = [packed, packed] if last else [sums]
    grid_spec = pltpu.PrefetchScalarGridSpec(
        num_scalar_prefetch=1,
        grid=(tiles,),
        in_specs=[
            blk(width),
            blk(width),
            *[blk(a.shape[1]) for a in (act, hg, *atts, *qgs)],
            *[full_spec(w.shape) for w in weights],
            *[full_spec(w.shape) for w in tail],
            *extra_specs,
        ],
        out_specs=[blk(width), blk(width), *[full_spec(g) for g in given]],
        scratch_shapes=scratch,
    )
    return pl.pallas_call(
        functools.partial(output_kernel, part, parts),
        grid_spec=grid_spec,
        out_shape=[
            jax.ShapeDtypeStruct((rows, width), bf16),
            jax.ShapeDtypeStruct((rows, width), bf16),
            *[jax.ShapeDtypeStruct(g, f32) for g in given],
        ],
        input_output_aliases=aliases,
        cost_estimate=cost(
            2 * rows * width * (512 + 2048 * 2 + 1536) // parts, 2 * rows * (4 * 512 + 4 * 2048) // parts
        ),
        name=f"outputs_{part}",
        compiler_params=pltpu.CompilerParams(vmem_limit_bytes=30 << 20),
    )(meta, tokens, grad, act, hg, *atts, *qgs, *weights, *tail, *extra)


def sum_kernel(n_in, *refs):
    ins, outs = refs[:n_in], refs[n_in:]
    for k, out in enumerate(outs):
        rows = out.shape[0]
        for i in range(rows):
            total = ins[0][k * rows + i].astype(f32)
            for term in ins[1:]:
                total += term[k * rows + i].astype(f32)
            out[i] = total.astype(out.dtype)


def sum_call(terms, count, name):
    shape, dtype = terms[0].shape, terms[0].dtype
    moved = len(terms) * terms[0].size * terms[0].dtype.itemsize
    return pl.pallas_call(
        functools.partial(sum_kernel, len(terms)),
        out_shape=[jax.ShapeDtypeStruct((shape[0] // count, *shape[1:]), dtype)] * count,
        compiler_params=pltpu.CompilerParams(vmem_limit_bytes=(moved * 3) // 2 + (4 << 20)),
        cost_estimate=cost(moved, 2 * moved),
        name=name,
    )(*terms)


def pair_kernel(*refs):
    own, got, outs = refs[:2], refs[2:4], refs[4:]
    for j, (mine, other) in enumerate(zip(own, got)):
        w = mine.shape[2]
        for k, out in enumerate(outs):
            total = mine[k].astype(f32) + other[k].astype(f32)
            out[0, :, j * w : (j + 1) * w] = total.astype(bf16)


def pair_call(own, got, name):
    rows, width = own[0].shape[1], 2 * own[0].shape[2]
    return pl.pallas_call(
        pair_kernel,
        out_shape=[jax.ShapeDtypeStruct((1, rows, width), bf16)] * 4,
        compiler_params=pltpu.CompilerParams(vmem_limit_bytes=12 << 20),
        cost_estimate=cost(8 * rows * width, 24 * rows * width),
        name=name,
    )(*own, *got)


def half_kernel(meta, mine_ref, got_ref, keep_ref, send_ref):
    rows = keep_ref.shape[1]
    for out, number in ((keep_ref, meta[3]), (send_ref, 1 - meta[3])):
        at = pl.ds(pl.multiple_of(number * rows, rows), rows)
        out[0] = (mine_ref[0, at, :].astype(f32) + got_ref[0, at, :].astype(f32)).astype(bf16)


def join_kernel(meta, mine_ref, got_ref, out_ref):
    rows = mine_ref.shape[1]
    for piece, number in ((mine_ref, meta[3]), (got_ref, 1 - meta[3])):
        out_ref[0, pl.ds(pl.multiple_of(number * rows, rows), rows), :] = piece[0]


def half_call(kernel, meta, terms, outs, name):
    moved = 2 * sum(a.size for a in terms)
    whole = pl.BlockSpec(memory_space=pltpu.VMEM)
    return pl.pallas_call(
        kernel,
        in_specs=[pl.BlockSpec(memory_space=pltpu.SMEM), whole, whole],
        out_specs=[whole] * len(outs),
        out_shape=[jax.ShapeDtypeStruct(o, bf16) for o in outs],
        compiler_params=pltpu.CompilerParams(vmem_limit_bytes=(moved * 3) // 2 + (4 << 20)),
        cost_estimate=cost(moved, 2 * moved),
        name=name,
    )(meta, *terms)


def exchange(a, reps, far, near):
    pairs = [(2 * i + c, 2 * (i ^ (near if c else far)) + c) for i in range(reps) for c in range(2)]
    return lax.ppermute(a, ("rep", "opt"), pairs)


def swap(a):
    return lax.ppermute(a, "opt", [(0, 1), (1, 0)])


def tie(value, *others):
    return lax.optimization_barrier((value, *others))[0]


def rest_bits(reps):
    return [1 << b for b in range(2, reps.bit_length() - 1)]


def crosses(pieces, reps):
    steps = ((2, 1), (1, 2), (3, 3))
    return [exchange(a, reps, *step) for a, step in zip(pieces, steps)]


def adamw(grad, mean, square, weight):
    new_mean = BETA_ONE * mean + (1.0 - BETA_ONE) * grad
    new_square = BETA_TWO * square + (1.0 - BETA_TWO) * grad * grad
    step = -LEARN_RATE * (
        new_mean * (1.0 / FIX_ONE) / (jnp.sqrt(new_square * (1.0 / FIX_TWO)) + ADAM_EPS)
        + WEIGHT_DECAY * weight.astype(f32)
    )
    return step, new_mean, new_square


def pick(refs, which, cols, rows=slice(None)):
    out = refs[0][0, rows, cols]
    for k in range(1, len(refs)):
        out = jnp.where(which == k, refs[k][0, rows, cols], out)
    return out.astype(f32)


def adam_block(grad, m_ref, s_ref, w_ref, g_out, st_out, m_out, s_out, at):
    step, mean, square = adamw(grad, m_ref[at], s_ref[at], w_ref[at])
    g_out[at] = grad
    st_out[at] = step
    m_out[at] = mean
    s_out[at] = square


def adam_ff_kernel(meta, *refs):
    pieces, proj, fc, proj_out, fc_out = refs[:-14], refs[-14:-11], refs[-11:-8], refs[-8:-4], refs[-4:]
    which = pl.program_id(0)
    n = fc[0].shape[0]
    rows = pl.ds(pl.multiple_of(pl.program_id(1) * n, n), n)
    for j in range(2):
        for k in range(2):
            col = 1024 * j + 512 * k
            at = (j, 0, k, slice(None), slice(None))
            adam_block(pick(pieces, which, slice(col, col + 512), rows), *proj, *proj_out, at)
            at = (slice(None), slice(col, col + 512))
            adam_block(pick(pieces, which, slice(2048 + col, 2048 + col + 512), rows), *fc, *fc_out, at)


def adam_qkv_kernel(meta, *refs):
    pieces, qkv, out, qkv_out, out_out = refs[:-14], refs[-14:-11], refs[-11:-8], refs[-8:-4], refs[-4:]
    c = meta[0]
    which = pl.program_id(0)
    sub = pl.program_id(1)
    n = qkv[0].shape[0]
    h = out[0].shape[1]
    rows = pl.ds(pl.multiple_of(sub * n, n), n)
    for j in range(2):
        for slot in range(2):
            for p in range(3):
                col = 1024 * j + 384 * slot + 128 * p
                grad = pick(pieces, which, slice(col, col + 128), rows)
                lanes = pl.ds(pl.multiple_of((p * 4 + (slot ^ c) * 2 + j) * 128, 128), 128)
                adam_block(grad, *qkv, *qkv_out, (slice(None), lanes))
        for k in range(2):
            col = 1024 * j + 768
            half = pl.ds(pl.multiple_of(k * (pieces[0].shape[1] // 2) + sub * h, h), h)
            grad = pick(pieces, which, slice(col, col + 256), half)
            adam_block(grad, *out, *out_out, (j, slice(None), slice(256 * k, 256 * k + 256)))


def adam_call(kernel, meta, start, pieces, first, second, first_spec, second_spec, subs, name, before=()):
    outs = [jax.ShapeDtypeStruct(first[0].shape, f32)] * 4 + [jax.ShapeDtypeStruct(second[0].shape, f32)] * 4
    specs = [
        pl.BlockSpec(shape, functools.partial(lambda at, i, k, m: at((start + i) ^ m[1], k), at))
        for shape, at in (first_spec, second_spec)
    ]
    count = len(before)

    def run(meta_ref, *refs):
        kernel(meta_ref, *refs[count:])

    grid_spec = pltpu.PrefetchScalarGridSpec(
        num_scalar_prefetch=1,
        grid=(len(pieces), subs),
        in_specs=[
            *[pl.BlockSpec(memory_space=pl.ANY)] * count,
            *[full_spec(a.shape) for a in pieces],
            *[specs[0]] * 3,
            *[specs[1]] * 3,
        ],
        out_specs=[*[specs[0]] * 4, *[specs[1]] * 4],
    )
    size = (first[0].size + second[0].size) * len(pieces) // 4
    return pl.pallas_call(
        run,
        grid_spec=grid_spec,
        out_shape=outs,
        input_output_aliases={1 + k: k for k in range(count)},
        compiler_params=pltpu.CompilerParams(vmem_limit_bytes=56 << 20),
        cost_estimate=cost(20 * size, 28 * size),
        name=name,
    )(meta, *before, *pieces, *first, *second)


def body(
    tokens,
    out_grad,
    vectors,
    qkv_weight,
    qkv_bias,
    out_weight,
    fc_weight,
    fc_bias,
    proj_weight,
    mean_vectors,
    mean_qkv_weight,
    mean_qkv_bias,
    mean_out_weight,
    mean_fc_weight,
    mean_fc_bias,
    mean_proj_weight,
    square_vectors,
    square_qkv_weight,
    square_qkv_bias,
    square_out_weight,
    square_fc_weight,
    square_fc_bias,
    square_proj_weight,
):
    reps = lax.axis_size("rep")
    c = lax.axis_index("opt")
    place = lax.axis_index("rep")
    low, high = place & 1, (place >> 1) & 1
    slot = lax.iota(jnp.int32, 4)
    ranks = jnp.where((slot == 1) == (c == 0), 2 * low + high, 2 * high + low)
    meta = jnp.where(slot == 0, c, jnp.where(slot == 3, (place >> 2) & 1, ranks)).astype(jnp.int32)
    trig = jnp.asarray(trig_tables())

    packed = jnp.concatenate(
        [vectors.reshape(12, 128), qkv_bias.reshape(6, 128), fc_bias.reshape(8, 128)], 0
    )
    packed_far = swap(packed)
    small = jnp.stack([jnp.where(c == 0, packed, packed_far), jnp.where(c == 0, packed_far, packed)])
    small = small.astype(f32).reshape(2 * SMALL_ROWS, 1, 128)
    fc_far = swap(tie(fc_weight, packed_far))
    proj_far = swap(tie(proj_weight, packed_far))
    qkv_far = swap(qkv_weight)
    out_far = swap(out_weight)

    first, second = norm_call(tokens, small)
    send, act, hg, fb = ff_call(
        meta, second, out_grad, fc_weight, fc_far, proj_weight, proj_far, small
    )
    ff_got = swap(send)
    own = ff_own_call(tie(meta, send), second, out_grad, act, hg)
    att = {}
    bits = rest_bits(reps)

    def attend(j, rel, *wait):
        out_w = out_far if rel else out_weight
        before = att[j, 1][:2] if rel == 0 else ()
        att[j, rel] = attention_call(
            j, rel, tie(meta, *wait), first, out_grad, qkv_weight, qkv_far, out_w, small, trig, before
        )
        return att[j, rel][4]

    def rest(total, start, name):
        for bit in bits[start:]:
            (total,) = sum_call([total, exchange(total, reps, bit, bit)], 1, name)
        return total

    keep, send = sum_call([own, ff_got], 2, "ff_pair")
    got = exchange(send, reps, 1, 2)
    mark = attend(0, 1, keep)
    keep, send = sum_call([tie(keep, mark), got], 2, "ff_sum0")
    got = exchange(send, reps, 2, 1)
    mark = attend(0, 0, keep)
    whole = keep.shape
    half = (1, whole[1] // 2, whole[2])
    keep, send = half_call(half_kernel, meta, [tie(keep, mark), got], [half] * 2, "ff_sum1")
    got = exchange(send, reps, bits[0], bits[0])
    own, others = [att[0, 0][0]], [swap(att[0, 0][1])]
    mark = attend(1, 1, keep)
    (piece,) = sum_call([tie(keep, mark), got], 1, "ff_sum2")
    ff_got = exchange(piece, reps, bits[1], bits[1])
    mark = attend(1, 0, piece, others[0])

    (piece,) = sum_call([tie(piece, mark), ff_got], 1, "ff_sum3")
    piece = rest(piece, 2, "ff_sum4")
    ff_got = exchange(piece, reps, bits[0], bits[0])
    own.append(att[1, 0][0])
    others.append(swap(tie(att[1, 0][1], piece)))
    chunks = pair_call(own, others, "att_pair")
    got = crosses(chunks[1:], reps)

    keys = [(0, 0), (0, 1), (1, 0), (1, 1)]
    give = lambda part, before, *wait: output_call(
        part,
        PARTS,
        tie(meta, *wait),
        tokens,
        out_grad,
        act,
        hg,
        [att[k][3] for k in keys],
        [att[k][2] for k in keys],
        (out_weight, out_far),
        (proj_weight, proj_far),
        (fc_weight, fc_far),
        (qkv_weight, qkv_far),
        small,
        [att[k][4] for k in keys],
        fb,
        before,
    )
    done = give(0, None, piece, chunks[0])
    (att_total,) = sum_call([tie(chunks[0], done[2]), *got], 1, "att_sum0")
    got = exchange(att_total, reps, bits[0], bits[0])
    (ff_total,) = half_call(join_kernel, meta, [tie(piece, att_total), ff_got], [whole], "ff_join")
    ff_pieces = [ff_total, exchange(ff_total, reps, 2, 1), exchange(ff_total, reps, 1, 2)]
    layer_out, tokens_grad, small_own, small_send = give(1, done, att_total, ff_total)

    (att_total,) = sum_call([tie(att_total, small_own, *ff_pieces[1:]), got], 1, "att_sum1")
    got = exchange(att_total, reps, bits[1], bits[1])
    ff_pieces.append(exchange(tie(ff_pieces[2], att_total), reps, 2, 1))
    (total,) = sum_call([tie(small_own, att_total), swap(small_send)], 1, "small_pair")
    small_got = exchange(total, reps, 1, 1)

    view = lambda a: a.reshape(2, 4, 2, 64, 512)
    adam_ff = lambda start, pieces, before, *wait: adam_call(
        adam_ff_kernel,
        tie(meta, *wait),
        start,
        pieces,
        [view(a) for a in (mean_proj_weight, square_proj_weight, proj_weight)],
        [mean_fc_weight, square_fc_weight, fc_weight],
        ((2, 1, 2, 64, 512), lambda q, k: (0, q, 0, k, 0)),
        ((64, 2048), lambda q, k: (q + k, 0)),
        1,
        f"adam_ff_{start}",
        before,
    )
    view_o = lambda a: a.reshape(2, 128, 512)
    adam_qkv = lambda start, pieces, before, *wait: adam_call(
        adam_qkv_kernel,
        tie(meta, *wait),
        start,
        pieces,
        [mean_qkv_weight, square_qkv_weight, qkv_weight],
        [view_o(a) for a in (mean_out_weight, square_out_weight, out_weight)],
        ((64, 1536), lambda q, k: (q + k, 0)),
        ((2, 32, 512), lambda q, k: (0, q + k, 0)),
        1,
        f"adam_qkv_{start}",
        before,
    )
    a_ff = adam_ff(0, ff_pieces[:3], (), total, att_total)
    (total,) = sum_call([tie(total, a_ff[4]), small_got], 1, "small_sum")
    small_got = exchange(total, reps, bits[0], bits[0])
    (att_total,) = sum_call([tie(att_total, total), got], 1, "att_sum2")
    att_total = rest(att_total, 2, "att_sum3")
    att_pieces = [att_total, *crosses([att_total] * 3, reps)]
    a_ff = adam_ff(3, ff_pieces[3:], a_ff, att_total)
    (total,) = sum_call([tie(total, a_ff[4]), small_got], 1, "small_sum")
    small_got = exchange(total, reps, bits[1], bits[1])
    a_qkv = adam_qkv(0, att_pieces[:1], (), total)
    (total,) = sum_call([tie(total, a_qkv[0]), small_got], 1, "small_sum")
    mark = tie(total, *att_pieces[1:])
    small_got = exchange(mark, reps, 2, 2)

    a_qkv = adam_qkv(1, att_pieces[1:], a_qkv, mark)
    a_proj = [a.reshape(1024, 512) for a in a_ff[:4]]
    a_fc = a_ff[4:]
    a_out = [a.reshape(256, 512) for a in a_qkv[4:]]
    a_qkv = a_qkv[:4]
    (total,) = sum_call([tie(mark, a_out[0]), small_got], 1, "small_sum")
    total = rest(total, 2, "small_sum")
    flat = total.reshape(32, 128)
    g_vec = flat[:12].reshape(6, 256)
    g_qb = flat[12:18].reshape(768)
    g_fb = flat[18:26].reshape(1024)

    a_vec = (g_vec, *adamw(g_vec, mean_vectors, square_vectors, vectors))
    a_qb = (g_qb, *adamw(g_qb, mean_qkv_bias, square_qkv_bias, qkv_bias))
    a_fb = (g_fb, *adamw(g_fb, mean_fc_bias, square_fc_bias, fc_bias))
    order = (a_vec, a_qkv, a_qb, a_out, a_fc, a_fb, a_proj)
    return (layer_out, tokens_grad, *[a[k] for k in range(4) for a in order])


def solution(mesh):
    rows = P(("rep", "opt"), None)
    weights = (P(None, "opt"), P("opt", None), P("opt"), P("opt", None), P("opt", None), P("opt"), P("opt", None))
    in_specs = (rows, rows, *weights, *weights, *weights)
    out_specs = (rows, rows, *weights, *weights, *weights, *weights)
    return jax.shard_map(body, mesh=mesh, in_specs=in_specs, out_specs=out_specs, check_vma=False)
```
